32 devices in a mesh: sector: 16 (over z, y, x), op: 2 (over core).
Axes of the slice: x: 2, y: 2, z: 4, core: 2. Of those that a mesh axis runs over, the one named last changes fastest.
Arguments:
- wave_start: float32 [32, 256, 256], P('sector'), may hold values from -6 to 6
- left_blocks: float32 [4, 32, 256, 256], P('op', 'sector'), may hold values from -0.375 to 0.375
- right_blocks: float32 [4, 32, 256, 256], P('op', 'sector'), may hold values from -0.1875 to 0.1875
- term_shifts: int32 [4], P('op'), may hold values from -1 to 1
- preconditioner: float32 [32, 256, 256], P('sector'), may hold values from 0.5 to 4
Outputs:
- basis: float32 [3, 32, 256, 256], P(None, 'sector', 'op')
- ritz: float32 [3], replicated
The draws below stay inside these ranges and needn't reach their ends.
Inputs may be any that keep to these rules, and one draw needn't show every extreme that they name: Each term changes the charge sector by term_shifts, one of -1, 0 and 1.
All inputs are finite; a program needn't handle non-finite values.
Results may differ from the reference program's by a relative error of at most 0.0003.
Values sent between devices are 32-bit elements; how exact they have to be, the bound alone decides.
No kernel may reach another device: no remote copies, remote signals or barrier semaphores. Data moves between devices by JAX's collectives and lax.ppermute only.
A program may use at most 64 MiB of HBM per device.

```python
import math
import jax
import jax.numpy as jnp
from jax import lax

M = 256
ITERS = 3
SECTORS = 32
TERMS = 4


def place_ends(result, key, least, largest):
    longest = result.shape.index(max(result.shape))
    spots = []
    for shift in (0, 1):
        where = [jax.random.randint(jax.random.fold_in(key, axis), (), 0, length) for axis, length in enumerate(result.shape)]
        where[longest] = (where[longest] + shift) % result.shape[longest]
        spots.append(tuple(where))
    return result.at[spots[0]].set(least).at[spots[1]].set(largest)


def shard_levels(rng, shape, shards, low, high):
    level, own = 1.0, jax.random.fold_in(rng, 6)
    for dim, blocks in shards:
        draws = jnp.exp(jax.random.uniform(jax.random.fold_in(own, dim), (blocks,), jnp.float32, low / len(shards), high / len(shards)))
        level = level * jnp.repeat(draws, shape[dim] // blocks).reshape([-1 if axis == dim else 1 for axis in range(len(shape))])
    return level


def bell_draw(stream_key, dims, width, limit, pieces=(), held_as=jnp.bfloat16):
    factor_of = shard_levels(stream_key, dims, pieces, -0.22, 0.18) if pieces else 1.0
    array = jax.random.normal(stream_key, dims, jnp.float32) * width * factor_of
    return jnp.minimum(jnp.maximum(array, -limit), limit).astype(held_as)


def setup_inputs(seed: int = 0) -> dict:
    keys = jax.random.split(jax.random.key(seed), 6)
    wave_start = bell_draw(keys[0], (SECTORS, M, M), 1.0, 6.0, ((0, 16),), jnp.float32)
    left_blocks = bell_draw(keys[1], (TERMS, SECTORS, M, M), M ** -0.5, 0.375, ((0, 2), (1, 16)), jnp.float32)
    right_blocks = bell_draw(keys[2], (TERMS, SECTORS, M, M), (M * TERMS) ** -0.5, 0.1875, ((0, 2), (1, 16)), jnp.float32)
    term_shifts = place_ends(jax.random.randint(keys[3], (TERMS,), -1, 2), jax.random.fold_in(keys[3], 1), -1, 1).astype(jnp.int32)
    preconditioner = jnp.clip(jnp.exp(math.log(4.0) - 2.0794415 * jax.random.uniform(keys[4], (SECTORS, M, M), jnp.float32) ** shard_levels(keys[4], (SECTORS, M, M), ((0, 16),), -0.2, 0.2)), 0.5, 4.0)
    return {"wave_start": wave_start, "left_blocks": left_blocks, "right_blocks": right_blocks, "term_shifts": term_shifts, "preconditioner": preconditioner}


EPSILON = 1e-06

def apply_operator(vectors, left_blocks, right_blocks, term_shifts):
    padded = jnp.pad(vectors, ((1, 1), (0, 0), (0, 0)))

    def one_sector(position):
        source = jnp.take(padded, (position + 1 - term_shifts).astype(jnp.int32), axis=0)
        inner = jnp.einsum('kab,kbc->kac', left_blocks[:, position], source, precision=lax.Precision.HIGHEST)
        return jnp.einsum('kac,kcd->ad', inner, right_blocks[:, position], precision=lax.Precision.HIGHEST)
    return lax.map(one_sector, jnp.arange(vectors.shape[0], dtype=jnp.int32))

def reference(wave_start, left_blocks, right_blocks, term_shifts, preconditioner):
    total = SECTORS * M * M
    start_sum = jnp.sum(wave_start * wave_start) / total
    current = wave_start * lax.rsqrt(start_sum + EPSILON)
    basis = [current]
    ritz = []
    for index in range(ITERS):
        latest = basis[-1]
        image = apply_operator(latest, left_blocks, right_blocks, term_shifts)
        theta = jnp.sum(latest * image) / total
        correction = (image - theta * latest) / preconditioner
        correlations = [jnp.sum(member * correction) / total for member in basis]
        ortho = correction
        for position, member in enumerate(basis):
            ortho = ortho - correlations[position] * member
        length = jnp.sum(ortho * ortho) / total
        basis.append(ortho * lax.rsqrt(length + EPSILON))
        ritz.append(theta)
    return (jnp.stack(basis[1:]), jnp.stack(ritz))
```

```python
import jax
import jax.numpy as jnp
from jax import lax
from jax.sharding import PartitionSpec as P

ITERS = 3


EPSILON = 1e-06

AXES = ("sector", "op")

LANES = 128


def total_sum(values):
    devices = lax.axis_size("sector") * lax.axis_size("op")
    row = jnp.pad(values, (0, LANES - values.shape[0]))
    rows = lax.all_to_all(jnp.broadcast_to(row, (devices, LANES)), AXES, 0, 0, tiled=True)
    return jnp.sum(rows, axis=0)[: values.shape[0]]


def coefficients(sums, total, count):
    sums = sums / total
    theta = sums[0]
    correlations = sums[4 : 4 + count] - theta * sums[4 + count : 4 + 2 * count]
    length = (
        sums[1]
        - 2.0 * theta * sums[2]
        + theta * theta * sums[3]
        - jnp.sum(jnp.square(correlations))
    )
    return theta, correlations, lax.rsqrt(length + EPSILON)


def products(members, image, inverse):
    latest = members[-1]
    ratio_image = image * inverse
    ratio_latest = latest * inverse
    pieces = [
        jnp.sum(latest * image),
        jnp.sum(ratio_image * ratio_image),
        jnp.sum(ratio_image * ratio_latest),
        jnp.sum(ratio_latest * ratio_latest),
    ]
    pieces = pieces + [jnp.sum(member * ratio_image) for member in members]
    pieces = pieces + [jnp.sum(member * ratio_latest) for member in members]
    return pieces


def one_sector_body(wave_start, left_blocks, right_blocks, term_shifts, preconditioner):
    highest = lax.Precision.HIGHEST
    op = lax.axis_index("op")
    chips = lax.axis_size("sector")
    devices = 2 * chips
    width = wave_start.shape[1]
    total = float(2 * chips * width * wave_start.shape[2])
    swap = [(i, i ^ 1) for i in range(devices)]
    across = [(i, i + 1) for i in range(1, devices - 1, 2)]
    across = across + [(j, i) for i, j in across]

    def mate(values):
        return lax.ppermute(values, AXES, swap)

    def facing(values):
        return lax.ppermute(values, AXES, across)

    def pick(values, index, axis):
        return lax.dynamic_index_in_dim(values, index, axis, keepdims=False)

    inverse = 1.0 / preconditioner
    own_wave, mate_wave = pick(wave_start, op, 0), pick(wave_start, 1 - op, 0)
    own_inverse, mate_inverse = pick(inverse, op, 0), pick(inverse, 1 - op, 0)
    facing_wave = facing(own_wave)
    facing_inverse = facing(own_inverse)
    left = jnp.concatenate([pick(left_blocks, op, 1), mate(pick(left_blocks, 1 - op, 1))])
    right = jnp.concatenate([pick(right_blocks, op, 1), mate(pick(right_blocks, 1 - op, 1))])
    shifts = jnp.concatenate([term_shifts, mate(term_shifts.astype(jnp.float32)).astype(jnp.int32)])
    toward_mate = jnp.where(op == 0, -1, 1)

    def operator(own, mates, facings):
        shift = shifts[:, None, None]
        source = jnp.where(
            shift == 0, own[None], jnp.where(shift == toward_mate, mates[None], facings[None])
        )
        inner = jnp.einsum("kab,kbc->kac", left, source, precision=highest)
        return jnp.einsum("kac,kcd->ad", inner, right, precision=highest)

    inverses = (own_inverse, mate_inverse, facing_inverse)
    waves = (own_wave, mate_wave, facing_wave)
    basis = []
    ritz = []
    latest = waves
    for index in range(ITERS):
        image = operator(*latest)
        mate_rows = image
        last = index + 1 == ITERS
        if last:
            half = width // 2
            mate_image = mate(lax.dynamic_slice_in_dim(image, (1 - op) * half, half, axis=0))
            images = (image, mate_image)
        else:
            images = (image, mate(image), facing(image))
        members = [member[0] for member in basis] if basis else [own_wave]
        pieces = products(members, image, own_inverse)
        if not basis:
            pieces = pieces + [jnp.sum(own_wave * own_wave)]
        sums = total_sum(jnp.stack(pieces))
        if not basis:
            factor = lax.rsqrt(sums[6] / total + EPSILON)
            square = factor * factor
            sums = sums[:6] * square
            basis.append(tuple(wave * factor for wave in waves))
            images = tuple(part * factor for part in images)
        theta, correlations, scale = coefficients(sums, total, len(basis))
        ritz.append(theta)

        def fresh(image, inverse, members):
            ortho = (image - theta * members[-1]) * inverse
            for position, member in enumerate(members):
                ortho = ortho - correlations[position] * member
            return ortho * scale

        if last:
            own_rows = lambda values: lax.dynamic_slice_in_dim(values, op * half, half, axis=0)
            basis.append(
                (
                    fresh(own_rows(image), own_rows(own_inverse), [own_rows(m[0]) for m in basis]),
                    fresh(mate_image, own_rows(mate_inverse), [own_rows(m[1]) for m in basis]),
                )
            )
        else:
            basis.append(
                tuple(
                    fresh(images[i], inverses[i], [member[i] for member in basis]) for i in range(3)
                )
            )
        latest = basis[-1]

    def placed(own, mates):
        return jnp.stack([jnp.where(op == 0, own, mates), jnp.where(op == 0, mates, own)])

    output = [placed(own_rows(m[0]), own_rows(m[1])) for m in basis[1:-1]] + [placed(*basis[-1])]
    return (jnp.stack(output), jnp.stack(ritz))


def with_halo(cells, sides, width):
    for axis, dim in sides:
        count = lax.axis_size(axis)
        ends = count - 1
        head = lax.slice_in_dim(cells, 0, width, axis=dim)
        tail = lax.slice_in_dim(cells, cells.shape[dim] - width, cells.shape[dim], axis=dim)
        cells = jnp.concatenate(
            [
                lax.ppermute(tail, axis, [(i, (i + 1) % count) for i in range(ends)]),
                cells,
                lax.ppermute(head, axis, [((i + 1) % count, i) for i in range(ends)]),
            ],
            axis=dim,
        )
    return cells


def split_terms_body(wave_start, left_blocks, right_blocks, term_shifts, preconditioner):
    highest = lax.Precision.HIGHEST
    width = wave_start.shape[1]
    row_count = width // lax.axis_size("op")
    first_row = lax.axis_index("op") * row_count
    total = float(wave_start.shape[0] * lax.axis_size("sector") * width * wave_start.shape[2])

    def portion(values):
        return lax.dynamic_slice_in_dim(values, first_row, row_count, axis=values.ndim - 2)

    start_sum = total_sum(jnp.sum(jnp.square(portion(wave_start)))[None])[0] / total
    basis = [wave_start * lax.rsqrt(start_sum + EPSILON)]
    ritz = []
    for _ in range(ITERS):
        latest = basis[-1]
        padded = with_halo(latest, (("sector", 0),), 1)
        shift = term_shifts[:, None, None, None]
        source = jnp.where(
            shift == 1,
            padded[None, :-2],
            jnp.where(shift == -1, padded[None, 2:], padded[None, 1:-1]),
        )
        inner = jnp.einsum("ksab,ksbc->ksac", left_blocks, source, precision=highest)
        image = lax.psum(jnp.einsum("ksac,kscd->sad", inner, right_blocks, precision=highest), "op")
        inverse = 1.0 / preconditioner
        pieces = products([portion(member) for member in basis], portion(image), portion(inverse))
        theta, correlations, scale = coefficients(
            total_sum(jnp.stack(pieces)), total, len(basis)
        )
        ortho = (image - theta * latest) * inverse
        for position, member in enumerate(basis):
            ortho = ortho - correlations[position] * member
        basis.append(ortho * scale)
        ritz.append(theta)
    output = jnp.stack([portion(member) for member in basis[1:]])
    return (output, jnp.stack(ritz))


def solution(mesh):
    placed = (
        P("sector", None, None),
        P("op", "sector", None, None),
        P("op", "sector", None, None),
        P("op"),
        P("sector", None, None),
    )

    def body(wave_start, *operands):
        one_each = mesh.shape["op"] == 2 and wave_start.shape[0] == 2
        return (one_sector_body if one_each else split_terms_body)(wave_start, *operands)

    return jax.shard_map(
        body,
        mesh=mesh,
        in_specs=placed,
        out_specs=(P(None, "sector", "op", None), P()),
        check_vma=False,
    )
```

```python
import functools

import jax
import jax.numpy as jnp
from jax import lax
from jax.experimental import pallas as pl
from jax.experimental.pallas import tpu as pltpu
from jax.sharding import PartitionSpec as P

ITERS = 3


EPSILON = 1e-06

AXES = ("sector", "op")

LANES = 128


def total_sum(values):
    devices = lax.axis_size("sector") * lax.axis_size("op")
    row = jnp.pad(values, (0, LANES - values.shape[0]))
    rows = lax.all_to_all(jnp.broadcast_to(row, (devices, LANES)), AXES, 0, 0, tiled=True)
    return jnp.sum(rows, axis=0)[: values.shape[0]]


def coefficients(sums, total, count):
    sums = sums / total
    theta = sums[0]
    correlations = sums[4 : 4 + count] - theta * sums[4 + count : 4 + 2 * count]
    length = (
        sums[1]
        - 2.0 * theta * sums[2]
        + theta * theta * sums[3]
        - jnp.sum(jnp.square(correlations))
    )
    return theta, correlations, lax.rsqrt(length + EPSILON)


def products(members, image, inverse):
    latest = members[-1]
    ratio_image = image * inverse
    ratio_latest = latest * inverse
    pieces = [
        jnp.sum(latest * image),
        jnp.sum(ratio_image * ratio_image),
        jnp.sum(ratio_image * ratio_latest),
        jnp.sum(ratio_latest * ratio_latest),
    ]
    pieces = pieces + [jnp.sum(member * ratio_image) for member in members]
    pieces = pieces + [jnp.sum(member * ratio_latest) for member in members]
    return pieces


def split(values):
    high = values.astype(jnp.bfloat16)
    return high, (values - high.astype(jnp.float32)).astype(jnp.bfloat16)


def dot_split(lhs_high, lhs_low, rhs_high, rhs_low):
    dot = functools.partial(jnp.dot, preferred_element_type=jnp.float32)
    return dot(lhs_high, rhs_high) + (dot(lhs_low, rhs_high) + dot(lhs_high, rhs_low))


def apply_terms(sources, vectors, left, right):
    left_high, left_low = left
    right_high, right_low = right
    vector_high, vector_low = vectors
    image = None
    for term, source in enumerate(sources):
        inner = dot_split(left_high[term], left_low[term], vector_high[source], vector_low[source])
        part = dot_split(*split(inner), right_high[term], right_low[term])
        image = part if image is None else image + part
    return image


def term_sources(own_shifts, mate_shifts):
    toward_mate = jnp.where(lax.axis_index("op") == 0, -1, 1)
    shifts = [refs[i] for refs in (own_shifts, mate_shifts) for i in range(refs.shape[0])]
    return [
        jnp.where(shift == 0, 0, jnp.where(shift == toward_mate, 1, 2)) for shift in shifts
    ]


def row_of_sums(factors, devices):
    lane = lax.broadcasted_iota(jnp.int32, (1, LANES), 1)
    row = jnp.zeros((1, LANES), jnp.float32)
    for position, (one, other) in enumerate(factors):
        product = (one * other).reshape(-1, 8, one.shape[1])
        whole = jnp.sum(jnp.sum(product, axis=0), axis=(0, 1), keepdims=True)
        row = jnp.where(lane == position, whole, row)
    return jnp.broadcast_to(row, (devices, LANES))


def factors_of(members, image, inverse):
    latest = members[-1]
    ratio_image = image * inverse
    ratio_latest = latest * inverse
    factors = [
        (latest, image),
        (ratio_image, ratio_image),
        (ratio_image, ratio_latest),
        (ratio_latest, ratio_latest),
    ]
    factors = factors + [(member, ratio_image) for member in members]
    return factors + [(member, ratio_latest) for member in members]


def summed(rows, total):
    whole = jnp.sum(rows[...], axis=0, keepdims=True) / total
    return [whole[:, i : i + 1] for i in range(10)]


def step_factors(sums, count):
    theta = sums[0]
    correlations = [sums[4 + i] - theta * sums[4 + count + i] for i in range(count)]
    length = sums[1] - 2.0 * theta * sums[2] + theta * theta * sums[3]
    for correlation in correlations:
        length = length - correlation * correlation
    return theta, correlations, lax.rsqrt(length + EPSILON)


def fresh(step, image, inverse, members):
    theta, correlations, scale = step
    ortho = (image - theta * members[-1]) * inverse
    for correlation, member in zip(correlations, members):
        ortho = ortho - correlation * member
    return ortho * scale


def start_factors(sums):
    factor = lax.rsqrt(sums[6] + EPSILON)
    return factor, [value * (factor * factor) for value in sums[:6]]


def inverted(values):
    return jnp.where(values > 0.0, 1.0 / values, 0.0)


def first_kernel(
    own_shifts, mate_shifts, wave, facing_wave, preconditioner, own_left, mate_left, own_right,
    mate_right, image_ref, row_ref, left_high, left_low, right_high, right_low, high, low,
):
    op = lax.axis_index("op")
    sources = term_sources(own_shifts, mate_shifts)
    for place, values in enumerate((wave[op], wave[1 - op], facing_wave[...])):
        high[place], low[place] = split(values)
    count = own_left.shape[0]
    for half, (left, right) in enumerate(((own_left, own_right), (mate_left, mate_right))):
        for term in range(count):
            place = half * count + term
            left_high[place], left_low[place] = split(left[term, op])
            right_high[place], right_low[place] = split(right[term, op])
    image = apply_terms(sources, (high, low), (left_high, left_low), (right_high, right_low))
    image_ref[...] = image
    own = wave[op]
    factors = factors_of([own], image, inverted(preconditioner[op])) + [(own, own)]
    row_ref[...] = row_of_sums(factors, row_ref.shape[0])


def second_kernel(
    total, own_shifts, mate_shifts, rows, wave, facing_wave, preconditioner, facing_preconditioner,
    own_image, mate_image, facing_image, left_high, left_low, right_high, right_low,
    image_ref, row_ref, start_ref, first_ref, inverse_ref, theta_ref, high, low,
):
    op = lax.axis_index("op")
    sources = term_sources(own_shifts, mate_shifts)
    factor, sums = start_factors(summed(rows, total))
    step = step_factors(sums, 1)
    theta_ref[...] = jnp.broadcast_to(step[0], theta_ref.shape)
    waves = (wave[op], wave[1 - op], facing_wave[...])
    divisors = (preconditioner[op], preconditioner[1 - op], facing_preconditioner[...])
    images = (own_image, mate_image, facing_image)
    for place in range(3):
        start = waves[place] * factor
        inverse = inverted(divisors[place])
        first = fresh(step, images[place][...] * factor, inverse, [start])
        start_ref[place] = start
        inverse_ref[place] = inverse
        first_ref[place] = first
        high[place], low[place] = split(first)
    image = apply_terms(sources, (high, low), (left_high, left_low), (right_high, right_low))
    image_ref[...] = image
    factors = factors_of([start_ref[0], first_ref[0]], image, inverse_ref[0])
    row_ref[...] = row_of_sums(factors, row_ref.shape[0])


def third_kernel(
    total, own_shifts, mate_shifts, rows, start, first, inverse,
    own_image, mate_image, facing_image, left_high, left_low, right_high, right_low,
    kept_ref, sent_ref, row_ref, second_ref, theta_ref, high, low,
):
    op = lax.axis_index("op")
    sources = term_sources(own_shifts, mate_shifts)
    step = step_factors(summed(rows, total), 2)
    theta_ref[...] = jnp.broadcast_to(step[0], theta_ref.shape)
    images = (own_image, mate_image, facing_image)
    for place in range(3):
        second = fresh(step, images[place][...], inverse[place], [start[place], first[place]])
        if place < 2:
            second_ref[place] = second
        high[place], low[place] = split(second)
    image = apply_terms(sources, (high, low), (left_high, left_low), (right_high, right_low))
    half = kept_ref.shape[0]
    kept_ref[...] = jnp.where(op == 0, image[:half], image[half:])
    sent_ref[...] = jnp.where(op == 0, image[half:], image[:half])
    factors = factors_of([start[0], first[0], second_ref[0]], image, inverse[0])
    row_ref[...] = row_of_sums(factors, row_ref.shape[0])


def last_kernel(
    total, rows, first_theta, second_theta, start, first, second, inverse, own_image, mate_image,
    basis_ref, ritz_ref,
):
    op = lax.axis_index("op")
    step = step_factors(summed(rows, total), 3)
    half = own_image.shape[0]
    mine = pl.ds(pl.multiple_of(op * half, half), half)
    for place, (image, sector) in enumerate(((own_image, op), (mate_image, 1 - op))):
        members = [member[place, mine] for member in (start, first, second)]
        basis_ref[0, sector] = members[1]
        basis_ref[1, sector] = members[2]
        basis_ref[2, sector] = fresh(step, image[...], inverse[place, mine], members)
    for position, theta in enumerate((first_theta[...], second_theta[...], step[0])):
        ritz_ref[position] = theta[0, 0]


def one_sector_body(wave_start, left_blocks, right_blocks, term_shifts, preconditioner):
    op = lax.axis_index("op")
    chips = lax.axis_size("sector")
    devices = 2 * chips
    rows, columns = wave_start.shape[1:]
    half = rows // 2
    terms = 2 * left_blocks.shape[0]
    total = float(devices * rows * columns)
    swap = [(i, i ^ 1) for i in range(devices)]
    across = [(i, i + 1) for i in range(1, devices - 1, 2)]
    across = across + [(j, i) for i, j in across]

    def mate(values):
        return lax.ppermute(values, AXES, swap)

    def facing(values):
        return lax.ppermute(values, AXES, across)

    def own_sector(values):
        return lax.dynamic_index_in_dim(values, op, 0, keepdims=False)

    def exchanged(row):
        spread = row.reshape(devices, 1, LANES)
        return lax.all_to_all(spread, AXES, 0, 0, tiled=True).reshape(devices, LANES)

    vmem = pl.BlockSpec(memory_space=pltpu.VMEM)
    smem = pl.BlockSpec(memory_space=pltpu.SMEM)

    def call(kernel, operands, shapes, scalars=0, out_scalars=0, scratch=True):
        return pl.pallas_call(
            kernel,
            out_shape=[jax.ShapeDtypeStruct(shape, kind) for shape, kind in shapes],
            in_specs=[smem] * scalars + [vmem] * (len(operands) - scalars),
            out_specs=[vmem] * (len(shapes) - out_scalars) + [smem] * out_scalars,
            scratch_shapes=[pltpu.VMEM((3, rows, columns), jnp.bfloat16)] * (2 if scratch else 0),
            compiler_params=pltpu.CompilerParams(vmem_limit_bytes=32 * 2**20),
        )(*operands)

    block = (rows, columns)
    f32, bf16 = jnp.float32, jnp.bfloat16
    row_shape = ((devices, LANES), f32)
    theta_shape = ((1, LANES), f32)

    facing_wave = facing(own_sector(wave_start))
    facing_preconditioner = facing(own_sector(preconditioner))
    mate_left = mate(left_blocks)
    mate_right = mate(right_blocks)
    shifts = (term_shifts, mate(term_shifts))

    split_shape = ((terms,) + left_blocks.shape[2:], bf16)
    image, row, *blocks = call(
        first_kernel,
        (*shifts, wave_start, facing_wave, preconditioner, left_blocks, mate_left, right_blocks,
         mate_right),
        [(block, f32), row_shape] + [split_shape] * 4,
        scalars=2,
    )
    images = (image, mate(image), facing(image))
    image, row, start, first, inverse, first_theta = call(
        functools.partial(second_kernel, total),
        (*shifts, exchanged(row), wave_start, facing_wave, preconditioner, facing_preconditioner,
         *images, *blocks),
        [(block, f32), row_shape] + [((3,) + block, f32)] * 3 + [theta_shape],
        scalars=2,
    )
    images = (image, mate(image), facing(image))
    kept, sent, row, second, second_theta = call(
        functools.partial(third_kernel, total),
        (*shifts, exchanged(row), start, first, inverse, *images, *blocks),
        [((half, columns), f32)] * 2 + [row_shape, ((2,) + block, f32), theta_shape],
        scalars=2,
    )
    basis, ritz = call(
        functools.partial(last_kernel, total),
        (exchanged(row), first_theta, second_theta, start, first, second, inverse, kept,
         mate(sent)),
        [((ITERS, 2, half, columns), f32), ((ITERS,), f32)],
        out_scalars=1,
        scratch=False,
    )
    return (basis, ritz)


def with_halo(cells, sides, width):
    for axis, dim in sides:
        count = lax.axis_size(axis)
        ends = count - 1
        head = lax.slice_in_dim(cells, 0, width, axis=dim)
        tail = lax.slice_in_dim(cells, cells.shape[dim] - width, cells.shape[dim], axis=dim)
        cells = jnp.concatenate(
            [
                lax.ppermute(tail, axis, [(i, (i + 1) % count) for i in range(ends)]),
                cells,
                lax.ppermute(head, axis, [((i + 1) % count, i) for i in range(ends)]),
            ],
            axis=dim,
        )
    return cells


def split_terms_body(wave_start, left_blocks, right_blocks, term_shifts, preconditioner):
    highest = lax.Precision.HIGHEST
    width = wave_start.shape[1]
    row_count = width // lax.axis_size("op")
    first_row = lax.axis_index("op") * row_count
    total = float(wave_start.shape[0] * lax.axis_size("sector") * width * wave_start.shape[2])

    def portion(values):
        return lax.dynamic_slice_in_dim(values, first_row, row_count, axis=values.ndim - 2)

    start_sum = total_sum(jnp.sum(jnp.square(portion(wave_start)))[None])[0] / total
    basis = [wave_start * lax.rsqrt(start_sum + EPSILON)]
    ritz = []
    for _ in range(ITERS):
        latest = basis[-1]
        padded = with_halo(latest, (("sector", 0),), 1)
        shift = term_shifts[:, None, None, None]
        source = jnp.where(
            shift == 1,
            padded[None, :-2],
            jnp.where(shift == -1, padded[None, 2:], padded[None, 1:-1]),
        )
        inner = jnp.einsum("ksab,ksbc->ksac", left_blocks, source, precision=highest)
        image = lax.psum(jnp.einsum("ksac,kscd->sad", inner, right_blocks, precision=highest), "op")
        inverse = 1.0 / preconditioner
        pieces = products([portion(member) for member in basis], portion(image), portion(inverse))
        theta, correlations, scale = coefficients(
            total_sum(jnp.stack(pieces)), total, len(basis)
        )
        ortho = (image - theta * latest) * inverse
        for position, member in enumerate(basis):
            ortho = ortho - correlations[position] * member
        basis.append(ortho * scale)
        ritz.append(theta)
    output = jnp.stack([portion(member) for member in basis[1:]])
    return (output, jnp.stack(ritz))


def solution(mesh):
    placed = (
        P("sector", None, None),
        P("op", "sector", None, None),
        P("op", "sector", None, None),
        P("op"),
        P("sector", None, None),
    )

    def body(wave_start, *operands):
        one_each = mesh.shape["op"] == 2 and wave_start.shape[0] == 2
        return (one_sector_body if one_each else split_terms_body)(wave_start, *operands)

    return jax.shard_map(
        body,
        mesh=mesh,
        in_specs=placed,
        out_specs=(P(None, "sector", "op", None), P()),
        check_vma=False,
    )
```

```python
import functools

import jax
import jax.numpy as jnp
from jax import lax
from jax.experimental import pallas as pl
from jax.experimental.pallas import tpu as pltpu
from jax.sharding import PartitionSpec as P

ITERS = 3


EPSILON = 1e-06

AXES = ("sector", "op")

LANES = 128


def total_sum(values):
    devices = lax.axis_size("sector") * lax.axis_size("op")
    row = jnp.pad(values, (0, LANES - values.shape[0]))
    rows = lax.all_to_all(jnp.broadcast_to(row, (devices, LANES)), AXES, 0, 0, tiled=True)
    return jnp.sum(rows, axis=0)[: values.shape[0]]


def coefficients(sums, total, count):
    sums = sums / total
    theta = sums[0]
    correlations = sums[4 : 4 + count] - theta * sums[4 + count : 4 + 2 * count]
    length = (
        sums[1]
        - 2.0 * theta * sums[2]
        + theta * theta * sums[3]
        - jnp.sum(jnp.square(correlations))
    )
    return theta, correlations, lax.rsqrt(length + EPSILON)


def products(members, image, inverse):
    latest = members[-1]
    ratio_image = image * inverse
    ratio_latest = latest * inverse
    pieces = [
        jnp.sum(latest * image),
        jnp.sum(ratio_image * ratio_image),
        jnp.sum(ratio_image * ratio_latest),
        jnp.sum(ratio_latest * ratio_latest),
    ]
    pieces = pieces + [jnp.sum(member * ratio_image) for member in members]
    pieces = pieces + [jnp.sum(member * ratio_latest) for member in members]
    return pieces


def split(values):
    high = values.astype(jnp.bfloat16)
    return high, (values - high.astype(jnp.float32)).astype(jnp.bfloat16)


def dot_split(lhs_high, lhs_low, rhs_high, rhs_low):
    dot = functools.partial(jnp.dot, preferred_element_type=jnp.float32)
    return dot(lhs_high, rhs_high) + (dot(lhs_low, rhs_high) + dot(lhs_high, rhs_low))


def apply_terms(sources, vectors, left, right):
    left_high, left_low = left
    right_high, right_low = right
    vector_high, vector_low = vectors
    image = None
    for term, source in enumerate(sources):
        inner = dot_split(left_high[term], left_low[term], vector_high[source], vector_low[source])
        part = dot_split(*split(inner), right_high[term], right_low[term])
        image = part if image is None else image + part
    return image


def term_sources(own_shifts, mate_shifts):
    toward_mate = jnp.where(lax.axis_index("op") == 0, -1, 1)
    shifts = [refs[i] for refs in (own_shifts, mate_shifts) for i in range(refs.shape[0])]
    return [
        jnp.where(shift == 0, 0, jnp.where(shift == toward_mate, 1, 2)) for shift in shifts
    ]


def row_of_sums(factors, devices):
    lane = lax.broadcasted_iota(jnp.int32, (1, LANES), 1)
    row = jnp.zeros((1, LANES), jnp.float32)
    for position, (one, other) in enumerate(factors):
        product = (one * other).reshape(-1, 8, one.shape[1])
        whole = jnp.sum(jnp.sum(product, axis=0), axis=(0, 1), keepdims=True)
        row = jnp.where(lane == position, whole, row)
    return jnp.broadcast_to(row, (devices, LANES))


def factors_of(members, image, inverse):
    latest = members[-1]
    ratio_image = image * inverse
    ratio_latest = latest * inverse
    factors = [
        (latest, image),
        (ratio_image, ratio_image),
        (ratio_image, ratio_latest),
        (ratio_latest, ratio_latest),
    ]
    factors = factors + [(member, ratio_image) for member in members]
    return factors + [(member, ratio_latest) for member in members]


def summed(rows, total):
    whole = jnp.sum(rows[...], axis=0, keepdims=True) / total
    return [whole[:, i : i + 1] for i in range(10)]


def step_factors(sums, count):
    theta = sums[0]
    correlations = [sums[4 + i] - theta * sums[4 + count + i] for i in range(count)]
    length = sums[1] - 2.0 * theta * sums[2] + theta * theta * sums[3]
    for correlation in correlations:
        length = length - correlation * correlation
    return theta, correlations, lax.rsqrt(length + EPSILON)


def fresh(step, image, inverse, members):
    theta, correlations, scale = step
    ortho = (image - theta * members[-1]) * inverse
    for correlation, member in zip(correlations, members):
        ortho = ortho - correlation * member
    return ortho * scale


def start_factors(sums):
    factor = lax.rsqrt(sums[6] + EPSILON)
    return factor, [value * (factor * factor) for value in sums[:6]]


def inverted(values):
    return jnp.where(values > 0.0, 1.0 / values, 0.0)


def picking_kernel(
    wave, preconditioner, left, right, own_wave, own_preconditioner, own_left, own_right, sent_left,
    sent_right, picked,
):
    op = lax.axis_index("op")
    pairs = [(wave.at[op], own_wave), (preconditioner.at[op], own_preconditioner)]
    for values, own, sent in ((left, own_left, sent_left), (right, own_right, sent_right)):
        for term in range(values.shape[0]):
            pairs.append((values.at[term, 1 - op], sent.at[term]))
            pairs.append((values.at[term, op], own.at[term]))
    copies = [
        pltpu.make_async_copy(source, target, picked.at[i])
        for i, (source, target) in enumerate(pairs)
    ]
    for copy in copies:
        copy.start()
    for copy in copies:
        copy.wait()


def blocks_kernel(
    own_left, mate_left, own_right, mate_right, left_high, left_low, right_high, right_low
):
    count = own_left.shape[0]
    for half, pair in enumerate(((own_left, own_right), (mate_left, mate_right))):
        for values, high, low in zip(pair, (left_high, right_high), (left_low, right_low)):
            for term in range(count):
                high[half * count + term], low[half * count + term] = split(values[term])


def first_kernel(
    own_shifts, mate_shifts, wave, facing_wave, preconditioner, left_high, left_low, right_high,
    right_low, image_ref, row_ref, high, low,
):
    op = lax.axis_index("op")
    sources = term_sources(own_shifts, mate_shifts)
    for place, values in enumerate((wave[op], wave[1 - op], facing_wave[...])):
        high[place], low[place] = split(values)
    image = apply_terms(sources, (high, low), (left_high, left_low), (right_high, right_low))
    image_ref[...] = image
    own = wave[op]
    factors = factors_of([own], image, inverted(preconditioner[op])) + [(own, own)]
    row_ref[...] = row_of_sums(factors, row_ref.shape[0])


def second_kernel(
    total, own_shifts, mate_shifts, rows, wave, facing_wave, preconditioner, facing_preconditioner,
    own_image, mate_image, facing_image, left_high, left_low, right_high, right_low,
    image_ref, row_ref, start_ref, first_ref, inverse_ref, theta_ref, high, low,
):
    op = lax.axis_index("op")
    sources = term_sources(own_shifts, mate_shifts)
    factor, sums = start_factors(summed(rows, total))
    step = step_factors(sums, 1)
    theta_ref[...] = jnp.broadcast_to(step[0], theta_ref.shape)
    waves = (wave[op], wave[1 - op], facing_wave[...])
    divisors = (preconditioner[op], preconditioner[1 - op], facing_preconditioner[...])
    images = (own_image, mate_image, facing_image)
    for place in range(3):
        start = waves[place] * factor
        inverse = inverted(divisors[place])
        first = fresh(step, images[place][...] * factor, inverse, [start])
        start_ref[place] = start
        inverse_ref[place] = inverse
        first_ref[place] = first
        high[place], low[place] = split(first)
    image = apply_terms(sources, (high, low), (left_high, left_low), (right_high, right_low))
    image_ref[...] = image
    factors = factors_of([start_ref[0], first_ref[0]], image, inverse_ref[0])
    row_ref[...] = row_of_sums(factors, row_ref.shape[0])


def third_kernel(
    total, own_shifts, mate_shifts, rows, start, first, inverse,
    own_image, mate_image, facing_image, left_high, left_low, right_high, right_low,
    kept_ref, sent_ref, row_ref, second_ref, theta_ref, high, low,
):
    op = lax.axis_index("op")
    sources = term_sources(own_shifts, mate_shifts)
    step = step_factors(summed(rows, total), 2)
    theta_ref[...] = jnp.broadcast_to(step[0], theta_ref.shape)
    images = (own_image, mate_image, facing_image)
    for place in range(3):
        second = fresh(step, images[place][...], inverse[place], [start[place], first[place]])
        if place < 2:
            second_ref[place] = second
        high[place], low[place] = split(second)
    image = apply_terms(sources, (high, low), (left_high, left_low), (right_high, right_low))
    half = kept_ref.shape[0]
    kept_ref[...] = jnp.where(op == 0, image[:half], image[half:])
    sent_ref[...] = jnp.where(op == 0, image[half:], image[:half])
    factors = factors_of([start[0], first[0], second_ref[0]], image, inverse[0])
    row_ref[...] = row_of_sums(factors, row_ref.shape[0])


def last_kernel(
    total, rows, first_theta, second_theta, start, first, second, inverse, own_image, mate_image,
    basis_ref, ritz_ref,
):
    op = lax.axis_index("op")
    step = step_factors(summed(rows, total), 3)
    half = own_image.shape[0]
    mine = pl.ds(pl.multiple_of(op * half, half), half)
    for place, (image, sector) in enumerate(((own_image, op), (mate_image, 1 - op))):
        members = [member[place, mine] for member in (start, first, second)]
        basis_ref[0, sector] = members[1]
        basis_ref[1, sector] = members[2]
        basis_ref[2, sector] = fresh(step, image[...], inverse[place, mine], members)
    for position, theta in enumerate((first_theta[...], second_theta[...], step[0])):
        ritz_ref[position] = theta[0, 0]


def one_sector_body(wave_start, left_blocks, right_blocks, term_shifts, preconditioner):
    op = lax.axis_index("op")
    chips = lax.axis_size("sector")
    devices = 2 * chips
    rows, columns = wave_start.shape[1:]
    half = rows // 2
    terms = 2 * left_blocks.shape[0]
    total = float(devices * rows * columns)
    swap = [(i, i ^ 1) for i in range(devices)]
    across = [(i, i + 1) for i in range(1, devices - 1, 2)]
    across = across + [(j, i) for i, j in across]

    def mate(values):
        return lax.ppermute(values, AXES, swap)

    def facing(values):
        return lax.ppermute(values, AXES, across)

    def own_sector(values):
        return lax.dynamic_index_in_dim(values, op, 0, keepdims=False)

    def exchanged(row):
        spread = row.reshape(devices, 1, LANES)
        return lax.all_to_all(spread, AXES, 0, 0, tiled=True).reshape(devices, LANES)

    vmem = pl.BlockSpec(memory_space=pltpu.VMEM)
    smem = pl.BlockSpec(memory_space=pltpu.SMEM)

    def call(kernel, operands, shapes, scalars=0, out_scalars=0, scratch=True):
        return pl.pallas_call(
            kernel,
            out_shape=[jax.ShapeDtypeStruct(shape, kind) for shape, kind in shapes],
            in_specs=[smem] * scalars + [vmem] * (len(operands) - scalars),
            out_specs=[vmem] * (len(shapes) - out_scalars) + [smem] * out_scalars,
            scratch_shapes=[pltpu.VMEM((3, rows, columns), jnp.bfloat16)] * (2 if scratch else 0),
            compiler_params=pltpu.CompilerParams(vmem_limit_bytes=16 * 2**20),
        )(*operands)

    block = (rows, columns)
    f32, bf16 = jnp.float32, jnp.bfloat16
    row_shape = ((devices, LANES), f32)
    theta_shape = ((1, LANES), f32)

    half_shape = left_blocks.shape[:1] + left_blocks.shape[2:]
    picked_shapes = [block] * 2 + [half_shape] * 4
    own_wave, own_preconditioner, own_left, own_right, sent_left, sent_right = pl.pallas_call(
        picking_kernel,
        out_shape=[jax.ShapeDtypeStruct(shape, f32) for shape in picked_shapes],
        in_specs=[pl.BlockSpec(memory_space=pl.ANY)] * 4,
        out_specs=[pl.BlockSpec(memory_space=pl.ANY)] * 6,
        scratch_shapes=[pltpu.SemaphoreType.DMA((2 + 2 * terms,))],
        compiler_params=pltpu.CompilerParams(vmem_limit_bytes=56 * 2**20),
    )(wave_start, preconditioner, left_blocks, right_blocks)
    facing_wave = facing(own_wave)
    facing_preconditioner = facing(own_preconditioner)
    shifts = (term_shifts, mate(term_shifts))

    blocks = call(
        blocks_kernel,
        (own_left, mate(sent_left), own_right, mate(sent_right)),
        [((terms,) + left_blocks.shape[2:], bf16)] * 4,
        scratch=False,
    )
    image, row = call(
        first_kernel,
        (*shifts, wave_start, facing_wave, preconditioner, *blocks),
        [(block, f32), row_shape],
        scalars=2,
    )
    images = (image, mate(image), facing(image))
    image, row, start, first, inverse, first_theta = call(
        functools.partial(second_kernel, total),
        (*shifts, exchanged(row), wave_start, facing_wave, preconditioner, facing_preconditioner,
         *images, *blocks),
        [(block, f32), row_shape] + [((3,) + block, f32)] * 3 + [theta_shape],
        scalars=2,
    )
    images = (image, mate(image), facing(image))
    kept, sent, row, second, second_theta = call(
        functools.partial(third_kernel, total),
        (*shifts, exchanged(row), start, first, inverse, *images, *blocks),
        [((half, columns), f32)] * 2 + [row_shape, ((2,) + block, f32), theta_shape],
        scalars=2,
    )
    basis, ritz = call(
        functools.partial(last_kernel, total),
        (exchanged(row), first_theta, second_theta, start, first, second, inverse, kept,
         mate(sent)),
        [((ITERS, 2, half, columns), f32), ((ITERS,), f32)],
        out_scalars=1,
        scratch=False,
    )
    return (basis, ritz)


def with_halo(cells, sides, width):
    for axis, dim in sides:
        count = lax.axis_size(axis)
        ends = count - 1
        head = lax.slice_in_dim(cells, 0, width, axis=dim)
        tail = lax.slice_in_dim(cells, cells.shape[dim] - width, cells.shape[dim], axis=dim)
        cells = jnp.concatenate(
            [
                lax.ppermute(tail, axis, [(i, (i + 1) % count) for i in range(ends)]),
                cells,
                lax.ppermute(head, axis, [((i + 1) % count, i) for i in range(ends)]),
            ],
            axis=dim,
        )
    return cells


def split_terms_body(wave_start, left_blocks, right_blocks, term_shifts, preconditioner):
    highest = lax.Precision.HIGHEST
    width = wave_start.shape[1]
    row_count = width // lax.axis_size("op")
    first_row = lax.axis_index("op") * row_count
    total = float(wave_start.shape[0] * lax.axis_size("sector") * width * wave_start.shape[2])

    def portion(values):
        return lax.dynamic_slice_in_dim(values, first_row, row_count, axis=values.ndim - 2)

    start_sum = total_sum(jnp.sum(jnp.square(portion(wave_start)))[None])[0] / total
    basis = [wave_start * lax.rsqrt(start_sum + EPSILON)]
    ritz = []
    for _ in range(ITERS):
        latest = basis[-1]
        padded = with_halo(latest, (("sector", 0),), 1)
        shift = term_shifts[:, None, None, None]
        source = jnp.where(
            shift == 1,
            padded[None, :-2],
            jnp.where(shift == -1, padded[None, 2:], padded[None, 1:-1]),
        )
        inner = jnp.einsum("ksab,ksbc->ksac", left_blocks, source, precision=highest)
        image = lax.psum(jnp.einsum("ksac,kscd->sad", inner, right_blocks, precision=highest), "op")
        inverse = 1.0 / preconditioner
        pieces = products([portion(member) for member in basis], portion(image), portion(inverse))
        theta, correlations, scale = coefficients(
            total_sum(jnp.stack(pieces)), total, len(basis)
        )
        ortho = (image - theta * latest) * inverse
        for position, member in enumerate(basis):
            ortho = ortho - correlations[position] * member
        basis.append(ortho * scale)
        ritz.append(theta)
    output = jnp.stack([portion(member) for member in basis[1:]])
    return (output, jnp.stack(ritz))


def solution(mesh):
    placed = (
        P("sector", None, None),
        P("op", "sector", None, None),
        P("op", "sector", None, None),
        P("op"),
        P("sector", None, None),
    )

    def body(wave_start, *operands):
        one_each = mesh.shape["op"] == 2 and wave_start.shape[0] == 2
        return (one_sector_body if one_each else split_terms_body)(wave_start, *operands)

    return jax.shard_map(
        body,
        mesh=mesh,
        in_specs=placed,
        out_specs=(P(None, "sector", "op", None), P()),
        check_vma=False,
    )
```

```python
import functools

import jax
import jax.numpy as jnp
from jax import lax
from jax.experimental import pallas as pl
from jax.experimental.pallas import tpu as pltpu
from jax.sharding import PartitionSpec as P

ITERS = 3


EPSILON = 1e-06

AXES = ("sector", "op")

LANES = 128


def total_sum(values):
    devices = lax.axis_size("sector") * lax.axis_size("op")
    row = jnp.pad(values, (0, LANES - values.shape[0]))
    rows = lax.all_to_all(jnp.broadcast_to(row, (devices, LANES)), AXES, 0, 0, tiled=True)
    return jnp.sum(rows, axis=0)[: values.shape[0]]


def coefficients(sums, total, count):
    sums = sums / total
    theta = sums[0]
    correlations = sums[4 : 4 + count] - theta * sums[4 + count : 4 + 2 * count]
    length = (
        sums[1]
        - 2.0 * theta * sums[2]
        + theta * theta * sums[3]
        - jnp.sum(jnp.square(correlations))
    )
    return theta, correlations, lax.rsqrt(length + EPSILON)


def products(members, image, inverse):
    latest = members[-1]
    ratio_image = image * inverse
    ratio_latest = latest * inverse
    pieces = [
        jnp.sum(latest * image),
        jnp.sum(ratio_image * ratio_image),
        jnp.sum(ratio_image * ratio_latest),
        jnp.sum(ratio_latest * ratio_latest),
    ]
    pieces = pieces + [jnp.sum(member * ratio_image) for member in members]
    pieces = pieces + [jnp.sum(member * ratio_latest) for member in members]
    return pieces


def split(values):
    high = values.astype(jnp.bfloat16)
    return high, (values - high.astype(jnp.float32)).astype(jnp.bfloat16)


def dot_split(lhs_high, lhs_low, rhs_high, rhs_low):
    dot = functools.partial(jnp.dot, preferred_element_type=jnp.float32)
    return dot(lhs_high, rhs_high) + (dot(lhs_low, rhs_high) + dot(lhs_high, rhs_low))


def apply_terms(sources, vectors, left, right):
    left_high, left_low = left
    right_high, right_low = right
    vector_high, vector_low = vectors
    image = None
    for term, source in enumerate(sources):
        inner = dot_split(left_high[term], left_low[term], vector_high[source], vector_low[source])
        part = dot_split(*split(inner), right_high[term], right_low[term])
        image = part if image is None else image + part
    return image


def term_sources(own_shifts, mate_shifts):
    toward_mate = jnp.where(lax.axis_index("op") == 0, -1, 1)
    shifts = [refs[i] for refs in (own_shifts, mate_shifts) for i in range(refs.shape[0])]
    return [
        jnp.where(shift == 0, 0, jnp.where(shift == toward_mate, 1, 2)) for shift in shifts
    ]


def row_of_sums(factors, first=0, row=None):
    lane = lax.broadcasted_iota(jnp.int32, (1, LANES), 1)
    if row is None:
        row = jnp.zeros((1, LANES), jnp.float32)
    for position, (one, other) in enumerate(factors):
        product = (one * other).reshape(-1, 8, one.shape[1])
        whole = jnp.sum(jnp.sum(product, axis=0), axis=(0, 1), keepdims=True)
        row = jnp.where(lane == first + position, whole, row)
    return row


def summed(rows, total, count):
    whole = jnp.sum(rows[...], axis=0, keepdims=True) * (1.0 / total)
    return [jnp.broadcast_to(whole[:, i : i + 1], (8, LANES)) for i in range(count)]


def one_of(value):
    return value[:1, :1]


EARLY_MOMENTS = (
    [("w", "w", n) for n in range(5)]
    + [("u", "w", n) for n in range(5)]
    + [("u", "u", n) for n in range(1, 5)]
    + [("a", "w", n) for n in range(4)]
    + [("a", "u", n) for n in range(1, 4)]
    + [("a", "a", 2)]
)
LATE_MOMENTS = (
    [("b", "w", n) for n in range(4)]
    + [("b", "u", n) for n in range(1, 4)]
    + [("a", "b", 2), ("b", "b", 2)]
)

H_OF = {("w", 0): "u", ("w", 1): "a", ("u", 1): "b"}

START_SCALE = 2.0**10
H_SCALE = 2.0**7


def moment_factors(moments, arrays, inverse):
    powers = {(name, 0): values for name, values in arrays.items()}

    def power(name, n):
        if (name, n) not in powers:
            powers[name, n] = power(name, n - 1) * inverse
        return powers[name, n]

    return [(power(x, n // 2), power(y, n - n // 2)) for x, y, n in moments]


def plus(vector, other, factor):
    result = dict(vector)
    for word, value in other.items():
        term = value * factor
        result[word] = result[word] + term if word in result else term
    return result


def times_inverse(vector):
    return {(name, n + 1): value for (name, n), value in vector.items()}


def times_h(vector):
    return {(H_OF[word], 0): value * H_SCALE for word, value in vector.items()}


def inner(one, other, moments):
    result = None
    for (x, n), value in one.items():
        part = None
        for (y, m), factor in other.items():
            term = factor * moments[tuple(sorted((x, y))) + (n + m,)]
            part = term if part is None else part + term
        part = value * part
        result = part if result is None else result + part
    return result


def first_two_steps(sums):
    moments = dict(zip(EARLY_MOMENTS + LATE_MOMENTS, sums))
    basis = [{("w", 0): lax.rsqrt(moments["w", "w", 0] + EPSILON * START_SCALE**2)}]
    thetas = []
    for _ in range(2):
        latest = basis[-1]
        image = times_h(latest)
        theta = inner(latest, image, moments)
        correction = times_inverse(plus(image, latest, -theta))
        ortho = correction
        for member in basis:
            ortho = plus(ortho, member, -inner(member, correction, moments))
        scale = lax.rsqrt(inner(ortho, ortho, moments) + EPSILON)
        basis.append({word: value * scale for word, value in ortho.items()})
        thetas.append(theta)
    return basis, thetas


def combined(vector, arrays, inverse):
    words = {name: (n, values) for (name, n), values in arrays.items()}
    result = None
    for n in range(max(n for _, n in vector), -1, -1):
        if result is not None:
            result = result * inverse
        for (name, m), value in vector.items():
            held, values = words[name]
            if m - held == n:
                term = one_of(value) * values
                result = term if result is None else result + term
    return result


def inverted(values):
    return jnp.where(values > 0.0, 1.0 / values, 0.0)


def copy_all(pairs, arrived):
    copies = [
        pltpu.make_async_copy(source, target, arrived.at[i])
        for i, (source, target) in enumerate(pairs)
    ]
    for copy in copies:
        copy.start()
    for copy in copies:
        copy.wait()


def picking_kernel(
    wave, preconditioner, left, right, own_wave, own_preconditioner, sent_left, sent_right, arrived
):
    op = lax.axis_index("op")
    pairs = [(wave.at[op], own_wave), (preconditioner.at[op], own_preconditioner)]
    for values, sent in ((left, sent_left), (right, sent_right)):
        for term in range(values.shape[0]):
            pairs.append((values.at[term, 1 - op], sent.at[term]))
    copy_all(pairs, arrived)


def splitting_kernel(
    wave, facing_wave, own_left, own_right, mate_left, mate_right, start_ref, high, low, left_high,
    left_low, right_high, right_low,
):
    op = lax.axis_index("op")
    for place, values in enumerate((wave[op], wave[1 - op], facing_wave[...])):
        start = values * START_SCALE
        start_ref[place] = start
        high[place], low[place] = split(start)
    count = own_left.shape[0]
    for term in range(count):
        left_high[term], left_low[term] = split(own_left[term, op] * (1.0 / H_SCALE))
        right_high[term], right_low[term] = split(own_right[term, op])
        place = count + term
        left_high[place], left_low[place] = split(mate_left[term] * (1.0 / H_SCALE))
        right_high[place], right_low[place] = split(mate_right[term])


def first_kernel(
    own_shifts, mate_shifts, high, low, left_high, left_low, right_high, right_low, image_ref
):
    sources = term_sources(own_shifts, mate_shifts)
    image_ref[...] = apply_terms(
        sources, (high, low), (left_high, left_low), (right_high, right_low)
    )


def side_kernel(
    own_shifts, mate_shifts, start, preconditioner, facing_preconditioner, image,
    left_high, left_low, right_high, right_low, side_ref, row_ref, inverse_ref, high, low,
):
    op = lax.axis_index("op")
    sources = term_sources(own_shifts, mate_shifts)
    divisors = (preconditioner[op], preconditioner[1 - op], facing_preconditioner[...])
    for place in range(3):
        inverse = inverted(divisors[place])
        inverse_ref[place] = inverse
        high[place], low[place] = split(start[place] * inverse)
    side = apply_terms(sources, (high, low), (left_high, left_low), (right_high, right_low))
    side_ref[...] = side
    arrays = {"w": start[0], "u": image[...], "a": side}
    row_ref[...] = row_of_sums(moment_factors(EARLY_MOMENTS, arrays, inverse_ref[0]))


def second_kernel(
    own_shifts, mate_shifts, start, own_image, mate_image, facing_image, inverse, side, early_row,
    left_high, left_low, right_high, right_low, image_ref, row_ref, ratio_ref, high, low,
):
    sources = term_sources(own_shifts, mate_shifts)
    for place, image in enumerate((own_image, mate_image, facing_image)):
        ratio = image[...] * inverse[place]
        ratio_ref[place] = ratio
        high[place], low[place] = split(ratio)
    image = apply_terms(sources, (high, low), (left_high, left_low), (right_high, right_low))
    image_ref[...] = image
    arrays = {"w": start[0], "u": own_image[...], "a": side[...], "b": image}
    factors = moment_factors(LATE_MOMENTS, arrays, inverse[0])
    row = row_of_sums(factors, len(EARLY_MOMENTS), early_row[...])
    row_ref[...] = jnp.broadcast_to(row, row_ref.shape)


MEMBER_PAIRS = [(i, j) for i in range(3) for j in range(i + 1)]


def third_kernel(
    total, own_shifts, mate_shifts, rows, start, inverse, ratio, own_side, mate_side,
    facing_side, own_second, mate_second, facing_second, left_high, left_low, right_high, right_low,
    kept_ref, sent_ref, row_ref, members_ref, theta_ref, high, low,
):
    op = lax.axis_index("op")
    sources = term_sources(own_shifts, mate_shifts)
    count = len(EARLY_MOMENTS + LATE_MOMENTS)
    basis, thetas = first_two_steps(summed(rows, total, count))
    for position, theta in enumerate(thetas):
        theta_ref[position] = theta
    half = kept_ref.shape[0]
    sides = (own_side, mate_side, facing_side)
    seconds = (own_second, mate_second, facing_second)

    def mine(values):
        return jnp.where(op == 0, values[:half], values[half:])

    for place in range(3):
        arrays = {
            ("w", 0): start[place],
            ("u", 1): ratio[place],
            ("a", 0): sides[place][...],
            ("b", 0): seconds[place][...],
        }
        latest = combined(basis[2], arrays, inverse[place])
        high[place], low[place] = split(latest)
        if place < 2:
            members = [combined(vector, arrays, inverse[place]) for vector in basis[:2]] + [latest]
            for position, member in enumerate(members):
                members_ref[position, place] = mine(member)
            if place == 0:
                own_members = members
    image = H_SCALE * apply_terms(
        sources, (high, low), (left_high, left_low), (right_high, right_low)
    )
    kept_ref[...] = mine(image)
    sent_ref[...] = jnp.where(op == 0, image[half:], image[:half])
    members = own_members
    ratio_image = image * inverse[0]
    ratio_latest = members[-1] * inverse[0]
    factors = [
        (members[-1], image),
        (ratio_image, ratio_image),
        (ratio_image, ratio_latest),
        (ratio_latest, ratio_latest),
    ]
    factors = factors + [(member, ratio_image) for member in members]
    factors = factors + [(member, ratio_latest) for member in members]
    factors = factors + [(members[i], members[j]) for i, j in MEMBER_PAIRS]
    row_ref[...] = jnp.broadcast_to(row_of_sums(factors), row_ref.shape)


def last_kernel(
    total, rows, thetas, members, inverse, own_image, mate_image, basis_ref, ritz_ref
):
    op = lax.axis_index("op")
    sums = summed(rows, total, 10 + len(MEMBER_PAIRS))
    theta = sums[0]
    correlations = [sums[4 + i] - theta * sums[7 + i] for i in range(3)]
    length = sums[1] - 2.0 * theta * sums[2] + theta * theta * sums[3]
    for correlation in correlations:
        length = length - 2.0 * correlation * correlation
    for (i, j), value in zip(MEMBER_PAIRS, sums[10:]):
        length = length + (1.0 if i == j else 2.0) * correlations[i] * correlations[j] * value
    scale = lax.rsqrt(length + EPSILON)
    half = own_image.shape[0]
    mine = pl.ds(pl.multiple_of(op * half, half), half)
    for place, (image, sector) in enumerate(((own_image, op), (mate_image, 1 - op))):
        basis_ref[0, sector] = members[1, place]
        basis_ref[1, sector] = members[2, place]
        ortho = (image[...] - one_of(theta) * members[2, place]) * inverse[place, mine]
        for i, correlation in enumerate(correlations):
            ortho = ortho - one_of(correlation) * members[i, place]
        basis_ref[2, sector] = ortho * one_of(scale)
    for position, value in enumerate((thetas[0], thetas[1], theta)):
        ritz_ref[position] = value[0, 0]


def one_sector_body(wave_start, left_blocks, right_blocks, term_shifts, preconditioner):
    op = lax.axis_index("op")
    chips = lax.axis_size("sector")
    devices = 2 * chips
    rows, columns = wave_start.shape[1:]
    half = rows // 2
    terms = 2 * left_blocks.shape[0]
    total = float(devices * rows * columns)
    swap = [(i, i ^ 1) for i in range(devices)]
    across = [(i, i + 1) for i in range(1, devices - 1, 2)]
    across = across + [(j, i) for i, j in across]

    def mate(values):
        return lax.ppermute(values, AXES, swap)

    def facing(values):
        return lax.ppermute(values, AXES, across)

    def own_sector(values):
        return lax.dynamic_index_in_dim(values, op, 0, keepdims=False)

    def exchanged(row):
        spread = row.reshape(devices, 1, LANES)
        return lax.all_to_all(spread, AXES, 0, 0, tiled=True).reshape(devices, LANES)

    vmem = pl.BlockSpec(memory_space=pltpu.VMEM)
    smem = pl.BlockSpec(memory_space=pltpu.SMEM)

    def call(kernel, operands, shapes, scalars=0, out_scalars=0, scratch=True):
        return pl.pallas_call(
            kernel,
            out_shape=[jax.ShapeDtypeStruct(shape, kind) for shape, kind in shapes],
            in_specs=[smem] * scalars + [vmem] * (len(operands) - scalars),
            out_specs=[vmem] * (len(shapes) - out_scalars) + [smem] * out_scalars,
            scratch_shapes=[pltpu.VMEM((3, rows, columns), jnp.bfloat16)] * (2 if scratch else 0),
            compiler_params=pltpu.CompilerParams(vmem_limit_bytes=16 * 2**20),
        )(*operands)

    block = (rows, columns)
    f32, bf16 = jnp.float32, jnp.bfloat16
    row_shape = ((devices, LANES), f32)

    half_shape = left_blocks.shape[:1] + left_blocks.shape[2:]
    own_wave, own_preconditioner, sent_left, sent_right = pl.pallas_call(
        picking_kernel,
        out_shape=[jax.ShapeDtypeStruct(shape, f32) for shape in [block] * 2 + [half_shape] * 2],
        in_specs=[pl.BlockSpec(memory_space=pl.ANY)] * 4,
        out_specs=[vmem] * 4,
        scratch_shapes=[pltpu.SemaphoreType.DMA((2 + terms,))],
        compiler_params=pltpu.CompilerParams(vmem_limit_bytes=56 * 2**20),
    )(wave_start, preconditioner, left_blocks, right_blocks)
    facing_wave = facing(own_wave)
    facing_preconditioner = facing(own_preconditioner)
    mate_left, mate_right = mate(sent_left), mate(sent_right)
    shifts = (term_shifts, mate(term_shifts))

    split_shape = (terms,) + left_blocks.shape[2:]
    start, start_high, start_low, *blocks = call(
        splitting_kernel,
        (wave_start, facing_wave, left_blocks, right_blocks, mate_left, mate_right),
        [((3,) + block, f32)] + [((3,) + block, bf16)] * 2 + [(split_shape, bf16)] * 4,
        scratch=False,
    )
    def around(values):
        return (values, mate(values), facing(values))

    (image,) = call(
        first_kernel,
        (*shifts, start_high, start_low, *blocks),
        [(block, f32)],
        scalars=2,
        scratch=False,
    )
    images = around(image)
    side, early_row, inverse = call(
        side_kernel,
        (*shifts, start, preconditioner, facing_preconditioner, image, *blocks),
        [(block, f32), ((1, LANES), f32), ((3,) + block, f32)],
        scalars=2,
    )
    sides = around(side)
    second, row, ratio = call(
        second_kernel,
        (*shifts, start, *images, inverse, side, early_row, *blocks),
        [(block, f32), row_shape, ((3,) + block, f32)],
        scalars=2,
    )
    seconds = around(second)
    row, *sides = lax.optimization_barrier((row, *sides))
    half_block = (half, columns)
    kept, sent, row, members, thetas = call(
        functools.partial(third_kernel, total),
        (*shifts, exchanged(row), start, inverse, ratio, *sides, *seconds, *blocks),
        [(half_block, f32)] * 2 + [row_shape, ((3, 2) + half_block, f32), ((2, 8, LANES), f32)],
        scalars=2,
    )
    basis, ritz = call(
        functools.partial(last_kernel, total),
        (exchanged(row), thetas, members, inverse, kept, mate(sent)),
        [((ITERS, 2) + half_block, f32), ((ITERS,), f32)],
        out_scalars=1,
        scratch=False,
    )
    return (basis, ritz)


def with_halo(cells, sides, width):
    for axis, dim in sides:
        count = lax.axis_size(axis)
        ends = count - 1
        head = lax.slice_in_dim(cells, 0, width, axis=dim)
        tail = lax.slice_in_dim(cells, cells.shape[dim] - width, cells.shape[dim], axis=dim)
        cells = jnp.concatenate(
            [
                lax.ppermute(tail, axis, [(i, (i + 1) % count) for i in range(ends)]),
                cells,
                lax.ppermute(head, axis, [((i + 1) % count, i) for i in range(ends)]),
            ],
            axis=dim,
        )
    return cells


def split_terms_body(wave_start, left_blocks, right_blocks, term_shifts, preconditioner):
    highest = lax.Precision.HIGHEST
    width = wave_start.shape[1]
    row_count = width // lax.axis_size("op")
    first_row = lax.axis_index("op") * row_count
    total = float(wave_start.shape[0] * lax.axis_size("sector") * width * wave_start.shape[2])

    def portion(values):
        return lax.dynamic_slice_in_dim(values, first_row, row_count, axis=values.ndim - 2)

    start_sum = total_sum(jnp.sum(jnp.square(portion(wave_start)))[None])[0] / total
    basis = [wave_start * lax.rsqrt(start_sum + EPSILON)]
    ritz = []
    for _ in range(ITERS):
        latest = basis[-1]
        padded = with_halo(latest, (("sector", 0),), 1)
        shift = term_shifts[:, None, None, None]
        source = jnp.where(
            shift == 1,
            padded[None, :-2],
            jnp.where(shift == -1, padded[None, 2:], padded[None, 1:-1]),
        )
        inner = jnp.einsum("ksab,ksbc->ksac", left_blocks, source, precision=highest)
        image = lax.psum(jnp.einsum("ksac,kscd->sad", inner, right_blocks, precision=highest), "op")
        inverse = 1.0 / preconditioner
        pieces = products([portion(member) for member in basis], portion(image), portion(inverse))
        theta, correlations, scale = coefficients(
            total_sum(jnp.stack(pieces)), total, len(basis)
        )
        ortho = (image - theta * latest) * inverse
        for position, member in enumerate(basis):
            ortho = ortho - correlations[position] * member
        basis.append(ortho * scale)
        ritz.append(theta)
    output = jnp.stack([portion(member) for member in basis[1:]])
    return (output, jnp.stack(ritz))


def solution(mesh):
    placed = (
        P("sector", None, None),
        P("op", "sector", None, None),
        P("op", "sector", None, None),
        P("op"),
        P("sector", None, None),
    )

    def body(wave_start, *operands):
        one_each = mesh.shape["op"] == 2 and wave_start.shape[0] == 2
        return (one_sector_body if one_each else split_terms_body)(wave_start, *operands)

    return jax.shard_map(
        body,
        mesh=mesh,
        in_specs=placed,
        out_specs=(P(None, "sector", "op", None), P()),
        check_vma=False,
    )
```

```python
import functools

import jax
import jax.numpy as jnp
from jax import lax
from jax.experimental import pallas as pl
from jax.experimental.pallas import tpu as pltpu
from jax.sharding import PartitionSpec as P

ITERS = 3


EPSILON = 1e-06

AXES = ("sector", "op")

LANES = 128


def total_sum(values):
    devices = lax.axis_size("sector") * lax.axis_size("op")
    row = jnp.pad(values, (0, LANES - values.shape[0]))
    rows = lax.all_to_all(jnp.broadcast_to(row, (devices, LANES)), AXES, 0, 0, tiled=True)
    return jnp.sum(rows, axis=0)[: values.shape[0]]


def coefficients(sums, total, count):
    sums = sums / total
    theta = sums[0]
    correlations = sums[4 : 4 + count] - theta * sums[4 + count : 4 + 2 * count]
    length = (
        sums[1]
        - 2.0 * theta * sums[2]
        + theta * theta * sums[3]
        - jnp.sum(jnp.square(correlations))
    )
    return theta, correlations, lax.rsqrt(length + EPSILON)


def products(members, image, inverse):
    latest = members[-1]
    ratio_image = image * inverse
    ratio_latest = latest * inverse
    pieces = [
        jnp.sum(latest * image),
        jnp.sum(ratio_image * ratio_image),
        jnp.sum(ratio_image * ratio_latest),
        jnp.sum(ratio_latest * ratio_latest),
    ]
    pieces = pieces + [jnp.sum(member * ratio_image) for member in members]
    pieces = pieces + [jnp.sum(member * ratio_latest) for member in members]
    return pieces


def split(values):
    high = values.astype(jnp.bfloat16)
    return high, (values - high.astype(jnp.float32)).astype(jnp.bfloat16)


def dot_split(lhs_high, lhs_low, rhs_high, rhs_low):
    dot = functools.partial(jnp.dot, preferred_element_type=jnp.float32)
    return dot(lhs_high, rhs_high) + (dot(lhs_low, rhs_high) + dot(lhs_high, rhs_low))


def apply_terms(sources, vectors, left, right):
    left_high, left_low = left
    right_high, right_low = right
    vector_high, vector_low = vectors
    image = None
    for term, source in enumerate(sources):
        inner = dot_split(left_high[term], left_low[term], vector_high[source], vector_low[source])
        part = dot_split(*split(inner), right_high[term], right_low[term])
        image = part if image is None else image + part
    return image


def term_sources(own_shifts, mate_shifts):
    toward_mate = jnp.where(lax.axis_index("op") == 0, -1, 1)
    shifts = [refs[i] for refs in (own_shifts, mate_shifts) for i in range(refs.shape[0])]
    return [
        jnp.where(shift == 0, 0, jnp.where(shift == toward_mate, 1, 2)) for shift in shifts
    ]


def row_of_sums(factors, first=0, row=None):
    lane = lax.broadcasted_iota(jnp.int32, (1, LANES), 1)
    if row is None:
        row = jnp.zeros((1, LANES), jnp.float32)
    for position, (one, other) in enumerate(factors):
        product = (one * other).reshape(-1, 8, one.shape[1])
        whole = jnp.sum(jnp.sum(product, axis=0), axis=(0, 1), keepdims=True)
        row = jnp.where(lane == first + position, whole, row)
    return row


def summed(rows, total, count):
    whole = jnp.sum(rows[...], axis=0, keepdims=True) * (1.0 / total)
    return [jnp.broadcast_to(whole[:, i : i + 1], (8, LANES)) for i in range(count)]


def one_of(value):
    return value[:1, :1]


EARLY_MOMENTS = (
    [("w", "w", n) for n in range(5)]
    + [("u", "w", n) for n in range(5)]
    + [("u", "u", n) for n in range(1, 5)]
    + [("a", "w", n) for n in range(4)]
    + [("a", "u", n) for n in range(1, 4)]
    + [("a", "a", 2)]
)
LATE_MOMENTS = (
    [("b", "w", n) for n in range(4)]
    + [("b", "u", n) for n in range(1, 4)]
    + [("a", "b", 2), ("b", "b", 2)]
)

H_OF = {("w", 0): "u", ("w", 1): "a", ("u", 1): "b"}

START_SCALE = 2.0**10
H_SCALE = 2.0**7


def moment_factors(moments, arrays, inverse):
    powers = {(name, 0): values for name, values in arrays.items()}

    def power(name, n):
        if (name, n) not in powers:
            powers[name, n] = power(name, n - 1) * inverse
        return powers[name, n]

    return [(power(x, n // 2), power(y, n - n // 2)) for x, y, n in moments]


def plus(vector, other, factor):
    result = dict(vector)
    for word, value in other.items():
        term = value * factor
        result[word] = result[word] + term if word in result else term
    return result


def times_inverse(vector):
    return {(name, n + 1): value for (name, n), value in vector.items()}


def times_h(vector):
    return {(H_OF[word], 0): value * H_SCALE for word, value in vector.items()}


def inner(one, other, moments):
    result = None
    for (x, n), value in one.items():
        part = None
        for (y, m), factor in other.items():
            term = factor * moments[tuple(sorted((x, y))) + (n + m,)]
            part = term if part is None else part + term
        part = value * part
        result = part if result is None else result + part
    return result


def first_two_steps(sums):
    moments = dict(zip(EARLY_MOMENTS + LATE_MOMENTS, sums))
    basis = [{("w", 0): lax.rsqrt(moments["w", "w", 0] + EPSILON * START_SCALE**2)}]
    thetas = []
    for _ in range(2):
        latest = basis[-1]
        image = times_h(latest)
        theta = inner(latest, image, moments)
        correction = times_inverse(plus(image, latest, -theta))
        ortho = correction
        for member in basis:
            ortho = plus(ortho, member, -inner(member, correction, moments))
        scale = lax.rsqrt(inner(ortho, ortho, moments) + EPSILON)
        basis.append({word: value * scale for word, value in ortho.items()})
        thetas.append(theta)
    return basis, thetas


def combined(vector, arrays, inverse):
    words = {name: (n, values) for (name, n), values in arrays.items()}
    result = None
    for n in range(max(n for _, n in vector), -1, -1):
        if result is not None:
            result = result * inverse
        for (name, m), value in vector.items():
            held, values = words[name]
            if m - held == n:
                term = one_of(value) * values
                result = term if result is None else result + term
    return result


def inverted(values):
    return jnp.where(values > 0.0, 1.0 / values, 0.0)


def copy_all(pairs, arrived):
    copies = [
        pltpu.make_async_copy(source, target, arrived.at[i])
        for i, (source, target) in enumerate(pairs)
    ]
    for copy in copies:
        copy.start()
    for copy in copies:
        copy.wait()


def picking_kernel(
    wave, preconditioner, left, right, own_wave, own_preconditioner, sent_left, sent_right, arrived
):
    op = lax.axis_index("op")
    pairs = [(wave.at[op], own_wave), (preconditioner.at[op], own_preconditioner)]
    for values, sent in ((left, sent_left), (right, sent_right)):
        for term in range(values.shape[0]):
            pairs.append((values.at[term, 1 - op], sent.at[term]))
    copy_all(pairs, arrived)


def splitting_kernel(
    wave, facing_wave, own_left, own_right, mate_left, mate_right, start_ref, high, low, left_high,
    left_low, right_high, right_low,
):
    op = lax.axis_index("op")
    for place, values in enumerate((wave[op], wave[1 - op], facing_wave[...])):
        start = values * START_SCALE
        start_ref[place] = start
        high[place], low[place] = split(start)
    count = own_left.shape[0]
    for term in range(count):
        left_high[term], left_low[term] = split(own_left[term, op] * (1.0 / H_SCALE))
        right_high[term], right_low[term] = split(own_right[term, op])
        place = count + term
        left_high[place], left_low[place] = split(mate_left[term] * (1.0 / H_SCALE))
        right_high[place], right_low[place] = split(mate_right[term])


def first_kernel(
    own_shifts, mate_shifts, high, low, left_high, left_low, right_high, right_low, image_ref
):
    sources = term_sources(own_shifts, mate_shifts)
    image_ref[...] = apply_terms(
        sources, (high, low), (left_high, left_low), (right_high, right_low)
    )


def side_kernel(
    own_shifts, mate_shifts, start, preconditioner, facing_preconditioner, image,
    left_high, left_low, right_high, right_low, side_ref, row_ref, inverse_ref, high, low,
):
    op = lax.axis_index("op")
    sources = term_sources(own_shifts, mate_shifts)
    divisors = (preconditioner[op], preconditioner[1 - op], facing_preconditioner[...])
    for place in range(3):
        inverse = inverted(divisors[place])
        inverse_ref[place] = inverse
        high[place], low[place] = split(start[place] * inverse)
    side = apply_terms(sources, (high, low), (left_high, left_low), (right_high, right_low))
    side_ref[...] = side
    arrays = {"w": start[0], "u": image[...], "a": side}
    row_ref[...] = row_of_sums(moment_factors(EARLY_MOMENTS, arrays, inverse_ref[0]))


def second_kernel(
    own_shifts, mate_shifts, start, own_image, mate_image, facing_image, inverse, side, early_row,
    left_high, left_low, right_high, right_low, image_ref, row_ref, ratio_ref, high, low,
):
    sources = term_sources(own_shifts, mate_shifts)
    for place, image in enumerate((own_image, mate_image, facing_image)):
        ratio = image[...] * inverse[place]
        ratio_ref[place] = ratio
        high[place], low[place] = split(ratio)
    image = apply_terms(sources, (high, low), (left_high, left_low), (right_high, right_low))
    image_ref[...] = image
    arrays = {"w": start[0], "u": own_image[...], "a": side[...], "b": image}
    factors = moment_factors(LATE_MOMENTS, arrays, inverse[0])
    row = row_of_sums(factors, len(EARLY_MOMENTS), early_row[...])
    row_ref[...] = jnp.broadcast_to(row, row_ref.shape)


MEMBER_PAIRS = [(i, j) for i in range(3) for j in range(i + 1)]


def third_kernel(
    total, own_shifts, mate_shifts, rows, start, inverse, ratio, own_side, mate_side,
    facing_side, own_second, mate_second, facing_second, left_high, left_low, right_high, right_low,
    kept_ref, sent_ref, row_ref, members_ref, theta_ref, high, low,
):
    op = lax.axis_index("op")
    sources = term_sources(own_shifts, mate_shifts)
    count = len(EARLY_MOMENTS + LATE_MOMENTS)
    basis, thetas = first_two_steps(summed(rows, total, count))
    for position, theta in enumerate(thetas):
        theta_ref[position] = theta
    half = kept_ref.shape[0]
    sides = (own_side, mate_side, facing_side)
    seconds = (own_second, mate_second, facing_second)

    def mine(values):
        return jnp.where(op == 0, values[:half], values[half:])

    for place in range(3):
        arrays = {
            ("w", 0): start[place],
            ("u", 1): ratio[place],
            ("a", 0): sides[place][...],
            ("b", 0): seconds[place][...],
        }
        latest = combined(basis[2], arrays, inverse[place])
        high[place], low[place] = split(latest)
        if place < 2:
            members = [combined(vector, arrays, inverse[place]) for vector in basis[:2]] + [latest]
            for position, member in enumerate(members):
                members_ref[position, place] = mine(member)
            if place == 0:
                own_members = members
    image = H_SCALE * apply_terms(
        sources, (high, low), (left_high, left_low), (right_high, right_low)
    )
    kept_ref[...] = mine(image)
    sent_ref[...] = jnp.where(op == 0, image[half:], image[:half])
    members = own_members
    ratio_image = image * inverse[0]
    ratio_latest = members[-1] * inverse[0]
    factors = [
        (members[-1], image),
        (ratio_image, ratio_image),
        (ratio_image, ratio_latest),
        (ratio_latest, ratio_latest),
    ]
    factors = factors + [(member, ratio_image) for member in members]
    factors = factors + [(member, ratio_latest) for member in members]
    factors = factors + [(members[i], members[j]) for i, j in MEMBER_PAIRS]
    row_ref[...] = jnp.broadcast_to(row_of_sums(factors), row_ref.shape)


def last_kernel(
    total, rows, thetas, members, inverse, own_image, mate_image, basis_ref, ritz_ref
):
    op = lax.axis_index("op")
    sums = summed(rows, total, 10 + len(MEMBER_PAIRS))
    theta = sums[0]
    correlations = [sums[4 + i] - theta * sums[7 + i] for i in range(3)]
    length = sums[1] - 2.0 * theta * sums[2] + theta * theta * sums[3]
    for correlation in correlations:
        length = length - 2.0 * correlation * correlation
    for (i, j), value in zip(MEMBER_PAIRS, sums[10:]):
        length = length + (1.0 if i == j else 2.0) * correlations[i] * correlations[j] * value
    scale = lax.rsqrt(length + EPSILON)
    half = own_image.shape[0]
    mine = pl.ds(pl.multiple_of(op * half, half), half)
    for place, (image, sector) in enumerate(((own_image, op), (mate_image, 1 - op))):
        basis_ref[0, sector] = members[1, place]
        basis_ref[1, sector] = members[2, place]
        ortho = (image[...] - one_of(theta) * members[2, place]) * inverse[place, mine]
        for i, correlation in enumerate(correlations):
            ortho = ortho - one_of(correlation) * members[i, place]
        basis_ref[2, sector] = ortho * one_of(scale)
    for position, value in enumerate((thetas[0], thetas[1], theta)):
        ritz_ref[position] = value[0, 0]


def one_sector_body(wave_start, left_blocks, right_blocks, term_shifts, preconditioner):
    op = lax.axis_index("op")
    chips = lax.axis_size("sector")
    devices = 2 * chips
    rows, columns = wave_start.shape[1:]
    half = rows // 2
    terms = 2 * left_blocks.shape[0]
    total = float(devices * rows * columns)
    swap = [(i, i ^ 1) for i in range(devices)]
    across = [(i, i + 1) for i in range(1, devices - 1, 2)]
    across = across + [(j, i) for i, j in across]

    def mate(values):
        return lax.ppermute(values, AXES, swap)

    def facing(values):
        return lax.ppermute(values, AXES, across)

    def own_sector(values):
        return lax.dynamic_index_in_dim(values, op, 0, keepdims=False)

    def exchanged(row):
        spread = row.reshape(devices, 1, LANES)
        return lax.all_to_all(spread, AXES, 0, 0, tiled=True).reshape(devices, LANES)

    vmem = pl.BlockSpec(memory_space=pltpu.VMEM)
    smem = pl.BlockSpec(memory_space=pltpu.SMEM)

    def call(kernel, operands, shapes, scalars=0, out_scalars=0, scratch=True):
        return pl.pallas_call(
            kernel,
            out_shape=[jax.ShapeDtypeStruct(shape, kind) for shape, kind in shapes],
            in_specs=[smem] * scalars + [vmem] * (len(operands) - scalars),
            out_specs=[vmem] * (len(shapes) - out_scalars) + [smem] * out_scalars,
            scratch_shapes=[pltpu.VMEM((3, rows, columns), jnp.bfloat16)] * (2 if scratch else 0),
            compiler_params=pltpu.CompilerParams(vmem_limit_bytes=16 * 2**20),
        )(*operands)

    block = (rows, columns)
    f32, bf16 = jnp.float32, jnp.bfloat16
    row_shape = ((devices, LANES), f32)

    half_shape = left_blocks.shape[:1] + left_blocks.shape[2:]
    own_wave, own_preconditioner, sent_left, sent_right = pl.pallas_call(
        picking_kernel,
        out_shape=[jax.ShapeDtypeStruct(shape, f32) for shape in [block] * 2 + [half_shape] * 2],
        in_specs=[pl.BlockSpec(memory_space=pl.ANY)] * 4,
        out_specs=[vmem] * 4,
        scratch_shapes=[pltpu.SemaphoreType.DMA((2 + terms,))],
        compiler_params=pltpu.CompilerParams(vmem_limit_bytes=52 * 2**20),
    )(wave_start, preconditioner, left_blocks, right_blocks)
    facing_wave = facing(own_wave)
    facing_preconditioner = facing(own_preconditioner)
    mate_left, mate_right = mate(sent_left), mate(sent_right)
    shifts = (term_shifts, mate(term_shifts))

    split_shape = (terms,) + left_blocks.shape[2:]
    start, start_high, start_low, *blocks = call(
        splitting_kernel,
        (wave_start, facing_wave, left_blocks, right_blocks, mate_left, mate_right),
        [((3,) + block, f32)] + [((3,) + block, bf16)] * 2 + [(split_shape, bf16)] * 4,
        scratch=False,
    )
    def around(values):
        return (values, mate(values), facing(values))

    (image,) = call(
        first_kernel,
        (*shifts, start_high, start_low, *blocks),
        [(block, f32)],
        scalars=2,
        scratch=False,
    )
    images = around(image)
    side, early_row, inverse = call(
        side_kernel,
        (*shifts, start, preconditioner, facing_preconditioner, image, *blocks),
        [(block, f32), ((1, LANES), f32), ((3,) + block, f32)],
        scalars=2,
    )
    sides = around(side)
    second, row, ratio = call(
        second_kernel,
        (*shifts, start, *images, inverse, side, early_row, *blocks),
        [(block, f32), row_shape, ((3,) + block, f32)],
        scalars=2,
    )
    seconds = around(second)
    row, *sides = lax.optimization_barrier((row, *sides))
    half_block = (half, columns)
    kept, sent, row, members, thetas = call(
        functools.partial(third_kernel, total),
        (*shifts, exchanged(row), start, inverse, ratio, *sides, *seconds, *blocks),
        [(half_block, f32)] * 2 + [row_shape, ((3, 2) + half_block, f32), ((2, 8, LANES), f32)],
        scalars=2,
    )
    basis, ritz = call(
        functools.partial(last_kernel, total),
        (exchanged(row), thetas, members, inverse, kept, mate(sent)),
        [((ITERS, 2) + half_block, f32), ((ITERS,), f32)],
        out_scalars=1,
        scratch=False,
    )
    return (basis, ritz)


def with_halo(cells, sides, width):
    for axis, dim in sides:
        count = lax.axis_size(axis)
        ends = count - 1
        head = lax.slice_in_dim(cells, 0, width, axis=dim)
        tail = lax.slice_in_dim(cells, cells.shape[dim] - width, cells.shape[dim], axis=dim)
        cells = jnp.concatenate(
            [
                lax.ppermute(tail, axis, [(i, (i + 1) % count) for i in range(ends)]),
                cells,
                lax.ppermute(head, axis, [((i + 1) % count, i) for i in range(ends)]),
            ],
            axis=dim,
        )
    return cells


def split_terms_body(wave_start, left_blocks, right_blocks, term_shifts, preconditioner):
    highest = lax.Precision.HIGHEST
    width = wave_start.shape[1]
    row_count = width // lax.axis_size("op")
    first_row = lax.axis_index("op") * row_count
    total = float(wave_start.shape[0] * lax.axis_size("sector") * width * wave_start.shape[2])

    def portion(values):
        return lax.dynamic_slice_in_dim(values, first_row, row_count, axis=values.ndim - 2)

    start_sum = total_sum(jnp.sum(jnp.square(portion(wave_start)))[None])[0] / total
    basis = [wave_start * lax.rsqrt(start_sum + EPSILON)]
    ritz = []
    for _ in range(ITERS):
        latest = basis[-1]
        padded = with_halo(latest, (("sector", 0),), 1)
        shift = term_shifts[:, None, None, None]
        source = jnp.where(
            shift == 1,
            padded[None, :-2],
            jnp.where(shift == -1, padded[None, 2:], padded[None, 1:-1]),
        )
        inner = jnp.einsum("ksab,ksbc->ksac", left_blocks, source, precision=highest)
        image = lax.psum(jnp.einsum("ksac,kscd->sad", inner, right_blocks, precision=highest), "op")
        inverse = 1.0 / preconditioner
        pieces = products([portion(member) for member in basis], portion(image), portion(inverse))
        theta, correlations, scale = coefficients(
            total_sum(jnp.stack(pieces)), total, len(basis)
        )
        ortho = (image - theta * latest) * inverse
        for position, member in enumerate(basis):
            ortho = ortho - correlations[position] * member
        basis.append(ortho * scale)
        ritz.append(theta)
    output = jnp.stack([portion(member) for member in basis[1:]])
    return (output, jnp.stack(ritz))


def solution(mesh):
    placed = (
        P("sector", None, None),
        P("op", "sector", None, None),
        P("op", "sector", None, None),
        P("op"),
        P("sector", None, None),
    )

    def body(wave_start, *operands):
        one_each = mesh.shape["op"] == 2 and wave_start.shape[0] == 2
        return (one_sector_body if one_each else split_terms_body)(wave_start, *operands)

    return jax.shard_map(
        body,
        mesh=mesh,
        in_specs=placed,
        out_specs=(P(None, "sector", "op", None), P()),
        check_vma=False,
    )
```

```python
import functools

import jax
import jax.numpy as jnp
from jax import lax
from jax.experimental import pallas as pl
from jax.experimental.pallas import tpu as pltpu
from jax.sharding import PartitionSpec as P

ITERS = 3


EPSILON = 1e-06

AXES = ("sector", "op")

LANES = 128


def total_sum(values):
    devices = lax.axis_size("sector") * lax.axis_size("op")
    row = jnp.pad(values, (0, LANES - values.shape[0]))
    rows = lax.all_to_all(jnp.broadcast_to(row, (devices, LANES)), AXES, 0, 0, tiled=True)
    return jnp.sum(rows, axis=0)[: values.shape[0]]


def coefficients(sums, total, count):
    sums = sums / total
    theta = sums[0]
    correlations = sums[4 : 4 + count] - theta * sums[4 + count : 4 + 2 * count]
    length = (
        sums[1]
        - 2.0 * theta * sums[2]
        + theta * theta * sums[3]
        - jnp.sum(jnp.square(correlations))
    )
    return theta, correlations, lax.rsqrt(length + EPSILON)


def products(members, image, inverse):
    latest = members[-1]
    ratio_image = image * inverse
    ratio_latest = latest * inverse
    pieces = [
        jnp.sum(latest * image),
        jnp.sum(ratio_image * ratio_image),
        jnp.sum(ratio_image * ratio_latest),
        jnp.sum(ratio_latest * ratio_latest),
    ]
    pieces = pieces + [jnp.sum(member * ratio_image) for member in members]
    pieces = pieces + [jnp.sum(member * ratio_latest) for member in members]
    return pieces


def split(values):
    high = values.astype(jnp.bfloat16)
    return high, (values - high.astype(jnp.float32)).astype(jnp.bfloat16)


def dot_split(lhs_high, lhs_low, rhs_high, rhs_low):
    dot = functools.partial(jnp.dot, preferred_element_type=jnp.float32)
    rows = lhs_high.shape[0]
    both = dot(jnp.concatenate([lhs_high, lhs_low], axis=0), rhs_high)
    return both[:rows] + (both[rows:] + dot(lhs_high, rhs_low))


def apply_terms(sources, vectors, left, right):
    left_high, left_low = left
    right_high, right_low = right
    vector_high, vector_low = vectors
    inners = [
        split(
            dot_split(left_high[term], left_low[term], vector_high[source], vector_low[source])
        )
        for term, source in enumerate(sources)
    ]
    image = None
    for term, inner in enumerate(inners):
        part = dot_split(*inner, right_high[term], right_low[term])
        image = part if image is None else image + part
    return image


def term_sources(own_shifts, mate_shifts):
    toward_mate = jnp.where(lax.axis_index("op") == 0, -1, 1)
    shifts = [refs[i] for refs in (own_shifts, mate_shifts) for i in range(refs.shape[0])]
    return [
        jnp.where(shift == 0, 0, jnp.where(shift == toward_mate, 1, 2)) for shift in shifts
    ]


def row_of_sums(factors, first=0, row=None):
    lane = lax.broadcasted_iota(jnp.int32, (1, LANES), 1)
    if row is None:
        row = jnp.zeros((1, LANES), jnp.float32)
    for position, (one, other) in enumerate(factors):
        product = (one * other).reshape(-1, 8, one.shape[1])
        whole = jnp.sum(jnp.sum(product, axis=0), axis=(0, 1), keepdims=True)
        row = jnp.where(lane == first + position, whole, row)
    return row


def summed(rows, total, count):
    whole = jnp.sum(rows[...], axis=0, keepdims=True) * (1.0 / total)
    return [jnp.broadcast_to(whole[:, i : i + 1], (8, LANES)) for i in range(count)]


def one_of(value):
    return value[:1, :1]


EARLY_MOMENTS = (
    [("w", "w", n) for n in range(5)]
    + [("u", "w", n) for n in range(5)]
    + [("u", "u", n) for n in range(1, 5)]
    + [("a", "w", n) for n in range(4)]
    + [("a", "u", n) for n in range(1, 4)]
    + [("a", "a", 2)]
)
LATE_MOMENTS = (
    [("b", "w", n) for n in range(4)]
    + [("b", "u", n) for n in range(1, 4)]
    + [("a", "b", 2), ("b", "b", 2)]
)

H_OF = {("w", 0): "u", ("w", 1): "a", ("u", 1): "b"}

START_SCALE = 2.0**10
H_SCALE = 2.0**7


def moment_factors(moments, arrays, inverse):
    powers = {(name, 0): values for name, values in arrays.items()}

    def power(name, n):
        if (name, n) not in powers:
            powers[name, n] = power(name, n - 1) * inverse
        return powers[name, n]

    return [(power(x, n // 2), power(y, n - n // 2)) for x, y, n in moments]


def plus(vector, other, factor):
    result = dict(vector)
    for word, value in other.items():
        term = value * factor
        result[word] = result[word] + term if word in result else term
    return result


def times_inverse(vector):
    return {(name, n + 1): value for (name, n), value in vector.items()}


def times_h(vector):
    return {(H_OF[word], 0): value * H_SCALE for word, value in vector.items()}


def inner(one, other, moments):
    result = None
    for (x, n), value in one.items():
        part = None
        for (y, m), factor in other.items():
            term = factor * moments[tuple(sorted((x, y))) + (n + m,)]
            part = term if part is None else part + term
        part = value * part
        result = part if result is None else result + part
    return result


def first_two_steps(sums):
    moments = dict(zip(EARLY_MOMENTS + LATE_MOMENTS, sums))
    basis = [{("w", 0): lax.rsqrt(moments["w", "w", 0] + EPSILON * START_SCALE**2)}]
    thetas = []
    for _ in range(2):
        latest = basis[-1]
        image = times_h(latest)
        theta = inner(latest, image, moments)
        correction = times_inverse(plus(image, latest, -theta))
        ortho = correction
        for member in basis:
            ortho = plus(ortho, member, -inner(member, correction, moments))
        scale = lax.rsqrt(inner(ortho, ortho, moments) + EPSILON)
        basis.append({word: value * scale for word, value in ortho.items()})
        thetas.append(theta)
    return basis, thetas


def combined(vector, arrays, inverse):
    words = {name: (n, values) for (name, n), values in arrays.items()}
    result = None
    for n in range(max(n for _, n in vector), -1, -1):
        if result is not None:
            result = result * inverse
        for (name, m), value in vector.items():
            held, values = words[name]
            if m - held == n:
                term = one_of(value) * values
                result = term if result is None else result + term
    return result


def inverted(values):
    return jnp.where(values > 0.0, 1.0 / values, 0.0)


def copy_all(pairs, arrived):
    copies = [
        pltpu.make_async_copy(source, target, arrived.at[i])
        for i, (source, target) in enumerate(pairs)
    ]
    for copy in copies:
        copy.start()
    for copy in copies:
        copy.wait()


def picking_kernel(
    wave, preconditioner, left, right, own_wave, own_preconditioner, sent_left, sent_right, arrived
):
    op = lax.axis_index("op")
    pairs = [(wave.at[op], own_wave), (preconditioner.at[op], own_preconditioner)]
    for values, sent in ((left, sent_left), (right, sent_right)):
        for term in range(values.shape[0]):
            pairs.append((values.at[term, 1 - op], sent.at[term]))
    copy_all(pairs, arrived)


def splitting_kernel(
    own_left, own_right, mate_left, mate_right, left_high, left_low, right_high, right_low
):
    op = lax.axis_index("op")
    count = own_left.shape[0]
    for term in range(count):
        left_high[term], left_low[term] = split(own_left[term, op] * (1.0 / H_SCALE))
        right_high[term], right_low[term] = split(own_right[term, op])
        place = count + term
        left_high[place], left_low[place] = split(mate_left[term] * (1.0 / H_SCALE))
        right_high[place], right_low[place] = split(mate_right[term])


def first_kernel(
    own_shifts, mate_shifts, wave, facing_wave, left_high, left_low, right_high, right_low,
    image_ref, start_ref, high, low,
):
    op = lax.axis_index("op")
    sources = term_sources(own_shifts, mate_shifts)
    for place, values in enumerate((wave[op], wave[1 - op], facing_wave[...])):
        start = values * START_SCALE
        start_ref[place] = start
        high[place], low[place] = split(start)
    image_ref[...] = apply_terms(
        sources, (high, low), (left_high, left_low), (right_high, right_low)
    )


def side_kernel(
    own_shifts, mate_shifts, start, preconditioner, facing_preconditioner,
    left_high, left_low, right_high, right_low, side_ref, inverse_ref, high, low,
):
    op = lax.axis_index("op")
    sources = term_sources(own_shifts, mate_shifts)
    divisors = (preconditioner[op], preconditioner[1 - op], facing_preconditioner[...])
    for place in range(3):
        inverse = inverted(divisors[place])
        inverse_ref[place] = inverse
        high[place], low[place] = split(start[place] * inverse)
    side_ref[...] = apply_terms(
        sources, (high, low), (left_high, left_low), (right_high, right_low)
    )


def moments_kernel(start, image, side, inverse, row_ref):
    arrays = {"w": start[0], "u": image[...], "a": side[...]}
    row_ref[...] = row_of_sums(moment_factors(EARLY_MOMENTS, arrays, inverse[0]))


def second_kernel(
    own_shifts, mate_shifts, start, own_image, mate_image, facing_image, inverse, side, early_row,
    left_high, left_low, right_high, right_low, image_ref, row_ref, ratio_ref, high, low,
):
    sources = term_sources(own_shifts, mate_shifts)
    for place, image in enumerate((own_image, mate_image, facing_image)):
        ratio = image[...] * inverse[place]
        ratio_ref[place] = ratio
        high[place], low[place] = split(ratio)
    image = apply_terms(sources, (high, low), (left_high, left_low), (right_high, right_low))
    image_ref[...] = image
    arrays = {"w": start[0], "u": own_image[...], "a": side[...], "b": image}
    factors = moment_factors(LATE_MOMENTS, arrays, inverse[0])
    row = row_of_sums(factors, len(EARLY_MOMENTS), early_row[...])
    row_ref[...] = jnp.broadcast_to(row, row_ref.shape)


MEMBER_PAIRS = [(i, j) for i in range(3) for j in range(i + 1)]


def third_kernel(
    total, own_shifts, mate_shifts, rows, start, inverse, ratio, own_side, mate_side,
    facing_side, own_second, mate_second, facing_second, left_high, left_low, right_high, right_low,
    kept_ref, sent_ref, row_ref, members_ref, theta_ref, high, low,
):
    op = lax.axis_index("op")
    sources = term_sources(own_shifts, mate_shifts)
    count = len(EARLY_MOMENTS + LATE_MOMENTS)
    basis, thetas = first_two_steps(summed(rows, total, count))
    for position, theta in enumerate(thetas):
        theta_ref[position] = theta
    half = kept_ref.shape[0]
    sides = (own_side, mate_side, facing_side)
    seconds = (own_second, mate_second, facing_second)

    def mine(values):
        return jnp.where(op == 0, values[:half], values[half:])

    for place in range(3):
        arrays = {
            ("w", 0): start[place],
            ("u", 1): ratio[place],
            ("a", 0): sides[place][...],
            ("b", 0): seconds[place][...],
        }
        latest = combined(basis[2], arrays, inverse[place])
        high[place], low[place] = split(latest)
        if place < 2:
            members = [combined(vector, arrays, inverse[place]) for vector in basis[:2]] + [latest]
            for position, member in enumerate(members):
                members_ref[position, place] = mine(member)
            if place == 0:
                own_members = members
    image = H_SCALE * apply_terms(
        sources, (high, low), (left_high, left_low), (right_high, right_low)
    )
    kept_ref[...] = mine(image)
    sent_ref[...] = jnp.where(op == 0, image[half:], image[:half])
    members = own_members
    ratio_image = image * inverse[0]
    ratio_latest = members[-1] * inverse[0]
    factors = [
        (members[-1], image),
        (ratio_image, ratio_image),
        (ratio_image, ratio_latest),
        (ratio_latest, ratio_latest),
    ]
    factors = factors + [(member, ratio_image) for member in members]
    factors = factors + [(member, ratio_latest) for member in members]
    factors = factors + [(members[i], members[j]) for i, j in MEMBER_PAIRS]
    row_ref[...] = jnp.broadcast_to(row_of_sums(factors), row_ref.shape)


def last_kernel(
    total, rows, thetas, members, inverse, own_image, mate_image, basis_ref, ritz_ref
):
    op = lax.axis_index("op")
    sums = summed(rows, total, 10 + len(MEMBER_PAIRS))
    theta = sums[0]
    correlations = [sums[4 + i] - theta * sums[7 + i] for i in range(3)]
    length = sums[1] - 2.0 * theta * sums[2] + theta * theta * sums[3]
    for correlation in correlations:
        length = length - 2.0 * correlation * correlation
    for (i, j), value in zip(MEMBER_PAIRS, sums[10:]):
        length = length + (1.0 if i == j else 2.0) * correlations[i] * correlations[j] * value
    scale = lax.rsqrt(length + EPSILON)
    half = own_image.shape[0]
    mine = pl.ds(pl.multiple_of(op * half, half), half)
    for place, (image, sector) in enumerate(((own_image, op), (mate_image, 1 - op))):
        basis_ref[0, sector] = members[1, place]
        basis_ref[1, sector] = members[2, place]
        ortho = (image[...] - one_of(theta) * members[2, place]) * inverse[place, mine]
        for i, correlation in enumerate(correlations):
            ortho = ortho - one_of(correlation) * members[i, place]
        basis_ref[2, sector] = ortho * one_of(scale)
    for position, value in enumerate((thetas[0], thetas[1], theta)):
        ritz_ref[position] = value[0, 0]


def one_sector_body(wave_start, left_blocks, right_blocks, term_shifts, preconditioner):
    op = lax.axis_index("op")
    chips = lax.axis_size("sector")
    devices = 2 * chips
    rows, columns = wave_start.shape[1:]
    half = rows // 2
    terms = 2 * left_blocks.shape[0]
    total = float(devices * rows * columns)
    swap = [(i, i ^ 1) for i in range(devices)]
    across = [(i, i + 1) for i in range(1, devices - 1, 2)]
    across = across + [(j, i) for i, j in across]

    def mate(values):
        return lax.ppermute(values, AXES, swap)

    def facing(values):
        return lax.ppermute(values, AXES, across)

    def own_sector(values):
        return lax.dynamic_index_in_dim(values, op, 0, keepdims=False)

    def exchanged(row):
        spread = row.reshape(devices, 1, LANES)
        return lax.all_to_all(spread, AXES, 0, 0, tiled=True).reshape(devices, LANES)

    vmem = pl.BlockSpec(memory_space=pltpu.VMEM)
    smem = pl.BlockSpec(memory_space=pltpu.SMEM)

    def call(kernel, operands, shapes, scalars=0, out_scalars=0, scratch=True):
        return pl.pallas_call(
            kernel,
            out_shape=[jax.ShapeDtypeStruct(shape, kind) for shape, kind in shapes],
            in_specs=[smem] * scalars + [vmem] * (len(operands) - scalars),
            out_specs=[vmem] * (len(shapes) - out_scalars) + [smem] * out_scalars,
            scratch_shapes=[pltpu.VMEM((3, rows, columns), jnp.bfloat16)] * (2 if scratch else 0),
            compiler_params=pltpu.CompilerParams(vmem_limit_bytes=16 * 2**20),
        )(*operands)

    block = (rows, columns)
    f32, bf16 = jnp.float32, jnp.bfloat16
    row_shape = ((devices, LANES), f32)

    half_shape = left_blocks.shape[:1] + left_blocks.shape[2:]
    own_wave, own_preconditioner, sent_left, sent_right = pl.pallas_call(
        picking_kernel,
        out_shape=[jax.ShapeDtypeStruct(shape, f32) for shape in [block] * 2 + [half_shape] * 2],
        in_specs=[pl.BlockSpec(memory_space=pl.ANY)] * 4,
        out_specs=[vmem] * 4,
        scratch_shapes=[pltpu.SemaphoreType.DMA((2 + terms,))],
        compiler_params=pltpu.CompilerParams(vmem_limit_bytes=52 * 2**20),
    )(wave_start, preconditioner, left_blocks, right_blocks)
    facing_wave = facing(own_wave)
    facing_preconditioner = facing(own_preconditioner)
    mate_left, mate_right = mate(sent_left), mate(sent_right)
    shifts = (term_shifts, mate(term_shifts))

    split_shape = (terms,) + left_blocks.shape[2:]
    blocks = call(
        splitting_kernel,
        (left_blocks, right_blocks, mate_left, mate_right),
        [(split_shape, bf16)] * 4,
        scratch=False,
    )

    def around(values):
        return (values, mate(values), facing(values))

    image, start = call(
        first_kernel,
        (*shifts, wave_start, facing_wave, *blocks),
        [(block, f32), ((3,) + block, f32)],
        scalars=2,
    )
    images = around(image)
    side, inverse = call(
        side_kernel,
        (*shifts, start, preconditioner, facing_preconditioner, *blocks),
        [(block, f32), ((3,) + block, f32)],
        scalars=2,
    )
    sides = around(side)
    (early_row,) = call(
        moments_kernel, (start, image, side, inverse), [((1, LANES), f32)], scratch=False
    )
    second, row, ratio = call(
        second_kernel,
        (*shifts, start, *images, inverse, side, early_row, *blocks),
        [(block, f32), row_shape, ((3,) + block, f32)],
        scalars=2,
    )
    seconds = around(second)
    row, *sides = lax.optimization_barrier((row, *sides))
    half_block = (half, columns)
    kept, sent, row, members, thetas = call(
        functools.partial(third_kernel, total),
        (*shifts, exchanged(row), start, inverse, ratio, *sides, *seconds, *blocks),
        [(half_block, f32)] * 2 + [row_shape, ((3, 2) + half_block, f32), ((2, 8, LANES), f32)],
        scalars=2,
    )
    basis, ritz = call(
        functools.partial(last_kernel, total),
        (exchanged(row), thetas, members, inverse, kept, mate(sent)),
        [((ITERS, 2) + half_block, f32), ((ITERS,), f32)],
        out_scalars=1,
        scratch=False,
    )
    return (basis, ritz)


def with_halo(cells, sides, width):
    for axis, dim in sides:
        count = lax.axis_size(axis)
        ends = count - 1
        head = lax.slice_in_dim(cells, 0, width, axis=dim)
        tail = lax.slice_in_dim(cells, cells.shape[dim] - width, cells.shape[dim], axis=dim)
        cells = jnp.concatenate(
            [
                lax.ppermute(tail, axis, [(i, (i + 1) % count) for i in range(ends)]),
                cells,
                lax.ppermute(head, axis, [((i + 1) % count, i) for i in range(ends)]),
            ],
            axis=dim,
        )
    return cells


def split_terms_body(wave_start, left_blocks, right_blocks, term_shifts, preconditioner):
    highest = lax.Precision.HIGHEST
    width = wave_start.shape[1]
    row_count = width // lax.axis_size("op")
    first_row = lax.axis_index("op") * row_count
    total = float(wave_start.shape[0] * lax.axis_size("sector") * width * wave_start.shape[2])

    def portion(values):
        return lax.dynamic_slice_in_dim(values, first_row, row_count, axis=values.ndim - 2)

    start_sum = total_sum(jnp.sum(jnp.square(portion(wave_start)))[None])[0] / total
    basis = [wave_start * lax.rsqrt(start_sum + EPSILON)]
    ritz = []
    for _ in range(ITERS):
        latest = basis[-1]
        padded = with_halo(latest, (("sector", 0),), 1)
        shift = term_shifts[:, None, None, None]
        source = jnp.where(
            shift == 1,
            padded[None, :-2],
            jnp.where(shift == -1, padded[None, 2:], padded[None, 1:-1]),
        )
        inner = jnp.einsum("ksab,ksbc->ksac", left_blocks, source, precision=highest)
        image = lax.psum(jnp.einsum("ksac,kscd->sad", inner, right_blocks, precision=highest), "op")
        inverse = 1.0 / preconditioner
        pieces = products([portion(member) for member in basis], portion(image), portion(inverse))
        theta, correlations, scale = coefficients(
            total_sum(jnp.stack(pieces)), total, len(basis)
        )
        ortho = (image - theta * latest) * inverse
        for position, member in enumerate(basis):
            ortho = ortho - correlations[position] * member
        basis.append(ortho * scale)
        ritz.append(theta)
    output = jnp.stack([portion(member) for member in basis[1:]])
    return (output, jnp.stack(ritz))


def solution(mesh):
    placed = (
        P("sector", None, None),
        P("op", "sector", None, None),
        P("op", "sector", None, None),
        P("op"),
        P("sector", None, None),
    )

    def body(wave_start, *operands):
        one_each = mesh.shape["op"] == 2 and wave_start.shape[0] == 2
        return (one_sector_body if one_each else split_terms_body)(wave_start, *operands)

    return jax.shard_map(
        body,
        mesh=mesh,
        in_specs=placed,
        out_specs=(P(None, "sector", "op", None), P()),
        check_vma=False,
    )
```

```python
import functools

import jax
import jax.numpy as jnp
from jax import lax
from jax.experimental import pallas as pl
from jax.experimental.pallas import tpu as pltpu
from jax.sharding import PartitionSpec as P

ITERS = 3


EPSILON = 1e-06

AXES = ("sector", "op")

LANES = 128


def total_sum(values):
    devices = lax.axis_size("sector") * lax.axis_size("op")
    row = jnp.pad(values, (0, LANES - values.shape[0]))
    rows = lax.all_to_all(jnp.broadcast_to(row, (devices, LANES)), AXES, 0, 0, tiled=True)
    return jnp.sum(rows, axis=0)[: values.shape[0]]


def coefficients(sums, total, count):
    sums = sums / total
    theta = sums[0]
    correlations = sums[4 : 4 + count] - theta * sums[4 + count : 4 + 2 * count]
    length = (
        sums[1]
        - 2.0 * theta * sums[2]
        + theta * theta * sums[3]
        - jnp.sum(jnp.square(correlations))
    )
    return theta, correlations, lax.rsqrt(length + EPSILON)


def products(members, image, inverse):
    latest = members[-1]
    ratio_image = image * inverse
    ratio_latest = latest * inverse
    pieces = [
        jnp.sum(latest * image),
        jnp.sum(ratio_image * ratio_image),
        jnp.sum(ratio_image * ratio_latest),
        jnp.sum(ratio_latest * ratio_latest),
    ]
    pieces = pieces + [jnp.sum(member * ratio_image) for member in members]
    pieces = pieces + [jnp.sum(member * ratio_latest) for member in members]
    return pieces


def split(values):
    high = values.astype(jnp.bfloat16)
    return high, (values - high.astype(jnp.float32)).astype(jnp.bfloat16)


def dot_split(lhs_high, lhs_low, rhs_high, rhs_low):
    dot = functools.partial(jnp.dot, preferred_element_type=jnp.float32)
    rows = lhs_high.shape[0]
    both = dot(jnp.concatenate([lhs_high, lhs_low], axis=0), rhs_high)
    return both[:rows] + (both[rows:] + dot(lhs_high, rhs_low))


def apply_terms(sources, vectors, left, right):
    left_high, left_low = left
    right_high, right_low = right
    vector_high, vector_low = vectors
    inners = [
        split(
            dot_split(left_high[term], left_low[term], vector_high[source], vector_low[source])
        )
        for term, source in enumerate(sources)
    ]
    image = None
    for term, inner in enumerate(inners):
        part = dot_split(*inner, right_high[term], right_low[term])
        image = part if image is None else image + part
    return image


def term_sources(own_shifts, mate_shifts):
    toward_mate = jnp.where(lax.axis_index("op") == 0, -1, 1)
    shifts = [refs[i] for refs in (own_shifts, mate_shifts) for i in range(refs.shape[0])]
    return [
        jnp.where(shift == 0, 0, jnp.where(shift == toward_mate, 1, 2)) for shift in shifts
    ]


def row_of_sums(factors, first=0, row=None):
    lane = lax.broadcasted_iota(jnp.int32, (1, LANES), 1)
    if row is None:
        row = jnp.zeros((1, LANES), jnp.float32)
    for position, (one, other) in enumerate(factors):
        product = (one * other).reshape(-1, 8, one.shape[1])
        whole = jnp.sum(jnp.sum(product, axis=0), axis=(0, 1), keepdims=True)
        row = jnp.where(lane == first + position, whole, row)
    return row


def summed(rows, total, count):
    whole = jnp.sum(rows[...], axis=0, keepdims=True) * (1.0 / total)
    return [jnp.broadcast_to(whole[:, i : i + 1], (8, LANES)) for i in range(count)]


def one_of(value):
    return value[:1, :1]


H_OF = {
    ("w", 0): "u",
    ("w", 1): "a",
    ("u", 1): "b",
    ("w", 2): "c",
    ("u", 2): "d",
    ("a", 1): "e",
    ("b", 1): "f",
}

START_SCALE = 2.0**10
H_SCALE = 2.0**7


def moment_factors(moments, arrays, inverse):
    powers = {(name, 0): values for name, values in arrays.items()}

    def power(name, n):
        if (name, n) not in powers:
            powers[name, n] = power(name, n - 1) * inverse
        return powers[name, n]

    return [(power(x, n // 2), power(y, n - n // 2)) for x, y, n in moments]


def plus(vector, other, factor):
    result = dict(vector)
    for word, value in other.items():
        term = value * factor
        result[word] = result[word] + term if word in result else term
    return result


def times_inverse(vector):
    return {(name, n + 1): value for (name, n), value in vector.items()}


def times_h(vector):
    return {(H_OF[word], 0): value * H_SCALE for word, value in vector.items()}


def inner(one, other, moment):
    result = None
    for (x, n), value in one.items():
        part = None
        for (y, m), factor in other.items():
            term = factor * moment(*sorted((x, y)), n + m)
            part = term if part is None else part + term
        part = value * part
        result = part if result is None else result + part
    return result


def all_steps(moment, inverse_root):
    basis = [{("w", 0): inverse_root(moment("w", "w", 0) + EPSILON * START_SCALE**2)}]
    thetas = []
    for _ in range(ITERS):
        latest = basis[-1]
        image = times_h(latest)
        theta = inner(latest, image, moment)
        correction = times_inverse(plus(image, latest, -theta))
        ortho = correction
        for member in basis:
            ortho = plus(ortho, member, -inner(member, correction, moment))
        scale = inverse_root(inner(ortho, ortho, moment) + EPSILON)
        basis.append({word: value * scale for word, value in ortho.items()})
        thetas.append(theta)
    return basis, thetas


def needed_moments():
    asked = {}

    def moment(x, y, n):
        asked[x, y, n] = True
        return 1.0

    all_steps(moment, lambda value: 1.0)
    stages = ("wua", "bcd", "e", "f")
    groups = [[] for _ in stages]
    for key in asked:
        groups[max(i for i, names in enumerate(stages) if set(key[:2]) & set(names))].append(key)
    return groups


def combined(vector, arrays, inverse):
    words = {name: (n, values) for (name, n), values in arrays.items()}
    result = None
    for n in range(max(n for _, n in vector), -1, -1):
        if result is not None:
            result = result * inverse
        for (name, m), value in vector.items():
            held, values = words[name]
            if m - held == n:
                term = one_of(value) * values
                result = term if result is None else result + term
    return result


MOMENTS = needed_moments()
FIRST_LANE = [sum(len(group) for group in MOMENTS[:i]) for i in range(len(MOMENTS) + 1)]


def inverted(values):
    return jnp.where(values > 0.0, 1.0 / values, 0.0)


def copy_all(pairs, arrived):
    copies = [
        pltpu.make_async_copy(source, target, arrived.at[i])
        for i, (source, target) in enumerate(pairs)
    ]
    for copy in copies:
        copy.start()
    for copy in copies:
        copy.wait()


def picking_kernel(
    wave, preconditioner, left, right, own_wave, own_preconditioner, sent_left, sent_right, arrived
):
    op = lax.axis_index("op")
    pairs = [(wave.at[op], own_wave), (preconditioner.at[op], own_preconditioner)]
    for values, sent in ((left, sent_left), (right, sent_right)):
        for term in range(values.shape[0]):
            pairs.append((values.at[term, 1 - op], sent.at[term]))
    copy_all(pairs, arrived)


def splitting_kernel(
    own_left, own_right, mate_left, mate_right, left_high, left_low, right_high, right_low
):
    op = lax.axis_index("op")
    count = own_left.shape[0]
    for term in range(count):
        left_high[term], left_low[term] = split(own_left[term, op] * (1.0 / H_SCALE))
        right_high[term], right_low[term] = split(own_right[term, op])
        place = count + term
        left_high[place], left_low[place] = split(mate_left[term] * (1.0 / H_SCALE))
        right_high[place], right_low[place] = split(mate_right[term])


def first_kernel(
    own_shifts, mate_shifts, wave, facing_wave, left_high, left_low, right_high, right_low,
    image_ref, start_ref, high, low,
):
    op = lax.axis_index("op")
    sources = term_sources(own_shifts, mate_shifts)
    for place, values in enumerate((wave[op], wave[1 - op], facing_wave[...])):
        start = values * START_SCALE
        start_ref[place] = start
        high[place], low[place] = split(start)
    image_ref[...] = apply_terms(
        sources, (high, low), (left_high, left_low), (right_high, right_low)
    )


def side_kernel(
    own_shifts, mate_shifts, start, preconditioner, facing_preconditioner,
    left_high, left_low, right_high, right_low, side_ref, inverse_ref, high, low,
):
    op = lax.axis_index("op")
    sources = term_sources(own_shifts, mate_shifts)
    divisors = (preconditioner[op], preconditioner[1 - op], facing_preconditioner[...])
    for place in range(3):
        inverse = inverted(divisors[place])
        inverse_ref[place] = inverse
        high[place], low[place] = split(start[place] * inverse)
    side_ref[...] = apply_terms(
        sources, (high, low), (left_high, left_low), (right_high, right_low)
    )


def moments_kernel(start, image, side, inverse, row_ref):
    arrays = {"w": start[0], "u": image[...], "a": side[...]}
    row_ref[...] = row_of_sums(moment_factors(MOMENTS[0], arrays, inverse[0]))


def second_kernel(
    own_shifts, mate_shifts, own_image, mate_image, facing_image, inverse, _,
    left_high, left_low, right_high, right_low, image_ref, ratio_ref, high, low,
):
    sources = term_sources(own_shifts, mate_shifts)
    for place, image in enumerate((own_image, mate_image, facing_image)):
        ratio = image[...] * inverse[place]
        ratio_ref[place] = ratio
        high[place], low[place] = split(ratio)
    image_ref[...] = apply_terms(
        sources, (high, low), (left_high, left_low), (right_high, right_low)
    )


def halves(image, kept_ref, sent_ref):
    op = lax.axis_index("op")
    half = kept_ref.shape[0]
    kept_ref[...] = jnp.where(op == 0, image[:half], image[half:])
    sent_ref[...] = jnp.where(op == 0, image[half:], image[:half])


def extra_kernel(
    own_shifts, mate_shifts, start, ratio, inverse, image, side, second, early_row,
    left_high, left_low, right_high, right_low, extra_ref, kept_ref, sent_ref, row_ref, high, low,
):
    sources = term_sources(own_shifts, mate_shifts)
    arrays = {"w": start[0], "u": image[...], "a": side[...], "b": second[...]}
    for i, name in enumerate("cd"):
        for place in range(3):
            once = start[place] * inverse[place] if name == "c" else ratio[place]
            high[place], low[place] = split(once * inverse[place])
        extra = apply_terms(sources, (high, low), (left_high, left_low), (right_high, right_low))
        arrays[name] = extra
        extra_ref[i] = extra
        halves(extra, kept_ref.at[i], sent_ref.at[i])
    factors = moment_factors(MOMENTS[1], arrays, inverse[0])
    row_ref[...] = row_of_sums(factors, FIRST_LANE[1], early_row[...])


def further_kernel(
    own_shifts, mate_shifts, start, inverse, image, own_side, mate_side, facing_side, second,
    extra, early_row, left_high, left_low, right_high, right_low, further_ref, kept_ref, sent_ref,
    row_ref, high, low,
):
    sources = term_sources(own_shifts, mate_shifts)
    for place, side in enumerate((own_side, mate_side, facing_side)):
        high[place], low[place] = split(side[...] * inverse[place])
    further = apply_terms(sources, (high, low), (left_high, left_low), (right_high, right_low))
    further_ref[...] = further
    halves(further, kept_ref, sent_ref)
    arrays = {"w": start[0], "u": image[...], "a": own_side[...], "b": second[...]}
    arrays.update(c=extra[0], d=extra[1], e=further)
    factors = moment_factors(MOMENTS[2], arrays, inverse[0])
    row_ref[...] = row_of_sums(factors, FIRST_LANE[2], early_row[...])


def third_kernel(
    own_shifts, mate_shifts, start, inverse, image, side, own_second, mate_second, facing_second,
    extra, further, early_row, left_high, left_low, right_high, right_low,
    kept_ref, sent_ref, row_ref, high, low,
):
    sources = term_sources(own_shifts, mate_shifts)
    for place, second in enumerate((own_second, mate_second, facing_second)):
        high[place], low[place] = split(second[...] * inverse[place])
    last = apply_terms(sources, (high, low), (left_high, left_low), (right_high, right_low))
    halves(last, kept_ref, sent_ref)
    arrays = {"w": start[0], "u": image[...], "a": side[...], "b": own_second[...]}
    arrays.update(c=extra[0], d=extra[1], e=further[...], f=last)
    factors = moment_factors(MOMENTS[3], arrays, inverse[0])
    row = row_of_sums(factors, FIRST_LANE[3], early_row[...])
    row_ref[...] = jnp.broadcast_to(row, row_ref.shape)


def last_kernel(
    total, rows, start, ratio, inverse, own_side, mate_side, own_second, mate_second, own_extra,
    mate_extra, own_further, mate_further, own_last, mate_last, basis_ref, ritz_ref
):
    op = lax.axis_index("op")
    keys = [key for group in MOMENTS for key in group]
    moments = dict(zip(keys, summed(rows, total, len(keys))))
    basis, thetas = all_steps(lambda *key: moments[key], lax.rsqrt)
    half = own_last.shape[0]
    mine = pl.ds(pl.multiple_of(op * half, half), half)
    for place, (sector, side, second, extra, further, last) in enumerate(
        (
            (op, own_side, own_second, own_extra, own_further, own_last),
            (1 - op, mate_side, mate_second, mate_extra, mate_further, mate_last),
        )
    ):
        arrays = {
            ("w", 0): start[place, mine],
            ("u", 1): ratio[place, mine],
            ("a", 0): side[mine],
            ("b", 0): second[mine],
            ("c", 0): extra[0],
            ("d", 0): extra[1],
            ("e", 0): further[...],
            ("f", 0): last[...],
        }
        for i in range(ITERS):
            basis_ref[i, sector] = combined(basis[i + 1], arrays, inverse[place, mine])
    for position, value in enumerate(thetas):
        ritz_ref[position] = value[0, 0]


def one_sector_body(wave_start, left_blocks, right_blocks, term_shifts, preconditioner):
    op = lax.axis_index("op")
    chips = lax.axis_size("sector")
    devices = 2 * chips
    rows, columns = wave_start.shape[1:]
    half = rows // 2
    terms = 2 * left_blocks.shape[0]
    total = float(devices * rows * columns)
    swap = [(i, i ^ 1) for i in range(devices)]
    across = [(i, i + 1) for i in range(1, devices - 1, 2)]
    across = across + [(j, i) for i, j in across]

    def mate(values):
        return lax.ppermute(values, AXES, swap)

    def facing(values):
        return lax.ppermute(values, AXES, across)

    def own_sector(values):
        return lax.dynamic_index_in_dim(values, op, 0, keepdims=False)

    def exchanged(row):
        spread = row.reshape(devices, 1, LANES)
        return lax.all_to_all(spread, AXES, 0, 0, tiled=True).reshape(devices, LANES)

    vmem = pl.BlockSpec(memory_space=pltpu.VMEM)
    smem = pl.BlockSpec(memory_space=pltpu.SMEM)

    def call(kernel, operands, shapes, scalars=0, out_scalars=0, scratch=True):
        return pl.pallas_call(
            kernel,
            out_shape=[jax.ShapeDtypeStruct(shape, kind) for shape, kind in shapes],
            in_specs=[smem] * scalars + [vmem] * (len(operands) - scalars),
            out_specs=[vmem] * (len(shapes) - out_scalars) + [smem] * out_scalars,
            scratch_shapes=[pltpu.VMEM((3, rows, columns), jnp.bfloat16)] * (2 if scratch else 0),
            compiler_params=pltpu.CompilerParams(vmem_limit_bytes=16 * 2**20),
        )(*operands)

    block = (rows, columns)
    f32, bf16 = jnp.float32, jnp.bfloat16
    row_shape = ((devices, LANES), f32)

    half_shape = left_blocks.shape[:1] + left_blocks.shape[2:]
    own_wave, own_preconditioner, sent_left, sent_right = pl.pallas_call(
        picking_kernel,
        out_shape=[jax.ShapeDtypeStruct(shape, f32) for shape in [block] * 2 + [half_shape] * 2],
        in_specs=[pl.BlockSpec(memory_space=pl.ANY)] * 4,
        out_specs=[vmem] * 4,
        scratch_shapes=[pltpu.SemaphoreType.DMA((2 + terms,))],
        compiler_params=pltpu.CompilerParams(vmem_limit_bytes=52 * 2**20),
    )(wave_start, preconditioner, left_blocks, right_blocks)
    facing_wave = facing(own_wave)
    facing_preconditioner = facing(own_preconditioner)
    mate_left, mate_right = mate(sent_left), mate(sent_right)
    shifts = (term_shifts, mate(term_shifts))

    split_shape = (terms,) + left_blocks.shape[2:]
    blocks = call(
        splitting_kernel,
        (left_blocks, right_blocks, mate_left, mate_right),
        [(split_shape, bf16)] * 4,
        scratch=False,
    )

    def around(values):
        return (values, mate(values), facing(values))

    image, start = call(
        first_kernel,
        (*shifts, wave_start, facing_wave, *blocks),
        [(block, f32), ((3,) + block, f32)],
        scalars=2,
    )
    images = around(image)
    side, inverse = call(
        side_kernel,
        (*shifts, start, preconditioner, facing_preconditioner, *blocks),
        [(block, f32), ((3,) + block, f32)],
        scalars=2,
    )
    sides = around(side)
    (early_row,) = call(
        moments_kernel, (start, image, side, inverse), [((1, LANES), f32)], scratch=False
    )
    second, ratio = call(
        second_kernel,
        (*shifts, *images, inverse, early_row, *blocks),
        [(block, f32), ((3,) + block, f32)],
        scalars=2,
    )
    seconds = around(second)
    half_block = (half, columns)
    extra, kept_extra, sent_extra, early_row = call(
        extra_kernel,
        (*shifts, start, ratio, inverse, image, side, second, early_row, *blocks),
        [((2,) + block, f32)] + [((2,) + half_block, f32)] * 2 + [((1, LANES), f32)],
        scalars=2,
    )
    mate_extra = mate(sent_extra)
    further, kept_further, sent_further, early_row = call(
        further_kernel,
        (*shifts, start, inverse, image, *sides, second, extra, early_row, *blocks),
        [(block, f32)] + [(half_block, f32)] * 2 + [((1, LANES), f32)],
        scalars=2,
    )
    mate_further = mate(sent_further)
    kept, sent, row = call(
        third_kernel,
        (*shifts, start, inverse, image, side, *seconds, extra, further, early_row, *blocks),
        [(half_block, f32)] * 2 + [row_shape],
        scalars=2,
    )
    mate_last = mate(sent)
    row, mate_extra, mate_further = lax.optimization_barrier((row, mate_extra, mate_further))
    basis, ritz = call(
        functools.partial(last_kernel, total),
        (exchanged(row), start, ratio, inverse, *sides[:2], *seconds[:2], kept_extra, mate_extra,
         kept_further, mate_further, kept, mate_last),
        [((ITERS, 2) + half_block, f32), ((ITERS,), f32)],
        out_scalars=1,
        scratch=False,
    )
    return (basis, ritz)


def with_halo(cells, sides, width):
    for axis, dim in sides:
        count = lax.axis_size(axis)
        ends = count - 1
        head = lax.slice_in_dim(cells, 0, width, axis=dim)
        tail = lax.slice_in_dim(cells, cells.shape[dim] - width, cells.shape[dim], axis=dim)
        cells = jnp.concatenate(
            [
                lax.ppermute(tail, axis, [(i, (i + 1) % count) for i in range(ends)]),
                cells,
                lax.ppermute(head, axis, [((i + 1) % count, i) for i in range(ends)]),
            ],
            axis=dim,
        )
    return cells


def split_terms_body(wave_start, left_blocks, right_blocks, term_shifts, preconditioner):
    highest = lax.Precision.HIGHEST
    width = wave_start.shape[1]
    row_count = width // lax.axis_size("op")
    first_row = lax.axis_index("op") * row_count
    total = float(wave_start.shape[0] * lax.axis_size("sector") * width * wave_start.shape[2])

    def portion(values):
        return lax.dynamic_slice_in_dim(values, first_row, row_count, axis=values.ndim - 2)

    start_sum = total_sum(jnp.sum(jnp.square(portion(wave_start)))[None])[0] / total
    basis = [wave_start * lax.rsqrt(start_sum + EPSILON)]
    ritz = []
    for _ in range(ITERS):
        latest = basis[-1]
        padded = with_halo(latest, (("sector", 0),), 1)
        shift = term_shifts[:, None, None, None]
        source = jnp.where(
            shift == 1,
            padded[None, :-2],
            jnp.where(shift == -1, padded[None, 2:], padded[None, 1:-1]),
        )
        inner = jnp.einsum("ksab,ksbc->ksac", left_blocks, source, precision=highest)
        image = lax.psum(jnp.einsum("ksac,kscd->sad", inner, right_blocks, precision=highest), "op")
        inverse = 1.0 / preconditioner
        pieces = products([portion(member) for member in basis], portion(image), portion(inverse))
        theta, correlations, scale = coefficients(
            total_sum(jnp.stack(pieces)), total, len(basis)
        )
        ortho = (image - theta * latest) * inverse
        for position, member in enumerate(basis):
            ortho = ortho - correlations[position] * member
        basis.append(ortho * scale)
        ritz.append(theta)
    output = jnp.stack([portion(member) for member in basis[1:]])
    return (output, jnp.stack(ritz))


def solution(mesh):
    placed = (
        P("sector", None, None),
        P("op", "sector", None, None),
        P("op", "sector", None, None),
        P("op"),
        P("sector", None, None),
    )

    def body(wave_start, *operands):
        one_each = mesh.shape["op"] == 2 and wave_start.shape[0] == 2
        return (one_sector_body if one_each else split_terms_body)(wave_start, *operands)

    return jax.shard_map(
        body,
        mesh=mesh,
        in_specs=placed,
        out_specs=(P(None, "sector", "op", None), P()),
        check_vma=False,
    )
```

```python
import functools

import jax
import jax.numpy as jnp
from jax import lax
from jax.experimental import pallas as pl
from jax.experimental.pallas import tpu as pltpu
from jax.sharding import PartitionSpec as P

ITERS = 3


EPSILON = 1e-06

AXES = ("sector", "op")

LANES = 128


def total_sum(values):
    devices = lax.axis_size("sector") * lax.axis_size("op")
    row = jnp.pad(values, (0, LANES - values.shape[0]))
    rows = lax.all_to_all(jnp.broadcast_to(row, (devices, LANES)), AXES, 0, 0, tiled=True)
    return jnp.sum(rows, axis=0)[: values.shape[0]]


def coefficients(sums, total, count):
    sums = sums / total
    theta = sums[0]
    correlations = sums[4 : 4 + count] - theta * sums[4 + count : 4 + 2 * count]
    length = (
        sums[1]
        - 2.0 * theta * sums[2]
        + theta * theta * sums[3]
        - jnp.sum(jnp.square(correlations))
    )
    return theta, correlations, lax.rsqrt(length + EPSILON)


def products(members, image, inverse):
    latest = members[-1]
    ratio_image = image * inverse
    ratio_latest = latest * inverse
    pieces = [
        jnp.sum(latest * image),
        jnp.sum(ratio_image * ratio_image),
        jnp.sum(ratio_image * ratio_latest),
        jnp.sum(ratio_latest * ratio_latest),
    ]
    pieces = pieces + [jnp.sum(member * ratio_image) for member in members]
    pieces = pieces + [jnp.sum(member * ratio_latest) for member in members]
    return pieces


def split(values):
    high = values.astype(jnp.bfloat16)
    return high, (values - high.astype(jnp.float32)).astype(jnp.bfloat16)


def dot_split(lhs_high, lhs_low, rhs_high, rhs_low):
    dot = functools.partial(jnp.dot, preferred_element_type=jnp.float32)
    rows = lhs_high.shape[0]
    both = dot(jnp.concatenate([lhs_high, lhs_low], axis=0), rhs_high)
    return both[:rows] + (both[rows:] + dot(lhs_high, rhs_low))


def apply_terms(sources, vectors, left, right):
    left_high, left_low = left
    right_high, right_low = right
    vector_high, vector_low = vectors
    inners = [
        split(
            dot_split(left_high[term], left_low[term], vector_high[source], vector_low[source])
        )
        for term, source in enumerate(sources)
    ]
    image = None
    for term, inner in enumerate(inners):
        part = dot_split(*inner, right_high[term], right_low[term])
        image = part if image is None else image + part
    return image


def term_sources(own_shifts, mate_shifts):
    toward_mate = jnp.where(lax.axis_index("op") == 0, -1, 1)
    shifts = [refs[i] for refs in (own_shifts, mate_shifts) for i in range(refs.shape[0])]
    return [
        jnp.where(shift == 0, 0, jnp.where(shift == toward_mate, 1, 2)) for shift in shifts
    ]


CHUNK = 32


def row_of_sums(moments, refs, inverse, first=0, row=None):
    rows, columns = inverse.shape
    lane = lax.broadcasted_iota(jnp.int32, (1, LANES), 1)
    if row is None:
        row = jnp.zeros((1, LANES), jnp.float32)
    pairs = {}
    for x, y, n in moments:
        pairs.setdefault((x, y), []).append(n)
    totals = {}
    for top in range(0, rows, CHUNK):
        here = pl.ds(top, CHUNK)
        powers = [None, inverse[here]]
        while len(powers) <= max(n for _, _, n in moments):
            powers.append(powers[-1] * powers[1])
        for (x, y), orders in pairs.items():
            product = refs[x][here] * refs[y][here]
            for n in orders:
                weighted = product * powers[n] if n else product
                part = jnp.sum(weighted.reshape(-1, 8, columns), axis=0)
                part = sum(part[:, i : i + LANES] for i in range(0, columns, LANES))
                totals[x, y, n] = totals[x, y, n] + part if top else part
    for position, moment in enumerate(moments):
        whole = jnp.sum(totals[moment], axis=(0, 1), keepdims=True)
        row = jnp.where(lane == first + position, whole, row)
    return row


def summed(rows, total, count):
    whole = jnp.sum(rows[...], axis=0, keepdims=True) * (1.0 / total)
    return [jnp.broadcast_to(whole[:, i : i + 1], (8, LANES)) for i in range(count)]


def one_of(value):
    return value[:1, :1]


H_OF = {
    ("w", 0): "u",
    ("w", 1): "a",
    ("u", 1): "b",
    ("w", 2): "c",
    ("u", 2): "d",
    ("a", 1): "e",
    ("b", 1): "f",
}

START_SCALE = 2.0**10
H_SCALE = 2.0**7


def plus(vector, other, factor):
    result = dict(vector)
    for word, value in other.items():
        term = value * factor
        result[word] = result[word] + term if word in result else term
    return result


def times_inverse(vector):
    return {(name, n + 1): value for (name, n), value in vector.items()}


def times_h(vector):
    return {(H_OF[word], 0): value * H_SCALE for word, value in vector.items()}


def inner(one, other, moment):
    result = None
    for (x, n), value in one.items():
        part = None
        for (y, m), factor in other.items():
            term = factor * moment(*sorted((x, y)), n + m)
            part = term if part is None else part + term
        part = value * part
        result = part if result is None else result + part
    return result


def all_steps(moment, inverse_root):
    basis = [{("w", 0): inverse_root(moment("w", "w", 0) + EPSILON * START_SCALE**2)}]
    thetas = []
    for _ in range(ITERS):
        latest = basis[-1]
        image = times_h(latest)
        theta = inner(latest, image, moment)
        correction = times_inverse(plus(image, latest, -theta))
        ortho = correction
        for member in basis:
            ortho = plus(ortho, member, -inner(member, correction, moment))
        scale = inverse_root(inner(ortho, ortho, moment) + EPSILON)
        basis.append({word: value * scale for word, value in ortho.items()})
        thetas.append(theta)
    return basis, thetas


def needed_moments():
    asked = {}

    def moment(x, y, n):
        asked[x, y, n] = True
        return 1.0

    all_steps(moment, lambda value: 1.0)
    stages = ("wua", "bcd", "e", "f")
    groups = [[] for _ in stages]
    for key in asked:
        groups[max(i for i, names in enumerate(stages) if set(key[:2]) & set(names))].append(key)
    return groups


def combined(vector, arrays, inverse):
    words = {name: (n, values) for (name, n), values in arrays.items()}
    result = None
    for n in range(max(n for _, n in vector), -1, -1):
        if result is not None:
            result = result * inverse
        for (name, m), value in vector.items():
            held, values = words[name]
            if m - held == n:
                term = one_of(value) * values
                result = term if result is None else result + term
    return result


MOMENTS = needed_moments()
FIRST_LANE = [sum(len(group) for group in MOMENTS[:i]) for i in range(len(MOMENTS) + 1)]


def inverted(values):
    return jnp.where(values > 0.0, 1.0 / values, 0.0)


def copy_all(pairs, arrived):
    copies = [
        pltpu.make_async_copy(source, target, arrived.at[i])
        for i, (source, target) in enumerate(pairs)
    ]
    for copy in copies:
        copy.start()
    for copy in copies:
        copy.wait()


def picking_kernel(
    wave, preconditioner, left, right, own_wave, own_preconditioner, sent_left, sent_right, arrived
):
    op = lax.axis_index("op")
    pairs = [(wave.at[op], own_wave), (preconditioner.at[op], own_preconditioner)]
    for values, sent in ((left, sent_left), (right, sent_right)):
        for term in range(values.shape[0]):
            pairs.append((values.at[term, 1 - op], sent.at[term]))
    copy_all(pairs, arrived)


def splitting_kernel(
    own_left, own_right, mate_left, mate_right, left_high, left_low, right_high, right_low
):
    op = lax.axis_index("op")
    count = own_left.shape[0]
    for term in range(count):
        left_high[term], left_low[term] = split(own_left[term, op] * (1.0 / H_SCALE))
        right_high[term], right_low[term] = split(own_right[term, op])
        place = count + term
        left_high[place], left_low[place] = split(mate_left[term] * (1.0 / H_SCALE))
        right_high[place], right_low[place] = split(mate_right[term])


def first_kernel(
    own_shifts, mate_shifts, wave, facing_wave, left_high, left_low, right_high, right_low,
    image_ref, start_ref, high, low,
):
    op = lax.axis_index("op")
    sources = term_sources(own_shifts, mate_shifts)
    for place, values in enumerate((wave[op], wave[1 - op], facing_wave[...])):
        start = values * START_SCALE
        start_ref[place] = start
        high[place], low[place] = split(start)
    image_ref[...] = apply_terms(
        sources, (high, low), (left_high, left_low), (right_high, right_low)
    )


def side_kernel(
    own_shifts, mate_shifts, start, preconditioner, facing_preconditioner,
    left_high, left_low, right_high, right_low, side_ref, inverse_ref, high, low,
):
    op = lax.axis_index("op")
    sources = term_sources(own_shifts, mate_shifts)
    divisors = (preconditioner[op], preconditioner[1 - op], facing_preconditioner[...])
    for place in range(3):
        inverse = inverted(divisors[place])
        inverse_ref[place] = inverse
        high[place], low[place] = split(start[place] * inverse)
    side_ref[...] = apply_terms(
        sources, (high, low), (left_high, left_low), (right_high, right_low)
    )


def moments_kernel(start, image, side, inverse, row_ref):
    refs = {"w": start.at[0], "u": image, "a": side}
    row_ref[...] = row_of_sums(MOMENTS[0], refs, inverse.at[0])


def second_kernel(
    own_shifts, mate_shifts, own_image, mate_image, facing_image, inverse, _,
    left_high, left_low, right_high, right_low, image_ref, ratio_ref, high, low,
):
    sources = term_sources(own_shifts, mate_shifts)
    for place, image in enumerate((own_image, mate_image, facing_image)):
        ratio = image[...] * inverse[place]
        ratio_ref[place] = ratio
        high[place], low[place] = split(ratio)
    image_ref[...] = apply_terms(
        sources, (high, low), (left_high, left_low), (right_high, right_low)
    )


def halves(image, kept_ref, sent_ref):
    op = lax.axis_index("op")
    half = kept_ref.shape[0]
    kept_ref[...] = jnp.where(op == 0, image[:half], image[half:])
    sent_ref[...] = jnp.where(op == 0, image[half:], image[:half])


def extra_kernel(
    own_shifts, mate_shifts, start, ratio, inverse, image, side, second, early_row,
    left_high, left_low, right_high, right_low, extra_ref, kept_ref, sent_ref, row_ref, high, low,
):
    sources = term_sources(own_shifts, mate_shifts)
    refs = {"w": start.at[0], "u": image, "a": side, "b": second}
    for i, name in enumerate("cd"):
        for place in range(3):
            once = start[place] * inverse[place] if name == "c" else ratio[place]
            high[place], low[place] = split(once * inverse[place])
        extra = apply_terms(sources, (high, low), (left_high, left_low), (right_high, right_low))
        refs[name] = extra_ref.at[i]
        extra_ref[i] = extra
        halves(extra, kept_ref.at[i], sent_ref.at[i])
    row_ref[...] = row_of_sums(MOMENTS[1], refs, inverse.at[0], FIRST_LANE[1], early_row[...])


def further_kernel(
    own_shifts, mate_shifts, start, inverse, image, own_side, mate_side, facing_side, second,
    extra, early_row, left_high, left_low, right_high, right_low, further_ref, kept_ref, sent_ref,
    row_ref, high, low,
):
    sources = term_sources(own_shifts, mate_shifts)
    for place, side in enumerate((own_side, mate_side, facing_side)):
        high[place], low[place] = split(side[...] * inverse[place])
    further = apply_terms(sources, (high, low), (left_high, left_low), (right_high, right_low))
    further_ref[...] = further
    halves(further, kept_ref, sent_ref)
    refs = {"w": start.at[0], "u": image, "a": own_side, "b": second}
    refs.update(c=extra.at[0], d=extra.at[1], e=further_ref)
    row_ref[...] = row_of_sums(MOMENTS[2], refs, inverse.at[0], FIRST_LANE[2], early_row[...])


def third_kernel(
    own_shifts, mate_shifts, start, inverse, image, side, own_second, mate_second, facing_second,
    extra, further, early_row, left_high, left_low, right_high, right_low,
    kept_ref, sent_ref, row_ref, high, low, last_ref,
):
    sources = term_sources(own_shifts, mate_shifts)
    for place, second in enumerate((own_second, mate_second, facing_second)):
        high[place], low[place] = split(second[...] * inverse[place])
    last = apply_terms(sources, (high, low), (left_high, left_low), (right_high, right_low))
    halves(last, kept_ref, sent_ref)
    last_ref[...] = last
    refs = {"w": start.at[0], "u": image, "a": side, "b": own_second}
    refs.update(c=extra.at[0], d=extra.at[1], e=further, f=last_ref)
    row = row_of_sums(MOMENTS[3], refs, inverse.at[0], FIRST_LANE[3], early_row[...])
    row_ref[...] = jnp.broadcast_to(row, row_ref.shape)


def last_kernel(
    total, rows, start, ratio, inverse, own_side, mate_side, own_second, mate_second, own_extra,
    mate_extra, own_further, mate_further, own_last, mate_last, basis_ref, ritz_ref
):
    op = lax.axis_index("op")
    keys = [key for group in MOMENTS for key in group]
    moments = dict(zip(keys, summed(rows, total, len(keys))))
    basis, thetas = all_steps(lambda *key: moments[key], lax.rsqrt)
    half = own_last.shape[0]
    mine = pl.ds(pl.multiple_of(op * half, half), half)
    for place, (sector, side, second, extra, further, last) in enumerate(
        (
            (op, own_side, own_second, own_extra, own_further, own_last),
            (1 - op, mate_side, mate_second, mate_extra, mate_further, mate_last),
        )
    ):
        arrays = {
            ("w", 0): start[place, mine],
            ("u", 1): ratio[place, mine],
            ("a", 0): side[mine],
            ("b", 0): second[mine],
            ("c", 0): extra[0],
            ("d", 0): extra[1],
            ("e", 0): further[...],
            ("f", 0): last[...],
        }
        for i in range(ITERS):
            basis_ref[i, sector] = combined(basis[i + 1], arrays, inverse[place, mine])
    for position, value in enumerate(thetas):
        ritz_ref[position] = value[0, 0]


def one_sector_body(wave_start, left_blocks, right_blocks, term_shifts, preconditioner):
    op = lax.axis_index("op")
    chips = lax.axis_size("sector")
    devices = 2 * chips
    rows, columns = wave_start.shape[1:]
    half = rows // 2
    terms = 2 * left_blocks.shape[0]
    total = float(devices * rows * columns)
    swap = [(i, i ^ 1) for i in range(devices)]
    across = [(i, i + 1) for i in range(1, devices - 1, 2)]
    across = across + [(j, i) for i, j in across]

    def mate(values):
        return lax.ppermute(values, AXES, swap)

    def facing(values):
        return lax.ppermute(values, AXES, across)

    def own_sector(values):
        return lax.dynamic_index_in_dim(values, op, 0, keepdims=False)

    def exchanged(row):
        spread = row.reshape(devices, 1, LANES)
        return lax.all_to_all(spread, AXES, 0, 0, tiled=True).reshape(devices, LANES)

    vmem = pl.BlockSpec(memory_space=pltpu.VMEM)
    smem = pl.BlockSpec(memory_space=pltpu.SMEM)

    def call(
        kernel, operands, shapes, scalars=0, out_scalars=0, scratch=True, more_scratch=()
    ):
        return pl.pallas_call(
            kernel,
            out_shape=[jax.ShapeDtypeStruct(shape, kind) for shape, kind in shapes],
            in_specs=[smem] * scalars + [vmem] * (len(operands) - scalars),
            out_specs=[vmem] * (len(shapes) - out_scalars) + [smem] * out_scalars,
            scratch_shapes=[pltpu.VMEM((3, rows, columns), jnp.bfloat16)] * (2 if scratch else 0)
            + list(more_scratch),
            compiler_params=pltpu.CompilerParams(vmem_limit_bytes=16 * 2**20),
        )(*operands)

    block = (rows, columns)
    f32, bf16 = jnp.float32, jnp.bfloat16
    row_shape = ((devices, LANES), f32)

    half_shape = left_blocks.shape[:1] + left_blocks.shape[2:]
    own_wave, own_preconditioner, sent_left, sent_right = pl.pallas_call(
        picking_kernel,
        out_shape=[jax.ShapeDtypeStruct(shape, f32) for shape in [block] * 2 + [half_shape] * 2],
        in_specs=[pl.BlockSpec(memory_space=pl.ANY)] * 4,
        out_specs=[vmem] * 4,
        scratch_shapes=[pltpu.SemaphoreType.DMA((2 + terms,))],
        compiler_params=pltpu.CompilerParams(vmem_limit_bytes=52 * 2**20),
    )(wave_start, preconditioner, left_blocks, right_blocks)
    facing_wave = facing(own_wave)
    facing_preconditioner = facing(own_preconditioner)
    mate_left, mate_right = mate(sent_left), mate(sent_right)
    shifts = (term_shifts, mate(term_shifts))

    split_shape = (terms,) + left_blocks.shape[2:]
    blocks = call(
        splitting_kernel,
        (left_blocks, right_blocks, mate_left, mate_right),
        [(split_shape, bf16)] * 4,
        scratch=False,
    )

    def around(values):
        return (values, mate(values), facing(values))

    image, start = call(
        first_kernel,
        (*shifts, wave_start, facing_wave, *blocks),
        [(block, f32), ((3,) + block, f32)],
        scalars=2,
    )
    images = around(image)
    side, inverse = call(
        side_kernel,
        (*shifts, start, preconditioner, facing_preconditioner, *blocks),
        [(block, f32), ((3,) + block, f32)],
        scalars=2,
    )
    sides = around(side)
    (early_row,) = call(
        moments_kernel, (start, image, side, inverse), [((1, LANES), f32)], scratch=False
    )
    second, ratio = call(
        second_kernel,
        (*shifts, *images, inverse, early_row, *blocks),
        [(block, f32), ((3,) + block, f32)],
        scalars=2,
    )
    seconds = around(second)
    half_block = (half, columns)
    extra, kept_extra, sent_extra, early_row = call(
        extra_kernel,
        (*shifts, start, ratio, inverse, image, side, second, early_row, *blocks),
        [((2,) + block, f32)] + [((2,) + half_block, f32)] * 2 + [((1, LANES), f32)],
        scalars=2,
    )
    mate_extra = mate(sent_extra)
    further, kept_further, sent_further, early_row = call(
        further_kernel,
        (*shifts, start, inverse, image, *sides, second, extra, early_row, *blocks),
        [(block, f32)] + [(half_block, f32)] * 2 + [((1, LANES), f32)],
        scalars=2,
    )
    mate_further = mate(sent_further)
    kept, sent, row = call(
        third_kernel,
        (*shifts, start, inverse, image, side, *seconds, extra, further, early_row, *blocks),
        [(half_block, f32)] * 2 + [row_shape],
        scalars=2,
        more_scratch=[pltpu.VMEM(block, f32)],
    )
    mate_last = mate(sent)
    row, mate_extra, mate_further = lax.optimization_barrier((row, mate_extra, mate_further))
    basis, ritz = call(
        functools.partial(last_kernel, total),
        (exchanged(row), start, ratio, inverse, *sides[:2], *seconds[:2], kept_extra, mate_extra,
         kept_further, mate_further, kept, mate_last),
        [((ITERS, 2) + half_block, f32), ((ITERS,), f32)],
        out_scalars=1,
        scratch=False,
    )
    return (basis, ritz)


def with_halo(cells, sides, width):
    for axis, dim in sides:
        count = lax.axis_size(axis)
        ends = count - 1
        head = lax.slice_in_dim(cells, 0, width, axis=dim)
        tail = lax.slice_in_dim(cells, cells.shape[dim] - width, cells.shape[dim], axis=dim)
        cells = jnp.concatenate(
            [
                lax.ppermute(tail, axis, [(i, (i + 1) % count) for i in range(ends)]),
                cells,
                lax.ppermute(head, axis, [((i + 1) % count, i) for i in range(ends)]),
            ],
            axis=dim,
        )
    return cells


def split_terms_body(wave_start, left_blocks, right_blocks, term_shifts, preconditioner):
    highest = lax.Precision.HIGHEST
    width = wave_start.shape[1]
    row_count = width // lax.axis_size("op")
    first_row = lax.axis_index("op") * row_count
    total = float(wave_start.shape[0] * lax.axis_size("sector") * width * wave_start.shape[2])

    def portion(values):
        return lax.dynamic_slice_in_dim(values, first_row, row_count, axis=values.ndim - 2)

    start_sum = total_sum(jnp.sum(jnp.square(portion(wave_start)))[None])[0] / total
    basis = [wave_start * lax.rsqrt(start_sum + EPSILON)]
    ritz = []
    for _ in range(ITERS):
        latest = basis[-1]
        padded = with_halo(latest, (("sector", 0),), 1)
        shift = term_shifts[:, None, None, None]
        source = jnp.where(
            shift == 1,
            padded[None, :-2],
            jnp.where(shift == -1, padded[None, 2:], padded[None, 1:-1]),
        )
        inner = jnp.einsum("ksab,ksbc->ksac", left_blocks, source, precision=highest)
        image = lax.psum(jnp.einsum("ksac,kscd->sad", inner, right_blocks, precision=highest), "op")
        inverse = 1.0 / preconditioner
        pieces = products([portion(member) for member in basis], portion(image), portion(inverse))
        theta, correlations, scale = coefficients(
            total_sum(jnp.stack(pieces)), total, len(basis)
        )
        ortho = (image - theta * latest) * inverse
        for position, member in enumerate(basis):
            ortho = ortho - correlations[position] * member
        basis.append(ortho * scale)
        ritz.append(theta)
    output = jnp.stack([portion(member) for member in basis[1:]])
    return (output, jnp.stack(ritz))


def solution(mesh):
    placed = (
        P("sector", None, None),
        P("op", "sector", None, None),
        P("op", "sector", None, None),
        P("op"),
        P("sector", None, None),
    )

    def body(wave_start, *operands):
        one_each = mesh.shape["op"] == 2 and wave_start.shape[0] == 2
        return (one_sector_body if one_each else split_terms_body)(wave_start, *operands)

    return jax.shard_map(
        body,
        mesh=mesh,
        in_specs=placed,
        out_specs=(P(None, "sector", "op", None), P()),
        check_vma=False,
    )
```

```python
import functools

import jax
import jax.numpy as jnp
from jax import lax
from jax.experimental import pallas as pl
from jax.experimental.pallas import tpu as pltpu
from jax.sharding import PartitionSpec as P

ITERS = 3


EPSILON = 1e-06

AXES = ("sector", "op")

LANES = 128


def total_sum(values):
    devices = lax.axis_size("sector") * lax.axis_size("op")
    row = jnp.pad(values, (0, LANES - values.shape[0]))
    rows = lax.all_to_all(jnp.broadcast_to(row, (devices, LANES)), AXES, 0, 0, tiled=True)
    return jnp.sum(rows, axis=0)[: values.shape[0]]


def coefficients(sums, total, count):
    sums = sums / total
    theta = sums[0]
    correlations = sums[4 : 4 + count] - theta * sums[4 + count : 4 + 2 * count]
    length = (
        sums[1]
        - 2.0 * theta * sums[2]
        + theta * theta * sums[3]
        - jnp.sum(jnp.square(correlations))
    )
    return theta, correlations, lax.rsqrt(length + EPSILON)


def products(members, image, inverse):
    latest = members[-1]
    ratio_image = image * inverse
    ratio_latest = latest * inverse
    pieces = [
        jnp.sum(latest * image),
        jnp.sum(ratio_image * ratio_image),
        jnp.sum(ratio_image * ratio_latest),
        jnp.sum(ratio_latest * ratio_latest),
    ]
    pieces = pieces + [jnp.sum(member * ratio_image) for member in members]
    pieces = pieces + [jnp.sum(member * ratio_latest) for member in members]
    return pieces


def split(values):
    high = values.astype(jnp.bfloat16)
    return high, (values - high.astype(jnp.float32)).astype(jnp.bfloat16)


def dot_split(lhs_high, lhs_low, rhs_high, rhs_low):
    dot = functools.partial(jnp.dot, preferred_element_type=jnp.float32)
    rows = lhs_high.shape[0]
    both = dot(jnp.concatenate([lhs_high, lhs_low], axis=0), rhs_high)
    return both[:rows] + (both[rows:] + dot(lhs_high, rhs_low))


def apply_terms(sources, vectors, left, right):
    left_high, left_low = left
    right_high, right_low = right
    vector_high, vector_low = vectors
    inners = [
        split(
            dot_split(left_high[term], left_low[term], vector_high[source], vector_low[source])
        )
        for term, source in enumerate(sources)
    ]
    image = None
    for term, inner in enumerate(inners):
        part = dot_split(*inner, right_high[term], right_low[term])
        image = part if image is None else image + part
    return image


def term_sources(own_shifts, mate_shifts):
    toward_mate = jnp.where(lax.axis_index("op") == 0, -1, 1)
    shifts = [refs[i] for refs in (own_shifts, mate_shifts) for i in range(refs.shape[0])]
    return [
        jnp.where(shift == 0, 0, jnp.where(shift == toward_mate, 1, 2)) for shift in shifts
    ]


CHUNK = 32


def row_of_sums(moments, refs, inverse, first=0, row=None):
    rows, columns = inverse.shape
    lane = lax.broadcasted_iota(jnp.int32, (1, LANES), 1)
    if row is None:
        row = jnp.zeros((1, LANES), jnp.float32)
    pairs = {}
    for x, y, n in moments:
        pairs.setdefault((x, y), []).append(n)
    totals = {}
    for top in range(0, rows, CHUNK):
        here = pl.ds(top, CHUNK)
        powers = [None, inverse[here]]
        while len(powers) <= max(n for _, _, n in moments):
            powers.append(powers[-1] * powers[1])
        for (x, y), orders in pairs.items():
            product = refs[x][here] * refs[y][here]
            for n in orders:
                weighted = product * powers[n] if n else product
                part = jnp.sum(weighted.reshape(-1, 8, columns), axis=0)
                part = sum(part[:, i : i + LANES] for i in range(0, columns, LANES))
                totals[x, y, n] = totals[x, y, n] + part if top else part
    for position, moment in enumerate(moments):
        whole = jnp.sum(totals[moment], axis=(0, 1), keepdims=True)
        row = jnp.where(lane == first + position, whole, row)
    return row


def summed(rows, total, count):
    whole = jnp.sum(rows[...], axis=0, keepdims=True) * (1.0 / total)
    return [jnp.broadcast_to(whole[:, i : i + 1], (8, LANES)) for i in range(count)]


def one_of(value):
    return value[:1, :1]


H_OF = {
    ("w", 0): "u",
    ("w", 1): "a",
    ("u", 1): "b",
    ("w", 2): "c",
    ("u", 2): "d",
    ("a", 1): "e",
    ("b", 1): "f",
}

START_SCALE = 2.0**10
H_SCALE = 2.0**7


def plus(vector, other, factor):
    result = dict(vector)
    for word, value in other.items():
        term = value * factor
        result[word] = result[word] + term if word in result else term
    return result


def times_inverse(vector):
    return {(name, n + 1): value for (name, n), value in vector.items()}


def times_h(vector):
    return {(H_OF[word], 0): value * H_SCALE for word, value in vector.items()}


def inner(one, other, moment):
    result = None
    for (x, n), value in one.items():
        part = None
        for (y, m), factor in other.items():
            term = factor * moment(*sorted((x, y)), n + m)
            part = term if part is None else part + term
        part = value * part
        result = part if result is None else result + part
    return result


def all_steps(moment, inverse_root):
    basis = [{("w", 0): inverse_root(moment("w", "w", 0) + EPSILON * START_SCALE**2)}]
    thetas = []
    for _ in range(ITERS):
        latest = basis[-1]
        image = times_h(latest)
        theta = inner(latest, image, moment)
        correction = times_inverse(plus(image, latest, -theta))
        ortho = correction
        for member in basis:
            ortho = plus(ortho, member, -inner(member, correction, moment))
        scale = inverse_root(inner(ortho, ortho, moment) + EPSILON)
        basis.append({word: value * scale for word, value in ortho.items()})
        thetas.append(theta)
    return basis, thetas


def needed_moments():
    asked = {}

    def moment(x, y, n):
        asked[x, y, n] = True
        return 1.0

    all_steps(moment, lambda value: 1.0)
    stages = ("wua", "bcd", "e", "f")
    groups = [[] for _ in stages]
    for key in asked:
        groups[max(i for i, names in enumerate(stages) if set(key[:2]) & set(names))].append(key)
    return groups


def combined(vector, arrays, inverse):
    words = {name: (n, values) for (name, n), values in arrays.items()}
    result = None
    for n in range(max(n for _, n in vector), -1, -1):
        if result is not None:
            result = result * inverse
        for (name, m), value in vector.items():
            held, values = words[name]
            if m - held == n:
                term = one_of(value) * values
                result = term if result is None else result + term
    return result


MOMENTS = needed_moments()
FIRST_LANE = [sum(len(group) for group in MOMENTS[:i]) for i in range(len(MOMENTS) + 1)]


def inverted(values):
    return jnp.where(values > 0.0, 1.0 / values, 0.0)


def copy_all(pairs, arrived):
    copies = [
        pltpu.make_async_copy(source, target, arrived.at[i])
        for i, (source, target) in enumerate(pairs)
    ]
    for copy in copies:
        copy.start()
    for copy in copies:
        copy.wait()


def picking_kernel(
    wave, preconditioner, left, right, own_wave, own_preconditioner, sent_left, sent_right, arrived
):
    op = lax.axis_index("op")
    pairs = [(wave.at[op], own_wave), (preconditioner.at[op], own_preconditioner)]
    for values, sent in ((left, sent_left), (right, sent_right)):
        for term in range(values.shape[0]):
            pairs.append((values.at[term, 1 - op], sent.at[term]))
    copy_all(pairs, arrived)


def splitting_kernel(
    own_left, own_right, mate_left, mate_right, left_high, left_low, right_high, right_low
):
    op = lax.axis_index("op")
    count = own_left.shape[0]
    for term in range(count):
        left_high[term], left_low[term] = split(own_left[term, op] * (1.0 / H_SCALE))
        right_high[term], right_low[term] = split(own_right[term, op])
        place = count + term
        left_high[place], left_low[place] = split(mate_left[term] * (1.0 / H_SCALE))
        right_high[place], right_low[place] = split(mate_right[term])


def first_kernel(
    own_shifts, mate_shifts, wave, facing_wave, left_high, left_low, right_high, right_low,
    image_ref, start_ref, high, low,
):
    op = lax.axis_index("op")
    sources = term_sources(own_shifts, mate_shifts)
    for place, values in enumerate((wave[op], wave[1 - op], facing_wave[...])):
        start = values * START_SCALE
        start_ref[place] = start
        high[place], low[place] = split(start)
    image_ref[...] = apply_terms(
        sources, (high, low), (left_high, left_low), (right_high, right_low)
    )


def side_kernel(
    own_shifts, mate_shifts, start, preconditioner, facing_preconditioner,
    left_high, left_low, right_high, right_low, side_ref, inverse_ref, high, low,
):
    op = lax.axis_index("op")
    sources = term_sources(own_shifts, mate_shifts)
    divisors = (preconditioner[op], preconditioner[1 - op], facing_preconditioner[...])
    for place in range(3):
        inverse = inverted(divisors[place])
        inverse_ref[place] = inverse
        high[place], low[place] = split(start[place] * inverse)
    side_ref[...] = apply_terms(
        sources, (high, low), (left_high, left_low), (right_high, right_low)
    )


def moments_kernel(start, image, side, inverse, row_ref):
    refs = {"w": start.at[0], "u": image, "a": side}
    row_ref[...] = row_of_sums(MOMENTS[0], refs, inverse.at[0])


def second_kernel(
    own_shifts, mate_shifts, own_image, mate_image, facing_image, inverse, _,
    left_high, left_low, right_high, right_low, image_ref, ratio_ref, high, low,
):
    sources = term_sources(own_shifts, mate_shifts)
    for place, image in enumerate((own_image, mate_image, facing_image)):
        ratio = image[...] * inverse[place]
        ratio_ref[place] = ratio
        high[place], low[place] = split(ratio)
    image_ref[...] = apply_terms(
        sources, (high, low), (left_high, left_low), (right_high, right_low)
    )


def halves(image, kept_ref, sent_ref):
    op = lax.axis_index("op")
    half = kept_ref.shape[0]
    kept_ref[...] = jnp.where(op == 0, image[:half], image[half:])
    sent_ref[...] = jnp.where(op == 0, image[half:], image[:half])


def extra_kernel(
    own_shifts, mate_shifts, start, ratio, inverse, image, side, second, early_row,
    left_high, left_low, right_high, right_low, extra_ref, kept_ref, sent_ref, row_ref, high, low,
):
    sources = term_sources(own_shifts, mate_shifts)
    refs = {"w": start.at[0], "u": image, "a": side, "b": second}
    for i, name in enumerate("cd"):
        for place in range(3):
            once = start[place] * inverse[place] if name == "c" else ratio[place]
            high[place], low[place] = split(once * inverse[place])
        extra = apply_terms(sources, (high, low), (left_high, left_low), (right_high, right_low))
        refs[name] = extra_ref.at[i]
        extra_ref[i] = extra
        halves(extra, kept_ref.at[i], sent_ref.at[i])
    row_ref[...] = row_of_sums(MOMENTS[1], refs, inverse.at[0], FIRST_LANE[1], early_row[...])


def further_kernel(
    own_shifts, mate_shifts, start, inverse, image, own_side, mate_side, facing_side, second,
    extra, early_row, left_high, left_low, right_high, right_low, further_ref, kept_ref, sent_ref,
    row_ref, high, low,
):
    sources = term_sources(own_shifts, mate_shifts)
    for place, side in enumerate((own_side, mate_side, facing_side)):
        high[place], low[place] = split(side[...] * inverse[place])
    further = apply_terms(sources, (high, low), (left_high, left_low), (right_high, right_low))
    further_ref[...] = further
    halves(further, kept_ref, sent_ref)
    refs = {"w": start.at[0], "u": image, "a": own_side, "b": second}
    refs.update(c=extra.at[0], d=extra.at[1], e=further_ref)
    row_ref[...] = row_of_sums(MOMENTS[2], refs, inverse.at[0], FIRST_LANE[2], early_row[...])


def third_kernel(
    own_shifts, mate_shifts, start, inverse, image, side, own_second, mate_second, facing_second,
    extra, further, early_row, left_high, left_low, right_high, right_low,
    kept_ref, sent_ref, row_ref, high, low, last_ref,
):
    sources = term_sources(own_shifts, mate_shifts)
    for place, second in enumerate((own_second, mate_second, facing_second)):
        high[place], low[place] = split(second[...] * inverse[place])
    last = apply_terms(sources, (high, low), (left_high, left_low), (right_high, right_low))
    halves(last, kept_ref, sent_ref)
    last_ref[...] = last
    refs = {"w": start.at[0], "u": image, "a": side, "b": own_second}
    refs.update(c=extra.at[0], d=extra.at[1], e=further, f=last_ref)
    row = row_of_sums(MOMENTS[3], refs, inverse.at[0], FIRST_LANE[3], early_row[...])
    row_ref[...] = jnp.broadcast_to(row, row_ref.shape)


def last_kernel(
    total, rows, start, ratio, inverse, own_side, mate_side, own_second, mate_second, own_extra,
    mate_extra, own_further, mate_further, own_last, mate_last, basis_ref, ritz_ref
):
    op = lax.axis_index("op")
    keys = [key for group in MOMENTS for key in group]
    moments = dict(zip(keys, summed(rows, total, len(keys))))
    basis, thetas = all_steps(lambda *key: moments[key], lax.rsqrt)
    half = own_last.shape[0]
    mine = pl.ds(pl.multiple_of(op * half, half), half)
    for place, (sector, side, second, extra, further, last) in enumerate(
        (
            (op, own_side, own_second, own_extra, own_further, own_last),
            (1 - op, mate_side, mate_second, mate_extra, mate_further, mate_last),
        )
    ):
        arrays = {
            ("w", 0): start[place, mine],
            ("u", 1): ratio[place, mine],
            ("a", 0): side[mine],
            ("b", 0): second[mine],
            ("c", 0): extra[0],
            ("d", 0): extra[1],
            ("e", 0): further[...],
            ("f", 0): last[...],
        }
        for i in range(ITERS):
            basis_ref[i, sector] = combined(basis[i + 1], arrays, inverse[place, mine])
    for position, value in enumerate(thetas):
        ritz_ref[position] = value[0, 0]


def one_sector_body(wave_start, left_blocks, right_blocks, term_shifts, preconditioner):
    op = lax.axis_index("op")
    chips = lax.axis_size("sector")
    devices = 2 * chips
    rows, columns = wave_start.shape[1:]
    half = rows // 2
    terms = 2 * left_blocks.shape[0]
    total = float(devices * rows * columns)
    swap = [(i, i ^ 1) for i in range(devices)]
    across = [(i, i + 1) for i in range(1, devices - 1, 2)]
    across = across + [(j, i) for i, j in across]

    def mate(values):
        return lax.ppermute(values, AXES, swap)

    def facing(values):
        return lax.ppermute(values, AXES, across)

    def own_sector(values):
        return lax.dynamic_index_in_dim(values, op, 0, keepdims=False)

    def exchanged(row):
        spread = row.reshape(devices, 1, LANES)
        return lax.all_to_all(spread, AXES, 0, 0, tiled=True).reshape(devices, LANES)

    vmem = pl.BlockSpec(memory_space=pltpu.VMEM)
    smem = pl.BlockSpec(memory_space=pltpu.SMEM)

    def call(
        kernel, operands, shapes, scalars=0, out_scalars=0, scratch=True, more_scratch=()
    ):
        return pl.pallas_call(
            kernel,
            out_shape=[jax.ShapeDtypeStruct(shape, kind) for shape, kind in shapes],
            in_specs=[smem] * scalars + [vmem] * (len(operands) - scalars),
            out_specs=[vmem] * (len(shapes) - out_scalars) + [smem] * out_scalars,
            scratch_shapes=[pltpu.VMEM((3, rows, columns), jnp.bfloat16)] * (2 if scratch else 0)
            + list(more_scratch),
            compiler_params=pltpu.CompilerParams(vmem_limit_bytes=16 * 2**20),
        )(*operands)

    block = (rows, columns)
    f32, bf16 = jnp.float32, jnp.bfloat16
    row_shape = ((devices, LANES), f32)

    half_shape = left_blocks.shape[:1] + left_blocks.shape[2:]
    own_wave, own_preconditioner, sent_left, sent_right = pl.pallas_call(
        picking_kernel,
        out_shape=[jax.ShapeDtypeStruct(shape, f32) for shape in [block] * 2 + [half_shape] * 2],
        in_specs=[pl.BlockSpec(memory_space=pl.ANY)] * 4,
        out_specs=[vmem] * 4,
        scratch_shapes=[pltpu.SemaphoreType.DMA((2 + terms,))],
        compiler_params=pltpu.CompilerParams(vmem_limit_bytes=52 * 2**20),
    )(wave_start, preconditioner, left_blocks, right_blocks)
    facing_wave = facing(own_wave)
    mate_left, mate_right = mate(sent_left), mate(sent_right)
    mate_shifts, own_preconditioner = lax.optimization_barrier(
        (mate(term_shifts), own_preconditioner)
    )
    facing_preconditioner = facing(own_preconditioner)
    shifts = (term_shifts, mate_shifts)

    split_shape = (terms,) + left_blocks.shape[2:]
    blocks = call(
        splitting_kernel,
        (left_blocks, right_blocks, mate_left, mate_right),
        [(split_shape, bf16)] * 4,
        scratch=False,
    )

    def around(values):
        return (values, mate(values), facing(values))

    image, start = call(
        first_kernel,
        (*shifts, wave_start, facing_wave, *blocks),
        [(block, f32), ((3,) + block, f32)],
        scalars=2,
    )
    images = around(image)
    side, inverse = call(
        side_kernel,
        (*shifts, start, preconditioner, facing_preconditioner, *blocks),
        [(block, f32), ((3,) + block, f32)],
        scalars=2,
    )
    sides = around(side)
    (early_row,) = call(
        moments_kernel, (start, image, side, inverse), [((1, LANES), f32)], scratch=False
    )
    second, ratio = call(
        second_kernel,
        (*shifts, *images, inverse, early_row, *blocks),
        [(block, f32), ((3,) + block, f32)],
        scalars=2,
    )
    seconds = around(second)
    half_block = (half, columns)
    extra, kept_extra, sent_extra, early_row = call(
        extra_kernel,
        (*shifts, start, ratio, inverse, image, side, second, early_row, *blocks),
        [((2,) + block, f32)] + [((2,) + half_block, f32)] * 2 + [((1, LANES), f32)],
        scalars=2,
    )
    mate_extra = mate(sent_extra)
    further, kept_further, sent_further, early_row = call(
        further_kernel,
        (*shifts, start, inverse, image, *sides, second, extra, early_row, *blocks),
        [(block, f32)] + [(half_block, f32)] * 2 + [((1, LANES), f32)],
        scalars=2,
    )
    mate_further = mate(sent_further)
    kept, sent, row = call(
        third_kernel,
        (*shifts, start, inverse, image, side, *seconds, extra, further, early_row, *blocks),
        [(half_block, f32)] * 2 + [row_shape],
        scalars=2,
        more_scratch=[pltpu.VMEM(block, f32)],
    )
    mate_last = mate(sent)
    row, mate_extra, mate_further = lax.optimization_barrier((row, mate_extra, mate_further))
    basis, ritz = call(
        functools.partial(last_kernel, total),
        (exchanged(row), start, ratio, inverse, *sides[:2], *seconds[:2], kept_extra, mate_extra,
         kept_further, mate_further, kept, mate_last),
        [((ITERS, 2) + half_block, f32), ((ITERS,), f32)],
        out_scalars=1,
        scratch=False,
    )
    return (basis, ritz)


def with_halo(cells, sides, width):
    for axis, dim in sides:
        count = lax.axis_size(axis)
        ends = count - 1
        head = lax.slice_in_dim(cells, 0, width, axis=dim)
        tail = lax.slice_in_dim(cells, cells.shape[dim] - width, cells.shape[dim], axis=dim)
        cells = jnp.concatenate(
            [
                lax.ppermute(tail, axis, [(i, (i + 1) % count) for i in range(ends)]),
                cells,
                lax.ppermute(head, axis, [((i + 1) % count, i) for i in range(ends)]),
            ],
            axis=dim,
        )
    return cells


def split_terms_body(wave_start, left_blocks, right_blocks, term_shifts, preconditioner):
    highest = lax.Precision.HIGHEST
    width = wave_start.shape[1]
    row_count = width // lax.axis_size("op")
    first_row = lax.axis_index("op") * row_count
    total = float(wave_start.shape[0] * lax.axis_size("sector") * width * wave_start.shape[2])

    def portion(values):
        return lax.dynamic_slice_in_dim(values, first_row, row_count, axis=values.ndim - 2)

    start_sum = total_sum(jnp.sum(jnp.square(portion(wave_start)))[None])[0] / total
    basis = [wave_start * lax.rsqrt(start_sum + EPSILON)]
    ritz = []
    for _ in range(ITERS):
        latest = basis[-1]
        padded = with_halo(latest, (("sector", 0),), 1)
        shift = term_shifts[:, None, None, None]
        source = jnp.where(
            shift == 1,
            padded[None, :-2],
            jnp.where(shift == -1, padded[None, 2:], padded[None, 1:-1]),
        )
        inner = jnp.einsum("ksab,ksbc->ksac", left_blocks, source, precision=highest)
        image = lax.psum(jnp.einsum("ksac,kscd->sad", inner, right_blocks, precision=highest), "op")
        inverse = 1.0 / preconditioner
        pieces = products([portion(member) for member in basis], portion(image), portion(inverse))
        theta, correlations, scale = coefficients(
            total_sum(jnp.stack(pieces)), total, len(basis)
        )
        ortho = (image - theta * latest) * inverse
        for position, member in enumerate(basis):
            ortho = ortho - correlations[position] * member
        basis.append(ortho * scale)
        ritz.append(theta)
    output = jnp.stack([portion(member) for member in basis[1:]])
    return (output, jnp.stack(ritz))


def solution(mesh):
    placed = (
        P("sector", None, None),
        P("op", "sector", None, None),
        P("op", "sector", None, None),
        P("op"),
        P("sector", None, None),
    )

    def body(wave_start, *operands):
        one_each = mesh.shape["op"] == 2 and wave_start.shape[0] == 2
        return (one_sector_body if one_each else split_terms_body)(wave_start, *operands)

    return jax.shard_map(
        body,
        mesh=mesh,
        in_specs=placed,
        out_specs=(P(None, "sector", "op", None), P()),
        check_vma=False,
    )
```

```python
import functools

import jax
import jax.numpy as jnp
from jax import lax
from jax.experimental import pallas as pl
from jax.experimental.pallas import tpu as pltpu
from jax.sharding import PartitionSpec as P

ITERS = 3


EPSILON = 1e-06

AXES = ("sector", "op")

LANES = 128


def total_sum(values):
    devices = lax.axis_size("sector") * lax.axis_size("op")
    row = jnp.pad(values, (0, LANES - values.shape[0]))
    rows = lax.all_to_all(jnp.broadcast_to(row, (devices, LANES)), AXES, 0, 0, tiled=True)
    return jnp.sum(rows, axis=0)[: values.shape[0]]


def coefficients(sums, total, count):
    sums = sums / total
    theta = sums[0]
    correlations = sums[4 : 4 + count] - theta * sums[4 + count : 4 + 2 * count]
    length = (
        sums[1]
        - 2.0 * theta * sums[2]
        + theta * theta * sums[3]
        - jnp.sum(jnp.square(correlations))
    )
    return theta, correlations, lax.rsqrt(length + EPSILON)


def products(members, image, inverse):
    latest = members[-1]
    ratio_image = image * inverse
    ratio_latest = latest * inverse
    pieces = [
        jnp.sum(latest * image),
        jnp.sum(ratio_image * ratio_image),
        jnp.sum(ratio_image * ratio_latest),
        jnp.sum(ratio_latest * ratio_latest),
    ]
    pieces = pieces + [jnp.sum(member * ratio_image) for member in members]
    pieces = pieces + [jnp.sum(member * ratio_latest) for member in members]
    return pieces


def split(values):
    high = values.astype(jnp.bfloat16)
    return high, (values - high.astype(jnp.float32)).astype(jnp.bfloat16)


def dot_split(lhs_high, lhs_low, rhs_high, rhs_low):
    dot = functools.partial(jnp.dot, preferred_element_type=jnp.float32)
    rows = lhs_high.shape[0]
    both = dot(jnp.concatenate([lhs_high, lhs_low], axis=0), rhs_high)
    return both[:rows] + (both[rows:] + dot(lhs_high, rhs_low))


def apply_terms(sources, vectors, left, right):
    left_high, left_low = left
    right_high, right_low = right
    vector_high, vector_low = vectors
    inners = [
        split(
            dot_split(left_high[term], left_low[term], vector_high[source], vector_low[source])
        )
        for term, source in enumerate(sources)
    ]
    image = None
    for term, inner in enumerate(inners):
        part = dot_split(*inner, right_high[term], right_low[term])
        image = part if image is None else image + part
    return image


def term_sources(own_shifts, mate_shifts):
    toward_mate = jnp.where(lax.axis_index("op") == 0, -1, 1)
    shifts = [refs[i] for refs in (own_shifts, mate_shifts) for i in range(refs.shape[0])]
    return [
        jnp.where(shift == 0, 0, jnp.where(shift == toward_mate, 1, 2)) for shift in shifts
    ]


CHUNK = 16


def row_of_sums(moments, refs, inverse, first=0, row=None):
    rows, columns = inverse.shape
    lane = lax.broadcasted_iota(jnp.int32, (1, LANES), 1)
    if row is None:
        row = jnp.zeros((1, LANES), jnp.float32)
    pairs = {}
    for x, y, n in moments:
        pairs.setdefault((x, y), []).append(n)
    totals = {}
    for top in range(0, rows, CHUNK):
        here = pl.ds(top, CHUNK)
        powers = [None, inverse[here]]
        while len(powers) <= max(n for _, _, n in moments):
            powers.append(powers[-1] * powers[1])
        for (x, y), orders in pairs.items():
            product = refs[x][here] * refs[y][here]
            for n in orders:
                weighted = product * powers[n] if n else product
                part = jnp.sum(weighted.reshape(-1, 8, columns), axis=0)
                part = sum(part[:, i : i + LANES] for i in range(0, columns, LANES))
                totals[x, y, n] = totals[x, y, n] + part if top else part
    for position, moment in enumerate(moments):
        whole = jnp.sum(totals[moment], axis=(0, 1), keepdims=True)
        row = jnp.where(lane == first + position, whole, row)
    return row


def summed(rows, total, count):
    whole = jnp.sum(rows[...], axis=0, keepdims=True) * (1.0 / total)
    return [jnp.broadcast_to(whole[:, i : i + 1], (8, LANES)) for i in range(count)]


def one_of(value):
    return value[:1, :1]


H_OF = {
    ("w", 0): "u",
    ("w", 1): "a",
    ("u", 1): "b",
    ("w", 2): "c",
    ("u", 2): "d",
    ("a", 1): "e",
    ("b", 1): "f",
}

START_SCALE = 2.0**10
H_SCALE = 2.0**7


def plus(vector, other, factor):
    result = dict(vector)
    for word, value in other.items():
        term = value * factor
        result[word] = result[word] + term if word in result else term
    return result


def times_inverse(vector):
    return {(name, n + 1): value for (name, n), value in vector.items()}


def times_h(vector):
    return {(H_OF[word], 0): value * H_SCALE for word, value in vector.items()}


def inner(one, other, moment):
    result = None
    for (x, n), value in one.items():
        part = None
        for (y, m), factor in other.items():
            term = factor * moment(*sorted((x, y)), n + m)
            part = term if part is None else part + term
        part = value * part
        result = part if result is None else result + part
    return result


def all_steps(moment, inverse_root):
    basis = [{("w", 0): inverse_root(moment("w", "w", 0) + EPSILON * START_SCALE**2)}]
    thetas = []
    for _ in range(ITERS):
        latest = basis[-1]
        image = times_h(latest)
        theta = inner(latest, image, moment)
        correction = times_inverse(plus(image, latest, -theta))
        ortho = correction
        for member in basis:
            ortho = plus(ortho, member, -inner(member, correction, moment))
        scale = inverse_root(inner(ortho, ortho, moment) + EPSILON)
        basis.append({word: value * scale for word, value in ortho.items()})
        thetas.append(theta)
    return basis, thetas


def needed_moments():
    asked = {}

    def moment(x, y, n):
        asked[x, y, n] = True
        return 1.0

    all_steps(moment, lambda value: 1.0)
    stages = ("wua", "bcd", "e", "f")
    groups = [[] for _ in stages]
    for key in asked:
        groups[max(i for i, names in enumerate(stages) if set(key[:2]) & set(names))].append(key)
    return groups


def combined(vector, arrays, inverse):
    words = {name: (n, values) for (name, n), values in arrays.items()}
    result = None
    for n in range(max(n for _, n in vector), -1, -1):
        if result is not None:
            result = result * inverse
        for (name, m), value in vector.items():
            held, values = words[name]
            if m - held == n:
                term = one_of(value) * values
                result = term if result is None else result + term
    return result


MOMENTS = needed_moments()
FIRST_LANE = [sum(len(group) for group in MOMENTS[:i]) for i in range(len(MOMENTS) + 1)]


def inverted(values):
    return jnp.where(values > 0.0, 1.0 / values, 0.0)


def copy_all(pairs, arrived):
    copies = [
        pltpu.make_async_copy(source, target, arrived.at[i])
        for i, (source, target) in enumerate(pairs)
    ]
    for copy in copies:
        copy.start()
    for copy in copies:
        copy.wait()


def picking_kernel(
    wave, preconditioner, left, right, own_wave, own_preconditioner, sent_left, sent_right, arrived
):
    op = lax.axis_index("op")
    pairs = [(wave.at[op], own_wave), (preconditioner.at[op], own_preconditioner)]
    for values, sent in ((left, sent_left), (right, sent_right)):
        for term in range(values.shape[0]):
            pairs.append((values.at[term, 1 - op], sent.at[term]))
    copy_all(pairs, arrived)


def splitting_kernel(
    own_left, own_right, mate_left, mate_right, left_high, left_low, right_high, right_low
):
    op = lax.axis_index("op")
    count = own_left.shape[0]
    for term in range(count):
        left_high[term], left_low[term] = split(own_left[term, op] * (1.0 / H_SCALE))
        right_high[term], right_low[term] = split(own_right[term, op])
        place = count + term
        left_high[place], left_low[place] = split(mate_left[term] * (1.0 / H_SCALE))
        right_high[place], right_low[place] = split(mate_right[term])


def first_kernel(
    own_shifts, mate_shifts, wave, facing_wave, left_high, left_low, right_high, right_low,
    image_ref, start_ref, high, low,
):
    op = lax.axis_index("op")
    sources = term_sources(own_shifts, mate_shifts)
    for place, values in enumerate((wave[op], wave[1 - op], facing_wave[...])):
        start = values * START_SCALE
        start_ref[place] = start
        high[place], low[place] = split(start)
    image_ref[...] = apply_terms(
        sources, (high, low), (left_high, left_low), (right_high, right_low)
    )


def side_kernel(
    own_shifts, mate_shifts, start, preconditioner, facing_preconditioner,
    left_high, left_low, right_high, right_low, side_ref, inverse_ref, high, low,
):
    op = lax.axis_index("op")
    sources = term_sources(own_shifts, mate_shifts)
    divisors = (preconditioner[op], preconditioner[1 - op], facing_preconditioner[...])
    for place in range(3):
        inverse = inverted(divisors[place])
        inverse_ref[place] = inverse
        high[place], low[place] = split(start[place] * inverse)
    side_ref[...] = apply_terms(
        sources, (high, low), (left_high, left_low), (right_high, right_low)
    )


def moments_kernel(start, image, side, inverse, row_ref):
    refs = {"w": start.at[0], "u": image, "a": side}
    row_ref[...] = row_of_sums(MOMENTS[0], refs, inverse.at[0])


def second_kernel(
    own_shifts, mate_shifts, own_image, mate_image, facing_image, inverse, _,
    left_high, left_low, right_high, right_low, image_ref, ratio_ref, high, low,
):
    sources = term_sources(own_shifts, mate_shifts)
    for place, image in enumerate((own_image, mate_image, facing_image)):
        ratio = image[...] * inverse[place]
        ratio_ref[place] = ratio
        high[place], low[place] = split(ratio)
    image_ref[...] = apply_terms(
        sources, (high, low), (left_high, left_low), (right_high, right_low)
    )


def halves(image, kept_ref, sent_ref):
    op = lax.axis_index("op")
    half = kept_ref.shape[0]
    kept_ref[...] = jnp.where(op == 0, image[:half], image[half:])
    sent_ref[...] = jnp.where(op == 0, image[half:], image[:half])


def extra_kernel(
    own_shifts, mate_shifts, start, ratio, inverse, image, side, second, early_row,
    left_high, left_low, right_high, right_low, extra_ref, kept_ref, sent_ref, row_ref, high, low,
):
    sources = term_sources(own_shifts, mate_shifts)
    refs = {"w": start.at[0], "u": image, "a": side, "b": second}
    for i, name in enumerate("cd"):
        for place in range(3):
            once = start[place] * inverse[place] if name == "c" else ratio[place]
            high[place], low[place] = split(once * inverse[place])
        extra = apply_terms(sources, (high, low), (left_high, left_low), (right_high, right_low))
        refs[name] = extra_ref.at[i]
        extra_ref[i] = extra
        halves(extra, kept_ref.at[i], sent_ref.at[i])
    row_ref[...] = row_of_sums(MOMENTS[1], refs, inverse.at[0], FIRST_LANE[1], early_row[...])


def further_kernel(
    own_shifts, mate_shifts, start, inverse, image, own_side, mate_side, facing_side, second,
    extra, early_row, left_high, left_low, right_high, right_low, further_ref, kept_ref, sent_ref,
    row_ref, high, low,
):
    sources = term_sources(own_shifts, mate_shifts)
    for place, side in enumerate((own_side, mate_side, facing_side)):
        high[place], low[place] = split(side[...] * inverse[place])
    further = apply_terms(sources, (high, low), (left_high, left_low), (right_high, right_low))
    further_ref[...] = further
    halves(further, kept_ref, sent_ref)
    refs = {"w": start.at[0], "u": image, "a": own_side, "b": second}
    refs.update(c=extra.at[0], d=extra.at[1], e=further_ref)
    row_ref[...] = row_of_sums(MOMENTS[2], refs, inverse.at[0], FIRST_LANE[2], early_row[...])


def third_kernel(
    own_shifts, mate_shifts, start, inverse, image, side, own_second, mate_second, facing_second,
    extra, further, early_row, left_high, left_low, right_high, right_low,
    kept_ref, sent_ref, row_ref, high, low, last_ref,
):
    sources = term_sources(own_shifts, mate_shifts)
    for place, second in enumerate((own_second, mate_second, facing_second)):
        high[place], low[place] = split(second[...] * inverse[place])
    last = apply_terms(sources, (high, low), (left_high, left_low), (right_high, right_low))
    last_ref[...] = last
    op, half = lax.axis_index("op"), kept_ref.shape[0]
    kept_ref[...] = last_ref[pl.ds(pl.multiple_of(op * half, half), half)]
    sent_ref[...] = last_ref[pl.ds(pl.multiple_of((1 - op) * half, half), half)]
    refs = {"w": start.at[0], "u": image, "a": side, "b": own_second}
    refs.update(c=extra.at[0], d=extra.at[1], e=further, f=last_ref)
    row = row_of_sums(MOMENTS[3], refs, inverse.at[0], FIRST_LANE[3], early_row[...])
    row_ref[...] = jnp.broadcast_to(row, row_ref.shape)


def last_kernel(
    total, rows, start, ratio, inverse, own_side, mate_side, own_second, mate_second, own_extra,
    mate_extra, own_further, mate_further, own_last, mate_last, basis_ref, ritz_ref
):
    op = lax.axis_index("op")
    keys = [key for group in MOMENTS for key in group]
    moments = dict(zip(keys, summed(rows, total, len(keys))))
    basis, thetas = all_steps(lambda *key: moments[key], lax.rsqrt)
    half = own_last.shape[0]
    mine = pl.ds(pl.multiple_of(op * half, half), half)
    for place, (sector, side, second, extra, further, last) in enumerate(
        (
            (op, own_side, own_second, own_extra, own_further, own_last),
            (1 - op, mate_side, mate_second, mate_extra, mate_further, mate_last),
        )
    ):
        arrays = {
            ("w", 0): start[place, mine],
            ("u", 1): ratio[place, mine],
            ("a", 0): side[mine],
            ("b", 0): second[mine],
            ("c", 0): extra[0],
            ("d", 0): extra[1],
            ("e", 0): further[...],
            ("f", 0): last[...],
        }
        for i in range(ITERS):
            basis_ref[i, sector] = combined(basis[i + 1], arrays, inverse[place, mine])
    for position, value in enumerate(thetas):
        ritz_ref[position] = value[0, 0]


def one_sector_body(wave_start, left_blocks, right_blocks, term_shifts, preconditioner):
    op = lax.axis_index("op")
    chips = lax.axis_size("sector")
    devices = 2 * chips
    rows, columns = wave_start.shape[1:]
    half = rows // 2
    terms = 2 * left_blocks.shape[0]
    total = float(devices * rows * columns)
    swap = [(i, i ^ 1) for i in range(devices)]
    across = [(i, i + 1) for i in range(1, devices - 1, 2)]
    across = across + [(j, i) for i, j in across]

    def mate(values):
        return lax.ppermute(values, AXES, swap)

    def facing(values):
        return lax.ppermute(values, AXES, across)

    def own_sector(values):
        return lax.dynamic_index_in_dim(values, op, 0, keepdims=False)

    def exchanged(row):
        spread = row.reshape(devices, 1, LANES)
        return lax.all_to_all(spread, AXES, 0, 0, tiled=True).reshape(devices, LANES)

    vmem = pl.BlockSpec(memory_space=pltpu.VMEM)
    smem = pl.BlockSpec(memory_space=pltpu.SMEM)

    def call(
        kernel, operands, shapes, scalars=0, out_scalars=0, scratch=True, more_scratch=()
    ):
        return pl.pallas_call(
            kernel,
            out_shape=[jax.ShapeDtypeStruct(shape, kind) for shape, kind in shapes],
            in_specs=[smem] * scalars + [vmem] * (len(operands) - scalars),
            out_specs=[vmem] * (len(shapes) - out_scalars) + [smem] * out_scalars,
            scratch_shapes=[pltpu.VMEM((3, rows, columns), jnp.bfloat16)] * (2 if scratch else 0)
            + list(more_scratch),
            compiler_params=pltpu.CompilerParams(vmem_limit_bytes=16 * 2**20),
        )(*operands)

    block = (rows, columns)
    f32, bf16 = jnp.float32, jnp.bfloat16
    row_shape = ((devices, LANES), f32)

    half_shape = left_blocks.shape[:1] + left_blocks.shape[2:]
    own_wave, own_preconditioner, sent_left, sent_right = pl.pallas_call(
        picking_kernel,
        out_shape=[jax.ShapeDtypeStruct(shape, f32) for shape in [block] * 2 + [half_shape] * 2],
        in_specs=[pl.BlockSpec(memory_space=pl.ANY)] * 4,
        out_specs=[vmem] * 4,
        scratch_shapes=[pltpu.SemaphoreType.DMA((2 + terms,))],
        compiler_params=pltpu.CompilerParams(vmem_limit_bytes=52 * 2**20),
    )(wave_start, preconditioner, left_blocks, right_blocks)
    facing_wave = facing(own_wave)
    mate_left, mate_right = mate(sent_left), mate(sent_right)
    mate_shifts, own_preconditioner = lax.optimization_barrier(
        (mate(term_shifts), own_preconditioner)
    )
    facing_preconditioner = facing(own_preconditioner)
    shifts = (term_shifts, mate_shifts)

    split_shape = (terms,) + left_blocks.shape[2:]
    blocks = call(
        splitting_kernel,
        (left_blocks, right_blocks, mate_left, mate_right),
        [(split_shape, bf16)] * 4,
        scratch=False,
    )

    def around(values):
        return (values, mate(values), facing(values))

    image, start = call(
        first_kernel,
        (*shifts, wave_start, facing_wave, *blocks),
        [(block, f32), ((3,) + block, f32)],
        scalars=2,
    )
    images = around(image)
    side, inverse = call(
        side_kernel,
        (*shifts, start, preconditioner, facing_preconditioner, *blocks),
        [(block, f32), ((3,) + block, f32)],
        scalars=2,
    )
    (early_row,) = call(
        moments_kernel, (start, image, side, inverse), [((1, LANES), f32)], scratch=False
    )
    side, early_row = lax.optimization_barrier((side, early_row))
    sides = around(side)
    second, ratio = call(
        second_kernel,
        (*shifts, *images, inverse, early_row, *blocks),
        [(block, f32), ((3,) + block, f32)],
        scalars=2,
    )
    seconds = around(second)
    half_block = (half, columns)
    extra, kept_extra, sent_extra, early_row = call(
        extra_kernel,
        (*shifts, start, ratio, inverse, image, side, second, early_row, *blocks),
        [((2,) + block, f32)] + [((2,) + half_block, f32)] * 2 + [((1, LANES), f32)],
        scalars=2,
    )
    mate_extra = mate(sent_extra)
    further, kept_further, sent_further, early_row = call(
        further_kernel,
        (*shifts, start, inverse, image, *sides, second, extra, early_row, *blocks),
        [(block, f32)] + [(half_block, f32)] * 2 + [((1, LANES), f32)],
        scalars=2,
    )
    mate_further = mate(sent_further)
    kept, sent, row = call(
        third_kernel,
        (*shifts, start, inverse, image, side, *seconds, extra, further, early_row, *blocks),
        [(half_block, f32)] * 2 + [row_shape],
        scalars=2,
        more_scratch=[pltpu.VMEM(block, f32)],
    )
    mate_last = mate(sent)
    row, mate_extra, mate_further = lax.optimization_barrier((row, mate_extra, mate_further))
    basis, ritz = call(
        functools.partial(last_kernel, total),
        (exchanged(row), start, ratio, inverse, *sides[:2], *seconds[:2], kept_extra, mate_extra,
         kept_further, mate_further, kept, mate_last),
        [((ITERS, 2) + half_block, f32), ((ITERS,), f32)],
        out_scalars=1,
        scratch=False,
    )
    return (basis, ritz)


def with_halo(cells, sides, width):
    for axis, dim in sides:
        count = lax.axis_size(axis)
        ends = count - 1
        head = lax.slice_in_dim(cells, 0, width, axis=dim)
        tail = lax.slice_in_dim(cells, cells.shape[dim] - width, cells.shape[dim], axis=dim)
        cells = jnp.concatenate(
            [
                lax.ppermute(tail, axis, [(i, (i + 1) % count) for i in range(ends)]),
                cells,
                lax.ppermute(head, axis, [((i + 1) % count, i) for i in range(ends)]),
            ],
            axis=dim,
        )
    return cells


def split_terms_body(wave_start, left_blocks, right_blocks, term_shifts, preconditioner):
    highest = lax.Precision.HIGHEST
    width = wave_start.shape[1]
    row_count = width // lax.axis_size("op")
    first_row = lax.axis_index("op") * row_count
    total = float(wave_start.shape[0] * lax.axis_size("sector") * width * wave_start.shape[2])

    def portion(values):
        return lax.dynamic_slice_in_dim(values, first_row, row_count, axis=values.ndim - 2)

    start_sum = total_sum(jnp.sum(jnp.square(portion(wave_start)))[None])[0] / total
    basis = [wave_start * lax.rsqrt(start_sum + EPSILON)]
    ritz = []
    for _ in range(ITERS):
        latest = basis[-1]
        padded = with_halo(latest, (("sector", 0),), 1)
        shift = term_shifts[:, None, None, None]
        source = jnp.where(
            shift == 1,
            padded[None, :-2],
            jnp.where(shift == -1, padded[None, 2:], padded[None, 1:-1]),
        )
        inner = jnp.einsum("ksab,ksbc->ksac", left_blocks, source, precision=highest)
        image = lax.psum(jnp.einsum("ksac,kscd->sad", inner, right_blocks, precision=highest), "op")
        inverse = 1.0 / preconditioner
        pieces = products([portion(member) for member in basis], portion(image), portion(inverse))
        theta, correlations, scale = coefficients(
            total_sum(jnp.stack(pieces)), total, len(basis)
        )
        ortho = (image - theta * latest) * inverse
        for position, member in enumerate(basis):
            ortho = ortho - correlations[position] * member
        basis.append(ortho * scale)
        ritz.append(theta)
    output = jnp.stack([portion(member) for member in basis[1:]])
    return (output, jnp.stack(ritz))


def solution(mesh):
    placed = (
        P("sector", None, None),
        P("op", "sector", None, None),
        P("op", "sector", None, None),
        P("op"),
        P("sector", None, None),
    )

    def body(wave_start, *operands):
        one_each = mesh.shape["op"] == 2 and wave_start.shape[0] == 2
        return (one_sector_body if one_each else split_terms_body)(wave_start, *operands)

    return jax.shard_map(
        body,
        mesh=mesh,
        in_specs=placed,
        out_specs=(P(None, "sector", "op", None), P()),
        check_vma=False,
    )
```

```python
import functools

import jax
import jax.numpy as jnp
from jax import lax
from jax.experimental import pallas as pl
from jax.experimental.pallas import tpu as pltpu
from jax.sharding import PartitionSpec as P

ITERS = 3


EPSILON = 1e-06

AXES = ("sector", "op")

LANES = 128


def total_sum(values):
    devices = lax.axis_size("sector") * lax.axis_size("op")
    row = jnp.pad(values, (0, LANES - values.shape[0]))
    rows = lax.all_to_all(jnp.broadcast_to(row, (devices, LANES)), AXES, 0, 0, tiled=True)
    return jnp.sum(rows, axis=0)[: values.shape[0]]


def coefficients(sums, total, count):
    sums = sums / total
    theta = sums[0]
    correlations = sums[4 : 4 + count] - theta * sums[4 + count : 4 + 2 * count]
    length = (
        sums[1]
        - 2.0 * theta * sums[2]
        + theta * theta * sums[3]
        - jnp.sum(jnp.square(correlations))
    )
    return theta, correlations, lax.rsqrt(length + EPSILON)


def products(members, image, inverse):
    latest = members[-1]
    ratio_image = image * inverse
    ratio_latest = latest * inverse
    pieces = [
        jnp.sum(latest * image),
        jnp.sum(ratio_image * ratio_image),
        jnp.sum(ratio_image * ratio_latest),
        jnp.sum(ratio_latest * ratio_latest),
    ]
    pieces = pieces + [jnp.sum(member * ratio_image) for member in members]
    pieces = pieces + [jnp.sum(member * ratio_latest) for member in members]
    return pieces


def split(values):
    high = values.astype(jnp.bfloat16)
    return high, (values - high.astype(jnp.float32)).astype(jnp.bfloat16)


def dot_split(lhs_high, lhs_low, rhs_high, rhs_low):
    dot = functools.partial(jnp.dot, preferred_element_type=jnp.float32)
    rows = lhs_high.shape[0]
    both = dot(jnp.concatenate([lhs_high, lhs_low], axis=0), rhs_high)
    return both[:rows] + (both[rows:] + dot(lhs_high, rhs_low))


def apply_terms(sources, vectors, left, right):
    left_high, left_low = left
    right_high, right_low = right
    vector_high, vector_low = vectors
    inners = [
        split(
            dot_split(left_high[term], left_low[term], vector_high[source], vector_low[source])
        )
        for term, source in enumerate(sources)
    ]
    image = None
    for term, inner in enumerate(inners):
        part = dot_split(*inner, right_high[term], right_low[term])
        image = part if image is None else image + part
    return image


def term_sources(own_shifts, mate_shifts):
    toward_mate = jnp.where(lax.axis_index("op") == 0, -1, 1)
    shifts = [refs[i] for refs in (own_shifts, mate_shifts) for i in range(refs.shape[0])]
    return [
        jnp.where(shift == 0, 0, jnp.where(shift == toward_mate, 1, 2)) for shift in shifts
    ]


CHUNK = 32


def row_of_sums(moments, refs, inverse, first=0, row=None):
    rows, columns = inverse.shape
    lane = lax.broadcasted_iota(jnp.int32, (1, LANES), 1)
    if row is None:
        row = jnp.zeros((1, LANES), jnp.float32)
    pairs = {}
    for x, y, n in moments:
        pairs.setdefault((x, y), []).append(n)
    totals = {}
    for top in range(0, rows, CHUNK):
        here = pl.ds(top, CHUNK)
        powers = [None, inverse[here]]
        while len(powers) <= max(n for _, _, n in moments):
            powers.append(powers[-1] * powers[1])
        for (x, y), orders in pairs.items():
            product = refs[x][here] * refs[y][here]
            for n in orders:
                weighted = product * powers[n] if n else product
                part = jnp.sum(weighted.reshape(-1, 8, columns), axis=0)
                part = sum(part[:, i : i + LANES] for i in range(0, columns, LANES))
                totals[x, y, n] = totals[x, y, n] + part if top else part
    for position, moment in enumerate(moments):
        whole = jnp.sum(totals[moment], axis=(0, 1), keepdims=True)
        row = jnp.where(lane == first + position, whole, row)
    return row


def summed(rows, total, count):
    whole = jnp.sum(rows[...], axis=0, keepdims=True) * (1.0 / total)
    return [jnp.broadcast_to(whole[:, i : i + 1], (8, LANES)) for i in range(count)]


def one_of(value):
    return value[:1, :1]


H_OF = {
    ("w", 0): "u",
    ("w", 1): "a",
    ("u", 1): "b",
    ("w", 2): "c",
    ("u", 2): "d",
    ("a", 1): "e",
    ("b", 1): "f",
}

START_SCALE = 2.0**10
H_SCALE = 2.0**7


def plus(vector, other, factor):
    result = dict(vector)
    for word, value in other.items():
        term = value * factor
        result[word] = result[word] + term if word in result else term
    return result


def times_inverse(vector):
    return {(name, n + 1): value for (name, n), value in vector.items()}


def times_h(vector):
    return {(H_OF[word], 0): value * H_SCALE for word, value in vector.items()}


def inner(one, other, moment):
    result = None
    for (x, n), value in one.items():
        part = None
        for (y, m), factor in other.items():
            term = factor * moment(*sorted((x, y)), n + m)
            part = term if part is None else part + term
        part = value * part
        result = part if result is None else result + part
    return result


def all_steps(moment, inverse_root):
    basis = [{("w", 0): inverse_root(moment("w", "w", 0) + EPSILON * START_SCALE**2)}]
    thetas = []
    for _ in range(ITERS):
        latest = basis[-1]
        image = times_h(latest)
        theta = inner(latest, image, moment)
        correction = times_inverse(plus(image, latest, -theta))
        ortho = correction
        for member in basis:
            ortho = plus(ortho, member, -inner(member, correction, moment))
        scale = inverse_root(inner(ortho, ortho, moment) + EPSILON)
        basis.append({word: value * scale for word, value in ortho.items()})
        thetas.append(theta)
    return basis, thetas


def needed_moments():
    asked = {}

    def moment(x, y, n):
        asked[x, y, n] = True
        return 1.0

    all_steps(moment, lambda value: 1.0)
    stages = ("wua", "bcd", "e", "f")
    groups = [[] for _ in stages]
    for key in asked:
        groups[max(i for i, names in enumerate(stages) if set(key[:2]) & set(names))].append(key)
    return groups


def combined(vector, arrays, inverse):
    words = {name: (n, values) for (name, n), values in arrays.items()}
    result = None
    for n in range(max(n for _, n in vector), -1, -1):
        if result is not None:
            result = result * inverse
        for (name, m), value in vector.items():
            held, values = words[name]
            if m - held == n:
                term = one_of(value) * values
                result = term if result is None else result + term
    return result


MOMENTS = needed_moments()
FIRST_LANE = [sum(len(group) for group in MOMENTS[:i]) for i in range(len(MOMENTS) + 1)]


def inverted(values):
    return jnp.where(values > 0.0, 1.0 / values, 0.0)


def copy_all(pairs, arrived):
    copies = [
        pltpu.make_async_copy(source, target, arrived.at[i])
        for i, (source, target) in enumerate(pairs)
    ]
    for copy in copies:
        copy.start()
    for copy in copies:
        copy.wait()


def picking_kernel(
    wave, preconditioner, left, right, own_wave, own_preconditioner, sent_left, sent_right, arrived
):
    op = lax.axis_index("op")
    pairs = [(wave.at[op], own_wave), (preconditioner.at[op], own_preconditioner)]
    for values, sent in ((left, sent_left), (right, sent_right)):
        for term in range(values.shape[0]):
            pairs.append((values.at[term, 1 - op], sent.at[term]))
    copy_all(pairs, arrived)


def splitting_kernel(
    own_left, own_right, mate_left, mate_right, left_high, left_low, right_high, right_low
):
    op = lax.axis_index("op")
    count = own_left.shape[0]
    for term in range(count):
        left_high[term], left_low[term] = split(own_left[term, op] * (1.0 / H_SCALE))
        right_high[term], right_low[term] = split(own_right[term, op])
        place = count + term
        left_high[place], left_low[place] = split(mate_left[term] * (1.0 / H_SCALE))
        right_high[place], right_low[place] = split(mate_right[term])


def first_kernel(
    own_shifts, mate_shifts, wave, facing_wave, left_high, left_low, right_high, right_low,
    image_ref, start_ref, high, low,
):
    op = lax.axis_index("op")
    sources = term_sources(own_shifts, mate_shifts)
    for place, values in enumerate((wave[op], wave[1 - op], facing_wave[...])):
        start = values * START_SCALE
        start_ref[place] = start
        high[place], low[place] = split(start)
    image_ref[...] = apply_terms(
        sources, (high, low), (left_high, left_low), (right_high, right_low)
    )


def side_kernel(
    own_shifts, mate_shifts, start, preconditioner, facing_preconditioner,
    left_high, left_low, right_high, right_low, side_ref, inverse_ref, high, low,
):
    op = lax.axis_index("op")
    sources = term_sources(own_shifts, mate_shifts)
    divisors = (preconditioner[op], preconditioner[1 - op], facing_preconditioner[...])
    for place in range(3):
        inverse = inverted(divisors[place])
        inverse_ref[place] = inverse
        high[place], low[place] = split(start[place] * inverse)
    side_ref[...] = apply_terms(
        sources, (high, low), (left_high, left_low), (right_high, right_low)
    )


def moments_kernel(start, image, side, inverse, row_ref):
    refs = {"w": start.at[0], "u": image, "a": side}
    row_ref[...] = row_of_sums(MOMENTS[0], refs, inverse.at[0])


def second_kernel(
    own_shifts, mate_shifts, own_image, mate_image, facing_image, inverse, _,
    left_high, left_low, right_high, right_low, image_ref, ratio_ref, high, low,
):
    sources = term_sources(own_shifts, mate_shifts)
    for place, image in enumerate((own_image, mate_image, facing_image)):
        ratio = image[...] * inverse[place]
        ratio_ref[place] = ratio
        high[place], low[place] = split(ratio)
    image_ref[...] = apply_terms(
        sources, (high, low), (left_high, left_low), (right_high, right_low)
    )


def halves(image, kept_ref, sent_ref):
    op = lax.axis_index("op")
    half = kept_ref.shape[0]
    kept_ref[...] = jnp.where(op == 0, image[:half], image[half:])
    sent_ref[...] = jnp.where(op == 0, image[half:], image[:half])


def extra_kernel(
    own_shifts, mate_shifts, start, ratio, inverse, image, side, second, early_row,
    left_high, left_low, right_high, right_low, extra_ref, kept_ref, sent_ref, row_ref, high, low,
):
    sources = term_sources(own_shifts, mate_shifts)
    refs = {"w": start.at[0], "u": image, "a": side, "b": second}
    for i, name in enumerate("cd"):
        for place in range(3):
            once = start[place] * inverse[place] if name == "c" else ratio[place]
            high[place], low[place] = split(once * inverse[place])
        extra = apply_terms(sources, (high, low), (left_high, left_low), (right_high, right_low))
        refs[name] = extra_ref.at[i]
        extra_ref[i] = extra
        halves(extra, kept_ref.at[i], sent_ref.at[i])
    row_ref[...] = row_of_sums(MOMENTS[1], refs, inverse.at[0], FIRST_LANE[1], early_row[...])


def further_kernel(
    own_shifts, mate_shifts, start, inverse, image, own_side, mate_side, facing_side, second,
    extra, early_row, left_high, left_low, right_high, right_low, further_ref, kept_ref, sent_ref,
    row_ref, high, low,
):
    sources = term_sources(own_shifts, mate_shifts)
    for place, side in enumerate((own_side, mate_side, facing_side)):
        high[place], low[place] = split(side[...] * inverse[place])
    further = apply_terms(sources, (high, low), (left_high, left_low), (right_high, right_low))
    further_ref[...] = further
    halves(further, kept_ref, sent_ref)
    refs = {"w": start.at[0], "u": image, "a": own_side, "b": second}
    refs.update(c=extra.at[0], d=extra.at[1], e=further_ref)
    row_ref[...] = row_of_sums(MOMENTS[2], refs, inverse.at[0], FIRST_LANE[2], early_row[...])


def third_kernel(
    own_shifts, mate_shifts, start, inverse, image, side, own_second, mate_second, facing_second,
    extra, further, early_row, left_high, left_low, right_high, right_low,
    kept_ref, sent_ref, row_ref, high, low, last_ref,
):
    sources = term_sources(own_shifts, mate_shifts)
    for place, second in enumerate((own_second, mate_second, facing_second)):
        high[place], low[place] = split(second[...] * inverse[place])
    last = apply_terms(sources, (high, low), (left_high, left_low), (right_high, right_low))
    halves(last, kept_ref, sent_ref)
    last_ref[...] = last
    refs = {"w": start.at[0], "u": image, "a": side, "b": own_second}
    refs.update(c=extra.at[0], d=extra.at[1], e=further, f=last_ref)
    row = row_of_sums(MOMENTS[3], refs, inverse.at[0], FIRST_LANE[3], early_row[...])
    row_ref[...] = jnp.broadcast_to(row, row_ref.shape)


def last_kernel(
    total, rows, start, ratio, inverse, own_side, mate_side, own_second, mate_second, own_extra,
    mate_extra, own_further, mate_further, own_last, mate_last, basis_ref, ritz_ref
):
    op = lax.axis_index("op")
    keys = [key for group in MOMENTS for key in group]
    moments = dict(zip(keys, summed(rows, total, len(keys))))
    basis, thetas = all_steps(lambda *key: moments[key], lax.rsqrt)
    half = own_last.shape[0]
    mine = pl.ds(pl.multiple_of(op * half, half), half)
    for place, (sector, side, second, extra, further, last) in enumerate(
        (
            (op, own_side, own_second, own_extra, own_further, own_last),
            (1 - op, mate_side, mate_second, mate_extra, mate_further, mate_last),
        )
    ):
        arrays = {
            ("w", 0): start[place, mine],
            ("u", 1): ratio[place, mine],
            ("a", 0): side[mine],
            ("b", 0): second[mine],
            ("c", 0): extra[0],
            ("d", 0): extra[1],
            ("e", 0): further[...],
            ("f", 0): last[...],
        }
        for i in range(ITERS):
            basis_ref[i, sector] = combined(basis[i + 1], arrays, inverse[place, mine])
    for position, value in enumerate(thetas):
        ritz_ref[position] = value[0, 0]


def one_sector_body(wave_start, left_blocks, right_blocks, term_shifts, preconditioner):
    op = lax.axis_index("op")
    chips = lax.axis_size("sector")
    devices = 2 * chips
    rows, columns = wave_start.shape[1:]
    half = rows // 2
    terms = 2 * left_blocks.shape[0]
    total = float(devices * rows * columns)
    swap = [(i, i ^ 1) for i in range(devices)]
    across = [(i, i + 1) for i in range(1, devices - 1, 2)]
    across = across + [(j, i) for i, j in across]

    def mate(values):
        return lax.ppermute(values, AXES, swap)

    def facing(values):
        return lax.ppermute(values, AXES, across)

    def own_sector(values):
        return lax.dynamic_index_in_dim(values, op, 0, keepdims=False)

    def exchanged(row):
        spread = row.reshape(devices, 1, LANES)
        return lax.all_to_all(spread, AXES, 0, 0, tiled=True).reshape(devices, LANES)

    vmem = pl.BlockSpec(memory_space=pltpu.VMEM)
    smem = pl.BlockSpec(memory_space=pltpu.SMEM)

    def call(
        kernel, operands, shapes, scalars=0, out_scalars=0, scratch=True, more_scratch=()
    ):
        return pl.pallas_call(
            kernel,
            out_shape=[jax.ShapeDtypeStruct(shape, kind) for shape, kind in shapes],
            in_specs=[smem] * scalars + [vmem] * (len(operands) - scalars),
            out_specs=[vmem] * (len(shapes) - out_scalars) + [smem] * out_scalars,
            scratch_shapes=[pltpu.VMEM((3, rows, columns), jnp.bfloat16)] * (2 if scratch else 0)
            + list(more_scratch),
            compiler_params=pltpu.CompilerParams(vmem_limit_bytes=16 * 2**20),
        )(*operands)

    block = (rows, columns)
    f32, bf16 = jnp.float32, jnp.bfloat16
    row_shape = ((devices, LANES), f32)

    half_shape = left_blocks.shape[:1] + left_blocks.shape[2:]
    own_wave, own_preconditioner, sent_left, sent_right = pl.pallas_call(
        picking_kernel,
        out_shape=[jax.ShapeDtypeStruct(shape, f32) for shape in [block] * 2 + [half_shape] * 2],
        in_specs=[pl.BlockSpec(memory_space=pl.ANY)] * 4,
        out_specs=[vmem] * 4,
        scratch_shapes=[pltpu.SemaphoreType.DMA((2 + terms,))],
        compiler_params=pltpu.CompilerParams(vmem_limit_bytes=52 * 2**20),
    )(wave_start, preconditioner, left_blocks, right_blocks)
    facing_wave = facing(own_wave)
    mate_left, mate_right = mate(sent_left), mate(sent_right)
    mate_shifts, own_preconditioner = lax.optimization_barrier(
        (mate(term_shifts), own_preconditioner)
    )
    facing_preconditioner = facing(own_preconditioner)
    shifts = (term_shifts, mate_shifts)

    split_shape = (terms,) + left_blocks.shape[2:]
    blocks = call(
        splitting_kernel,
        (left_blocks, right_blocks, mate_left, mate_right),
        [(split_shape, bf16)] * 4,
        scratch=False,
    )

    def around(values):
        return (values, mate(values), facing(values))

    image, start = call(
        first_kernel,
        (*shifts, wave_start, facing_wave, *blocks),
        [(block, f32), ((3,) + block, f32)],
        scalars=2,
    )
    images = around(image)
    side, inverse = call(
        side_kernel,
        (*shifts, start, preconditioner, facing_preconditioner, *blocks),
        [(block, f32), ((3,) + block, f32)],
        scalars=2,
    )
    (early_row,) = call(
        moments_kernel, (start, image, side, inverse), [((1, LANES), f32)], scratch=False
    )
    side, early_row = lax.optimization_barrier((side, early_row))
    sides = around(side)
    second, ratio = call(
        second_kernel,
        (*shifts, *images, inverse, early_row, *blocks),
        [(block, f32), ((3,) + block, f32)],
        scalars=2,
    )
    seconds = around(second)
    half_block = (half, columns)
    extra, kept_extra, sent_extra, early_row = call(
        extra_kernel,
        (*shifts, start, ratio, inverse, image, side, second, early_row, *blocks),
        [((2,) + block, f32)] + [((2,) + half_block, f32)] * 2 + [((1, LANES), f32)],
        scalars=2,
    )
    mate_extra = mate(sent_extra)
    further, kept_further, sent_further, early_row = call(
        further_kernel,
        (*shifts, start, inverse, image, *sides, second, extra, early_row, *blocks),
        [(block, f32)] + [(half_block, f32)] * 2 + [((1, LANES), f32)],
        scalars=2,
    )
    mate_further = mate(sent_further)
    kept, sent, row = call(
        third_kernel,
        (*shifts, start, inverse, image, side, *seconds, extra, further, early_row, *blocks),
        [(half_block, f32)] * 2 + [row_shape],
        scalars=2,
        more_scratch=[pltpu.VMEM(block, f32)],
    )
    mate_last = mate(sent)
    row, mate_extra, mate_further = lax.optimization_barrier((row, mate_extra, mate_further))
    basis, ritz = call(
        functools.partial(last_kernel, total),
        (exchanged(row), start, ratio, inverse, *sides[:2], *seconds[:2], kept_extra, mate_extra,
         kept_further, mate_further, kept, mate_last),
        [((ITERS, 2) + half_block, f32), ((ITERS,), f32)],
        out_scalars=1,
        scratch=False,
    )
    return (basis, ritz)


def with_halo(cells, sides, width):
    for axis, dim in sides:
        count = lax.axis_size(axis)
        ends = count - 1
        head = lax.slice_in_dim(cells, 0, width, axis=dim)
        tail = lax.slice_in_dim(cells, cells.shape[dim] - width, cells.shape[dim], axis=dim)
        cells = jnp.concatenate(
            [
                lax.ppermute(tail, axis, [(i, (i + 1) % count) for i in range(ends)]),
                cells,
                lax.ppermute(head, axis, [((i + 1) % count, i) for i in range(ends)]),
            ],
            axis=dim,
        )
    return cells


def split_terms_body(wave_start, left_blocks, right_blocks, term_shifts, preconditioner):
    highest = lax.Precision.HIGHEST
    width = wave_start.shape[1]
    row_count = width // lax.axis_size("op")
    first_row = lax.axis_index("op") * row_count
    total = float(wave_start.shape[0] * lax.axis_size("sector") * width * wave_start.shape[2])

    def portion(values):
        return lax.dynamic_slice_in_dim(values, first_row, row_count, axis=values.ndim - 2)

    start_sum = total_sum(jnp.sum(jnp.square(portion(wave_start)))[None])[0] / total
    basis = [wave_start * lax.rsqrt(start_sum + EPSILON)]
    ritz = []
    for _ in range(ITERS):
        latest = basis[-1]
        padded = with_halo(latest, (("sector", 0),), 1)
        shift = term_shifts[:, None, None, None]
        source = jnp.where(
            shift == 1,
            padded[None, :-2],
            jnp.where(shift == -1, padded[None, 2:], padded[None, 1:-1]),
        )
        inner = jnp.einsum("ksab,ksbc->ksac", left_blocks, source, precision=highest)
        image = lax.psum(jnp.einsum("ksac,kscd->sad", inner, right_blocks, precision=highest), "op")
        inverse = 1.0 / preconditioner
        pieces = products([portion(member) for member in basis], portion(image), portion(inverse))
        theta, correlations, scale = coefficients(
            total_sum(jnp.stack(pieces)), total, len(basis)
        )
        ortho = (image - theta * latest) * inverse
        for position, member in enumerate(basis):
            ortho = ortho - correlations[position] * member
        basis.append(ortho * scale)
        ritz.append(theta)
    output = jnp.stack([portion(member) for member in basis[1:]])
    return (output, jnp.stack(ritz))


def solution(mesh):
    placed = (
        P("sector", None, None),
        P("op", "sector", None, None),
        P("op", "sector", None, None),
        P("op"),
        P("sector", None, None),
    )

    def body(wave_start, *operands):
        one_each = mesh.shape["op"] == 2 and wave_start.shape[0] == 2
        return (one_sector_body if one_each else split_terms_body)(wave_start, *operands)

    return jax.shard_map(
        body,
        mesh=mesh,
        in_specs=placed,
        out_specs=(P(None, "sector", "op", None), P()),
        check_vma=False,
    )
```
